32 devices in a mesh: seq: 2 (over core), ctx: 16 (over z, y, x).
Axes of the slice: x: 2, y: 2, z: 4, core: 2. Of those that a mesh axis runs over, the one named last changes fastest.
Arguments:
- pixels: bfloat16 [4, 261, 16384], P('seq', None, 'ctx'), may hold values from -6 to 6
- lengths: int32 [4], P('seq'), may hold values from 1024 to 16384, as said below
- latents: bfloat16 [4, 512, 1024], P('seq', 'ctx'), may hold values from -6 to 6
- w_square: bfloat16 [10, 1024, 1024], P(None, ('seq', 'ctx'))
- w_input: bfloat16 [2, 1024, 261], P(None, ('seq', 'ctx')), may hold values from -0.375 to 0.375
- vec_d: bfloat16 [18, 1024], P(None, ('seq', 'ctx'))
- vec_c: bfloat16 [2, 261], replicated
- cotangent: bfloat16 [4, 512, 1024], P('seq', 'ctx'), may hold values from -6 to 6
Outputs:
- latents_out: bfloat16 [4, 512, 1024], P('seq', 'ctx')
- grad_latents: float32 [4, 512, 1024], P('seq', 'ctx')
- grad_pixels: float32 [4, 261, 16384], P('seq', None, 'ctx')
- grad_square: float32 [10, 1024, 1024], P(None, ('seq', 'ctx'))
- grad_input: float32 [2, 1024, 261], P(None, ('seq', 'ctx'))
- grad_vec: float32 [18, 1024], P(None, ('seq', 'ctx'))
- grad_vec_c: float32 [2, 261], replicated
The draws below stay inside these ranges and needn't reach their ends.
Inputs may be any that keep to these rules, and one draw needn't show every extreme that they name: Slots 0 to lengths[b] - 1 of sequence b are valid, the rest padding; some sequence has all 16384 slots valid and some exactly 1024.
All inputs are finite; a program needn't handle non-finite values.
Results may differ from the reference program's by a relative error of at most 0.014.
Values may be sent and summed in bfloat16 or wider, within the bound.
No kernel may reach another device: no remote copies, remote signals or barrier semaphores. Data moves between devices by JAX's collectives and lax.ppermute only.
A program may use at most 384 MiB of HBM per device.

```python
import math
import jax
import jax.numpy as jnp
from jax import lax

D = 1024
NL = 512
C = 261
H = 8
HD = 128
LEN_MIN = 1024
SEQS = 4
LENGTH = 16384


def draw_lengths(key, part):
    drawn = jax.random.randint(key, (SEQS,), LEN_MIN, LENGTH + 1, dtype=jnp.int32)
    order = jax.random.permutation(jax.random.fold_in(key, 7), SEQS)
    drawn = drawn.at[order[0]].set(LENGTH)
    return drawn.at[order[1]].set(LEN_MIN)


def draw_w_square(key, part):
    cross_factor = math.sqrt(LENGTH) / 3.0
    self_factor = math.sqrt(NL) / 2.0
    factors = jnp.array([1.0, cross_factor, 1.0, 1.0, 1.0, 1.0, 1.0, self_factor, 1.0, 1.0], jnp.float32)
    base = jax.random.normal(key, (10, D, D), jnp.float32)
    return (base * D ** (-0.5) * factors[:, None, None]).astype(jnp.bfloat16)


def draw_vec_d(key, part):
    offsets = jnp.array([1, 0, 0, 0, 0, 1, 0, 0, 0, 1, 0, 0, 0, 0, 1, 0, 0, 0], jnp.float32)
    scales = jnp.array([0.1, 0.2, 0.2, 0.02, 0.2, 0.1, 0.2, 0.2, 0.2, 0.1, 0.2, 0.2, 0.05, 0.2, 0.1, 0.2, 0.2, 0.2], jnp.float32)
    base = jax.random.normal(key, (18, D), jnp.float32)
    return (offsets[:, None] + scales[:, None] * base).astype(jnp.bfloat16)


def draw_vec_c(key, part):
    offsets = jnp.array([1.0, 0.0], jnp.float32)
    scales = jnp.array([0.1, 0.02], jnp.float32)
    base = jax.random.normal(key, (2, C), jnp.float32)
    return (offsets[:, None] + scales[:, None] * base).astype(jnp.bfloat16)


def steps_of(rng, dims, pieces, least, top_value):
    level, own = 1.0, jax.random.fold_in(rng, 6)
    for dim, parts in pieces:
        steps = jnp.exp(jax.random.uniform(jax.random.fold_in(own, dim), (parts,), jnp.float32, least / len(pieces), top_value / len(pieces)))
        level = level * jnp.repeat(steps, dims[dim] // parts).reshape([-1 if axis == dim else 1 for axis in range(len(dims))])
    return level


def normal_values(rng, dims, scale, most, split=(), kind=jnp.bfloat16):
    entries = jax.random.normal(rng, dims, jnp.float32) * scale
    if len(split) > 0:
        entries = steps_of(rng, dims, split, -0.22, 0.18) * entries
    return jnp.clip(entries, min=-most, max=most).astype(kind)


def setup_inputs(seed: int = 0) -> dict:
    streams_of = jax.random.split(jax.random.key(seed), 9)
    pixels = normal_values(streams_of[0], (SEQS, C, LENGTH), 1.0, 6.0, ((0, 2), (2, 16)))
    lengths = draw_lengths(jax.random.fold_in(streams_of[8], 71), 0)
    latents = normal_values(streams_of[2], (SEQS, NL, D), 1.0, 6.0, ((0, 2), (1, 16)))
    w_square = draw_w_square(jax.random.fold_in(streams_of[8], 71), 0)
    w_input = normal_values(streams_of[4], (2, D, C), C ** -0.5, 0.375, ((1, 32),))
    vec_d = draw_vec_d(jax.random.fold_in(streams_of[8], 71), 0)
    vec_c = draw_vec_c(jax.random.fold_in(streams_of[8], 71), 0)
    cotangent = normal_values(streams_of[7], (SEQS, NL, D), 1.0, 6.0, ((0, 2), (1, 16)))
    return {"pixels": pixels, "lengths": lengths, "latents": latents, "w_square": w_square, "w_input": w_input, "vec_d": vec_d, "vec_c": vec_c, "cotangent": cotangent}


@jax.custom_vjp
def low(v):
    return lax.optimization_barrier(v.astype(jnp.bfloat16)).astype(jnp.float32)

@jax.custom_vjp
def low_back(v):
    return v

def low_keep(v):
    return (low(v), None)

def low_pass(kept, grad):
    return (grad,)

def back_keep(v):
    return (v, None)

def back_low(kept, grad):
    return (low(grad),)
low.defvjp(low_keep, low_pass)
low_back.defvjp(back_keep, back_low)

def matmul(form, left, right):
    return jnp.einsum(form, left, right, precision=lax.Precision.HIGHEST)

def layer_norm(value, gain, shift, axis):
    center = value - lax.optimization_barrier(jnp.mean(value, axis=axis, keepdims=True))
    spread = lax.optimization_barrier(jnp.mean(center * center, axis=axis, keepdims=True))
    return center * lax.rsqrt(spread + 1e-05) * gain + shift

def one_sequence(latent, pixel, valid_len, square, inward, vector, vec_in):
    cross_norm = low(layer_norm(latent, vector[0], vector[1], 1))
    query = low(low_back(matmul('id,de->ie', cross_norm, square[0]) + vector[2]))
    in_norm = low(layer_norm(pixel, vec_in[0][:, None], vec_in[1][:, None], 0))
    keys = low(low_back(matmul('cj,dc->jd', in_norm, inward[0])))
    values = low(low_back(matmul('cj,dc->jd', in_norm, inward[1]) + vector[3]))
    scores = low_back(matmul('id,jd->ij', query, keys) * (1.0 / math.sqrt(D)))
    valid = (jnp.arange(LENGTH) < valid_len)[None, :]
    highest = lax.optimization_barrier(jnp.max(jnp.where(valid, scores, -1e+30), axis=1, keepdims=True))
    expo = jnp.where(valid, jnp.exp(scores - highest), 0.0)
    cross_low = low(expo / lax.optimization_barrier(jnp.sum(expo, axis=1, keepdims=True)))
    attended = low(low_back(matmul('ij,jd->id', cross_low, values)))
    after_cross = latent + low_back(matmul('id,de->ie', attended, square[1]) + vector[4])
    ffn_norm = low(layer_norm(after_cross, vector[5], vector[6], 1))
    ffn_pre = low_back(matmul('id,de->ie', ffn_norm, square[2]) + vector[7])
    ffn_act = low(jax.nn.gelu(ffn_pre))
    after_ffn = after_cross + low_back(matmul('id,de->ie', ffn_act, square[3]) + vector[8])
    self_norm = low(layer_norm(after_ffn, vector[9], vector[10], 1))
    self_query = low(low_back(matmul('id,de->ie', self_norm, square[4]) + vector[11])).reshape(NL, H, HD)
    self_keys = low(low_back(matmul('id,de->ie', self_norm, square[5]))).reshape(NL, H, HD)
    self_values = low(low_back(matmul('id,de->ie', self_norm, square[6]) + vector[12])).reshape(NL, H, HD)
    self_scores = low_back(matmul('ihe,jhe->hij', self_query, self_keys) * (1.0 / math.sqrt(HD)))
    self_exp = jnp.exp(self_scores - lax.optimization_barrier(jnp.max(self_scores, axis=2, keepdims=True)))
    self_low = low(self_exp / lax.optimization_barrier(jnp.sum(self_exp, axis=2, keepdims=True)))
    self_mix = low(low_back(matmul('hij,jhe->ihe', self_low, self_values).reshape(NL, D)))
    after_self = after_ffn + low_back(matmul('id,de->ie', self_mix, square[7]) + vector[13])
    out_norm = low(layer_norm(after_self, vector[14], vector[15], 1))
    out_pre = low_back(matmul('id,de->ie', out_norm, square[8]) + vector[16])
    out_act = low(jax.nn.gelu(out_pre))
    return after_self + low_back(matmul('id,de->ie', out_act, square[9]) + vector[17])

def reference(pixels, lengths, latents, w_square, w_input, vec_d, vec_c, cotangent):
    square = w_square.astype(jnp.float32)
    inward = w_input.astype(jnp.float32)
    vector = vec_d.astype(jnp.float32)
    vec_in = vec_c.astype(jnp.float32)

    def visit(totals, sequence_data):
        pixel, valid_len, latent, tangent = sequence_data

        def forward(lat_value, pix_value, sq_value, in_value, vd_value, vc_value):
            return one_sequence(lat_value, pix_value, valid_len, sq_value, in_value, vd_value, vc_value)
        final, pull = jax.vjp(forward, latent.astype(jnp.float32), pixel.astype(jnp.float32), square, inward, vector, vec_in)
        grads = pull(tangent.astype(jnp.float32))
        totals = (totals[0] + grads[2], totals[1] + grads[3], totals[2] + grads[4], totals[3] + grads[5])
        return (totals, (final.astype(jnp.bfloat16), grads[0], grads[1]))
    start = (jnp.zeros_like(square), jnp.zeros_like(inward), jnp.zeros_like(vector), jnp.zeros_like(vec_in))
    totals, stacked = lax.scan(visit, start, (pixels, lengths, latents, cotangent))
    return (stacked[0], stacked[1], stacked[2], totals[0], totals[1], totals[2], totals[3])
```

```python
import math

import jax
import jax.numpy as jnp
from jax import lax
from jax.sharding import PartitionSpec as P

H = 8
epsilon = 1e-05
f32 = jnp.float32
b16 = jnp.bfloat16


def matmul(form, left, right):
    return jnp.einsum(form, left, right, preferred_element_type=f32)


def layer_norm(value, gain, shift, axis):
    center = value - jnp.mean(value, axis=axis, keepdims=True)
    spread = jnp.mean(center * center, axis=axis, keepdims=True)
    inverse = lax.rsqrt(spread + epsilon)
    unit = center * inverse
    return (unit * gain + shift, unit, inverse)


def norm_back(grad, unit, inverse, gain, axis):
    scaled = grad * gain
    inner = (
        scaled
        - jnp.mean(scaled, axis=axis, keepdims=True)
        - unit * jnp.mean(scaled * unit, axis=axis, keepdims=True)
    )
    return inner * inverse


def gelu_back(value, grad):
    unused, pull = jax.vjp(jax.nn.gelu, value)
    return pull(grad)[0]


def split_two(value):
    high = value.astype(b16)
    low = (value - high.astype(f32)).astype(b16)
    return high, low


def pick(array, index):
    return lax.dynamic_index_in_dim(array, index, 0, keepdims=False)


def body(pixels, lengths, latents, w_square, w_input, vec_d, vec_c, cotangent):
    n = lax.axis_size("ctx")
    bits_all = n.bit_length() - 1
    rows = latents.shape[1]
    width = latents.shape[2]
    own_w = w_square.shape[1]
    channels = pixels.shape[1]
    slots = pixels.shape[2]
    total_rows = rows * n
    head_size = width // H
    scale = 1.0 / math.sqrt(width)
    scale_self = 1.0 / math.sqrt(head_size)
    core = lax.axis_index("seq")
    place = lax.axis_index("ctx")
    parity = place & 1
    pair = place >> 1
    wide = [4 << i for i in range(bits_all - 2)]

    def swap(x, bit):
        return lax.ppermute(x, "ctx", [(i, i ^ bit) for i in range(n)])

    def swap_core(x):
        return lax.ppermute(x, "seq", [(0, 1), (1, 0)])

    def ordered(mine, other, flag, axis):
        first = jnp.where(flag == 0, mine, other)
        second = jnp.where(flag == 0, other, mine)
        return jnp.concatenate([first, second], axis=axis)

    def gather(x, order, low_bit):
        levels = bits_all - low_bit
        m, r, c = x.shape
        x = x.reshape((m,) + (1,) * levels + (r, c))
        for bit in order:
            level = bit.bit_length() - 1 - low_bit
            axis = 1 + (levels - 1 - level)
            other = swap(x, bit)
            x = ordered(x, other, (place // bit) & 1, axis)
        return x.reshape(m, (n >> low_bit) * r, c)

    def both(x):
        return ordered(x, swap_core(x), core, 1)

    order_a = wide + [2, 1]
    order_b = wide + [1, 2]

    def own_sequence(array, order):
        mine = pick(array, parity)
        theirs = swap(pick(array, 1 - parity), 1)
        block = ordered(mine, theirs, parity, 0)
        return gather(block[None], order, 1)[0]

    lanes = 384
    packed = jnp.concatenate(
        [
            jnp.pad(w_input[0], ((0, 0), (0, lanes - channels))),
            w_input[1],
            vec_d.T,
            jnp.zeros((own_w, lanes - channels - vec_d.shape[0]), b16),
        ],
        axis=1,
    )
    packed = both(gather(packed[None], order_a, 0))[0]
    v_key = packed[:, :channels]
    v_val = packed[:, lanes : lanes + channels]
    vecf = packed[:, lanes + channels : lanes + channels + vec_d.shape[0]].T.astype(f32)
    lat = own_sequence(latents, wide + [2])
    square = [None] * 10
    for group, order in (((0,), order_b), ((1, 2), order_a), ((3, 4), order_b), ((5, 6), order_a), ((7, 8, 9), order_b)):
        full = both(gather(w_square[group[0] : group[-1] + 1], order, 0))
        for i, k in enumerate(group):
            square[k] = full[i]
    cot = own_sequence(cotangent, wide + [2])

    latent = lat.astype(f32)
    norm_a, unit_a, inv_a = layer_norm(latent, vecf[0], vecf[1], 1)
    low_a = norm_a.astype(b16)
    query = (matmul("id,de->ie", low_a, square[0]) + vecf[2]).astype(b16)
    gate = (matmul("dc,id->ci", v_key, query) * scale).astype(b16)
    gates = ordered(gate[None], swap(gate, 1)[None], parity, 0)

    gain_in = vec_c.astype(f32)
    norm_x, unit_x, inv_x = layer_norm(pixels.astype(f32), gain_in[0][:, None], gain_in[1][:, None], 1)
    low_x = norm_x.astype(b16)
    position = place * slots + jnp.arange(slots, dtype=jnp.int32)
    valid = (position[None, :] < lengths[:, None])[:, None, :]
    scores = matmul("qci,qcj->qij", gates, low_x)
    top = jnp.max(jnp.where(valid, scores, -1e30), axis=2)
    top_hi, top_lo = split_two(top)
    shift = top_hi.astype(f32) + top_lo.astype(f32)
    expo = jnp.where(valid, jnp.exp(scores - shift[..., None]), 0.0)
    total_hi, total_lo = split_two(jnp.sum(expo, axis=2))
    mixed = matmul("qij,qcj->qci", expo.astype(b16), low_x).astype(b16)
    tall = (channels + 6 + 15) // 16 * 16
    stats = jnp.stack([top_hi, top_lo, total_hi, total_lo], axis=1)
    pay = jnp.concatenate([mixed, stats, jnp.zeros((2, tall - channels - 4, total_rows), b16)], axis=1)

    def opened(p):
        s = p[channels : channels + 4].astype(f32)
        return p[:channels].astype(f32), s[0] + s[1], s[2] + s[3]

    def merge(a, b):
        va, ta, la = opened(a)
        vb, tb, lb = opened(b)
        t = jnp.maximum(ta, tb)
        ea = jnp.exp(ta - t)
        eb = jnp.exp(tb - t)
        return va * ea + vb * eb, t, la * ea + lb * eb

    def closed(v, t, l):
        th, tl = split_two(t)
        lh, ll = split_two(l)
        s = jnp.stack([th, tl, lh, ll], axis=0)
        return jnp.concatenate([v.astype(b16), s, jnp.zeros((tall - channels - 4, total_rows), b16)], axis=0)

    state = merge(pick(pay, parity), swap(pick(pay, 1 - parity), 1))
    for bit in [2] + wide:
        mine = closed(*state)
        state = merge(mine, swap(mine, bit))
    mix_sum, top_all, total_all = state
    mean_x = mix_sum / total_all
    mean_low = mean_x.astype(b16)

    attended = (matmul("ci,dc->id", mean_low, v_val) + vecf[3]).astype(b16)
    after_cross = latent + matmul("id,de->ie", attended, square[1]) + vecf[4]
    norm_b, unit_b, inv_b = layer_norm(after_cross, vecf[5], vecf[6], 1)
    low_b = norm_b.astype(b16)
    ffn_pre = matmul("id,de->ie", low_b, square[2]) + vecf[7]
    ffn_act = jax.nn.gelu(ffn_pre).astype(b16)
    after_ffn = after_cross + matmul("id,de->ie", ffn_act, square[3]) + vecf[8]
    norm_c, unit_c, inv_c = layer_norm(after_ffn, vecf[9], vecf[10], 1)
    low_c = norm_c.astype(b16)

    def heads(x):
        return x.reshape(total_rows, H, head_size)

    self_query = (matmul("id,de->ie", low_c, square[4]) + vecf[11]).astype(b16)
    self_keys = matmul("id,de->ie", low_c, square[5]).astype(b16)
    self_values = (matmul("id,de->ie", low_c, square[6]) + vecf[12]).astype(b16)
    query_heads, key_heads, value_heads = heads(self_query), heads(self_keys), heads(self_values)
    self_scores = matmul("ihe,jhe->hij", query_heads, key_heads) * scale_self
    self_exp = jnp.exp(self_scores - jnp.max(self_scores, axis=2, keepdims=True))
    self_weight = self_exp / jnp.sum(self_exp, axis=2, keepdims=True)
    self_low = self_weight.astype(b16)
    self_mix = matmul("hij,jhe->ihe", self_low, value_heads).reshape(total_rows, width).astype(b16)
    after_self = after_ffn + matmul("id,de->ie", self_mix, square[7]) + vecf[13]
    norm_e, unit_e, inv_e = layer_norm(after_self, vecf[14], vecf[15], 1)
    low_e = norm_e.astype(b16)
    out_pre = matmul("id,de->ie", low_e, square[8]) + vecf[16]
    out_act = jax.nn.gelu(out_pre).astype(b16)
    final = (after_self + matmul("id,de->ie", out_act, square[9]) + vecf[17]).astype(b16)

    def own_rows(array):
        mine = lax.dynamic_slice_in_dim(array, place * rows, rows, 0)
        theirs = lax.dynamic_slice_in_dim(array, (place ^ 1) * rows, rows, 0)
        return ordered(mine[None], swap(theirs, 1)[None], parity, 0)

    latents_out = own_rows(final)

    def share(a):
        parts = [lax.dynamic_slice_in_dim(a, s * n * own_w + pair * 2 * own_w, 2 * own_w, a.ndim - 1) for s in range(2)]
        return jnp.stack(parts, axis=0)

    def settle(x, axis):
        x = pick(x, core) + swap_core(pick(x, 1 - core))
        mine = lax.dynamic_slice_in_dim(x, parity * own_w, own_w, axis)
        theirs = lax.dynamic_slice_in_dim(x, (1 - parity) * own_w, own_w, axis)
        return mine + swap(theirs, 1)

    def weight_grad(a, r):
        return matmul("sia,ie->sae", jnp.moveaxis(share(a), 0, 0), r)

    def sums(x):
        return jnp.sum(x.astype(f32), axis=0)

    d_final = cot.astype(f32)
    round_nine = cot
    part9 = weight_grad(out_act, round_nine)
    d_out_pre = gelu_back(out_pre, matmul("ie,de->id", round_nine, square[9])).astype(b16)
    part8 = weight_grad(low_e, d_out_pre)
    d_norm_e = matmul("ie,de->id", d_out_pre, square[8])
    d_after_self = d_final + norm_back(d_norm_e, unit_e, inv_e, vecf[14], 1)
    round_seven = d_after_self.astype(b16)
    part7 = weight_grad(self_mix, round_seven)
    d_mix = matmul("ie,de->id", round_seven, square[7]).astype(b16)
    d_mix_heads = heads(d_mix)
    d_self_weight = matmul("ihe,jhe->hij", d_mix_heads, value_heads)
    d_self_scores = (
        self_weight * (d_self_weight - jnp.sum(d_self_weight * self_weight, axis=2, keepdims=True))
    ).astype(b16)
    d_self_query = (matmul("hij,jhe->ihe", d_self_scores, key_heads) * scale_self).reshape(total_rows, width).astype(b16)
    d_self_keys = (matmul("hij,ihe->jhe", d_self_scores, query_heads) * scale_self).reshape(total_rows, width).astype(b16)
    d_self_values = matmul("hij,ihe->jhe", self_low, d_mix_heads).reshape(total_rows, width).astype(b16)
    part4 = weight_grad(low_c, d_self_query)
    part5 = weight_grad(low_c, d_self_keys)
    part6 = weight_grad(low_c, d_self_values)
    d_norm_c = (
        matmul("ie,de->id", d_self_query, square[4])
        + matmul("ie,de->id", d_self_keys, square[5])
        + matmul("ie,de->id", d_self_values, square[6])
    )
    d_after_ffn = d_after_self + norm_back(d_norm_c, unit_c, inv_c, vecf[9], 1)
    round_three = d_after_ffn.astype(b16)
    part3 = weight_grad(ffn_act, round_three)
    d_ffn_pre = gelu_back(ffn_pre, matmul("ie,de->id", round_three, square[3])).astype(b16)
    part2 = weight_grad(low_b, d_ffn_pre)
    d_norm_b = matmul("ie,de->id", d_ffn_pre, square[2])
    d_after_cross = d_after_ffn + norm_back(d_norm_b, unit_b, inv_b, vecf[5], 1)
    round_one = d_after_cross.astype(b16)
    part1 = weight_grad(attended, round_one)
    d_attended = matmul("ie,de->id", round_one, square[1]).astype(b16)

    pull = matmul("dc,id->ci", v_val, d_attended).astype(b16)
    delta = jnp.sum(pull.astype(f32) * mean_x, axis=0)
    pieces = split_two(top_all) + split_two(total_all) + split_two(delta)
    sent = jnp.concatenate([pull, jnp.stack(pieces, axis=0), jnp.zeros((tall - channels - 6, total_rows), b16)], axis=0)
    sents = ordered(sent[None], swap(sent, 1)[None], parity, 0)
    pulls = sents[:, :channels]
    side = sents[:, channels : channels + 6].astype(f32)
    top_q = side[:, 0] + side[:, 1]
    total_q = side[:, 2] + side[:, 3]
    delta_q = side[:, 4] + side[:, 5]
    scores_again = matmul("qci,qcj->qij", gates, low_x)
    weight = jnp.where(valid, jnp.exp(scores_again - top_q[..., None]), 0.0) / total_q[..., None]
    d_weight = matmul("qci,qcj->qij", pulls, low_x)
    d_scores = (weight * (d_weight - delta_q[..., None])).astype(b16)
    weight_low = weight.astype(b16)
    force = matmul("qij,qcj->qci", d_scores, low_x).astype(b16)
    d_in_norm = matmul("qci,qij->qcj", gates, d_scores) + matmul("qci,qij->qcj", pulls, weight_low)
    grad_pixels = norm_back(d_in_norm, unit_x, inv_x, gain_in[0][:, None], 1)
    grad_vc = jnp.stack([jnp.sum(d_in_norm * unit_x, axis=(0, 2)), jnp.sum(d_in_norm, axis=(0, 2))])
    grad_vc = grad_vc + swap_core(grad_vc)
    for bit in [1, 2] + wide:
        grad_vc = grad_vc + swap(grad_vc, bit)

    force_sum = pick(force, parity).astype(f32) + swap(pick(force, 1 - parity), 1).astype(f32)
    for bit in [2] + wide:
        mine = force_sum.astype(b16)
        force_sum = mine.astype(f32) + swap(mine, bit).astype(f32)
    force_low = (force_sum * scale).astype(b16)
    d_query = matmul("ci,dc->id", force_low, v_key).astype(b16)
    part0 = weight_grad(low_a, d_query)
    d_norm_a = matmul("ie,de->id", d_query, square[0])
    grad_lat = d_after_cross + norm_back(d_norm_a, unit_a, inv_a, vecf[0], 1)
    grad_latents = own_rows(grad_lat)

    share_q = share(query)
    share_att = share(d_attended)
    part_in = jnp.stack(
        [matmul("sia,ci->sac", share_q, force_low), matmul("sia,ci->sac", share_att, mean_low)], axis=1
    )
    grad_input = settle(part_in, 1)
    vec_part = jnp.stack(
        [
            sums(d_norm_a * unit_a),
            sums(d_norm_a),
            sums(d_query),
            sums(d_attended),
            sums(round_one),
            sums(d_norm_b * unit_b),
            sums(d_norm_b),
            sums(d_ffn_pre),
            sums(round_three),
            sums(d_norm_c * unit_c),
            sums(d_norm_c),
            sums(d_self_query),
            sums(d_self_values),
            sums(round_seven),
            sums(d_norm_e * unit_e),
            sums(d_norm_e),
            sums(d_out_pre),
            sums(round_nine),
        ]
    )
    grad_vec = settle(share(vec_part), 1)
    late = settle(part0, 0)[None]
    mid = settle(jnp.stack([part1, part2, part3], axis=1), 1)
    heads_part = settle(jnp.stack([part4, part5, part6], axis=1), 1)
    early = settle(jnp.stack([part7, part8, part9], axis=1), 1)
    grad_square = jnp.concatenate([late, mid, heads_part, early], axis=0)
    return (latents_out, grad_latents, grad_pixels, grad_square, grad_input, grad_vec, grad_vc)


def solution(mesh):
    placed = (
        P("seq", None, "ctx"),
        P("seq"),
        P("seq", "ctx", None),
        P(None, ("seq", "ctx"), None),
        P(None, ("seq", "ctx"), None),
        P(None, ("seq", "ctx")),
        P(),
        P("seq", "ctx", None),
    )
    return jax.shard_map(
        body,
        mesh=mesh,
        in_specs=placed,
        out_specs=(
            P("seq", "ctx", None),
            P("seq", "ctx", None),
            P("seq", None, "ctx"),
            P(None, ("seq", "ctx"), None),
            P(None, ("seq", "ctx"), None),
            P(None, ("seq", "ctx")),
            P(),
        ),
        check_vma=False,
    )
```

```python
import math

import jax
import jax.numpy as jnp
from jax import lax
from jax.sharding import PartitionSpec as P

H = 8
epsilon = 1e-05
f32 = jnp.float32
b16 = jnp.bfloat16


def matmul(form, left, right):
    return jnp.einsum(form, left, right, preferred_element_type=f32)


def layer_norm(value, gain, shift, axis):
    center = value - jnp.mean(value, axis=axis, keepdims=True)
    spread = jnp.mean(center * center, axis=axis, keepdims=True)
    inverse = lax.rsqrt(spread + epsilon)
    unit = center * inverse
    return (unit * gain + shift, unit, inverse)


def norm_back(grad, unit, inverse, gain, axis):
    scaled = grad * gain
    inner = (
        scaled
        - jnp.mean(scaled, axis=axis, keepdims=True)
        - unit * jnp.mean(scaled * unit, axis=axis, keepdims=True)
    )
    return inner * inverse


def gelu_back(value, grad):
    unused, pull = jax.vjp(jax.nn.gelu, value)
    return pull(grad)[0]


def split_two(value):
    high = value.astype(b16)
    low = (value - high.astype(f32)).astype(b16)
    return high, low


def after(value, *needed):
    return lax.optimization_barrier((value,) + needed)[0]


def pick(array, index):
    return lax.dynamic_index_in_dim(array, index, 0, keepdims=False)


def body(pixels, lengths, latents, w_square, w_input, vec_d, vec_c, cotangent):
    n = lax.axis_size("ctx")
    bits_all = n.bit_length() - 1
    rows = latents.shape[1]
    width = latents.shape[2]
    own_w = w_square.shape[1]
    channels = pixels.shape[1]
    slots = pixels.shape[2]
    total_rows = rows * n
    head_size = width // H
    scale = 1.0 / math.sqrt(width)
    scale_self = 1.0 / math.sqrt(head_size)
    core = lax.axis_index("seq")
    place = lax.axis_index("ctx")
    parity = place & 1
    pair = place >> 1
    wide = [4 << i for i in range(bits_all - 2)]

    def swap(x, bit):
        return lax.ppermute(x, "ctx", [(i, i ^ bit) for i in range(n)])

    def swap_core(x):
        return lax.ppermute(x, "seq", [(0, 1), (1, 0)])

    def ordered(mine, other, flag, axis):
        first = jnp.where(flag == 0, mine, other)
        second = jnp.where(flag == 0, other, mine)
        return jnp.concatenate([first, second], axis=axis)

    def gather(x, order, low_bit):
        levels = bits_all - low_bit
        m, r, c = x.shape
        x = x.reshape((m,) + (1,) * levels + (r, c))
        for bit in order:
            level = bit.bit_length() - 1 - low_bit
            axis = 1 + (levels - 1 - level)
            other = swap(x, bit)
            x = ordered(x, other, (place // bit) & 1, axis)
        return x.reshape(m, (n >> low_bit) * r, c)

    def both(x):
        return ordered(x, swap_core(x), core, 1)

    order_a = wide + [2, 1]
    order_b = wide + [1, 2]

    def own_sequence(array, order):
        mine = pick(array, parity)
        theirs = swap(pick(array, 1 - parity), 1)
        block = ordered(mine, theirs, parity, 0)
        return gather(block[None], order, 1)[0]

    lanes = 384
    packed = jnp.concatenate(
        [
            jnp.pad(w_input[0], ((0, 0), (0, lanes - channels))),
            w_input[1],
            vec_d.T,
            jnp.zeros((own_w, lanes - channels - vec_d.shape[0]), b16),
        ],
        axis=1,
    )
    packed = both(gather(packed[None], order_a, 0))[0]
    tall = (channels + 6 + 15) // 16 * 16
    v_key = packed[:, :tall]
    v_val = jnp.where(jnp.arange(tall) < channels, packed[:, lanes : lanes + tall], jnp.zeros((), b16))
    vecf = packed[:, lanes + channels : lanes + channels + vec_d.shape[0]].T.astype(f32)
    lat = own_sequence(latents, wide + [2])
    late_squares = lax.all_gather(w_square[4:], ("seq", "ctx"), axis=1, tiled=True)
    square = [both(gather(w_square[:1], order_b, 0))[0], None, None, None] + [late_squares[k] for k in range(6)]

    latent = lat.astype(f32)
    norm_a, unit_a, inv_a = layer_norm(latent, vecf[0], vecf[1], 1)
    low_a = norm_a.astype(b16)
    held = after(w_square[1:4], lat, square[0][0, 0])
    first = both(gather(held[:1], order_a, 0))
    second = both(gather(held[1:], order_b, 0))
    square[1], square[2], square[3] = first[0], second[0], second[1]
    query = (matmul("id,de->ie", low_a, square[0]) + vecf[2]).astype(b16)
    gate = (matmul("dc,id->ci", v_key, query) * scale).astype(b16)
    cot = own_sequence(after(cotangent, gate), wide + [2])
    gates = ordered(gate[None], swap(gate, 1)[None], parity, 0)

    gain_in = vec_c.astype(f32)
    norm_x, unit_x, inv_x = layer_norm(pixels.astype(f32), gain_in[0][:, None], gain_in[1][:, None], 1)
    low_x = jnp.pad(norm_x.astype(b16), ((0, 0), (0, tall - channels), (0, 0)))
    position = place * slots + jnp.arange(slots, dtype=jnp.int32)
    valid = (position[None, :] < lengths[:, None])[:, None, :]
    scores = matmul("qci,qcj->qij", gates, low_x)
    top = jnp.max(jnp.where(valid, scores, -1e30), axis=2)
    top_hi, top_lo = split_two(top)
    shift = top_hi.astype(f32) + top_lo.astype(f32)
    expo = jnp.where(valid, jnp.exp(scores - shift[..., None]), 0.0)
    total_hi, total_lo = split_two(jnp.sum(expo, axis=2))
    mixed = matmul("qij,qcj->qci", expo.astype(b16), low_x).astype(b16)
    row = jnp.arange(tall)[:, None]

    def write(v, parts):
        for k, part in enumerate(parts):
            v = jnp.where(row == channels + k, part[..., None, :], v)
        return v

    pay = write(mixed, [top_hi, top_lo, total_hi, total_lo])

    def opened(p):
        s = p[channels : channels + 4].astype(f32)
        return p.astype(f32), s[0] + s[1], s[2] + s[3]

    def merge(a, b):
        va, ta, la = opened(a)
        vb, tb, lb = opened(b)
        t = jnp.maximum(ta, tb)
        ea = jnp.exp(ta - t)
        eb = jnp.exp(tb - t)
        return va * ea + vb * eb, t, la * ea + lb * eb

    def closed(v, t, l):
        return write(v.astype(b16), split_two(t) + split_two(l))

    state = merge(pick(pay, parity), swap(pick(pay, 1 - parity), 1))
    for bit in [2] + wide:
        mine = closed(*state)
        state = merge(mine, swap(mine, bit))
    mix_sum, top_all, total_all = state
    mean_x = jnp.where(row < channels, mix_sum / total_all, 0.0)
    mean_low = mean_x.astype(b16)

    attended = (matmul("ci,dc->id", mean_low, v_val) + vecf[3]).astype(b16)
    after_cross = latent + matmul("id,de->ie", attended, square[1]) + vecf[4]
    norm_b, unit_b, inv_b = layer_norm(after_cross, vecf[5], vecf[6], 1)
    low_b = norm_b.astype(b16)
    ffn_pre = matmul("id,de->ie", low_b, square[2]) + vecf[7]
    ffn_act = jax.nn.gelu(ffn_pre).astype(b16)
    after_ffn = after_cross + matmul("id,de->ie", ffn_act, square[3]) + vecf[8]
    norm_c, unit_c, inv_c = layer_norm(after_ffn, vecf[9], vecf[10], 1)
    low_c = norm_c.astype(b16)

    def heads(x):
        return x.reshape(total_rows, H, head_size)

    self_query = (matmul("id,de->ie", low_c, square[4]) + vecf[11]).astype(b16)
    self_keys = matmul("id,de->ie", low_c, square[5]).astype(b16)
    self_values = (matmul("id,de->ie", low_c, square[6]) + vecf[12]).astype(b16)
    query_heads, key_heads, value_heads = heads(self_query), heads(self_keys), heads(self_values)
    self_scores = matmul("ihe,jhe->hij", query_heads, key_heads) * scale_self
    self_exp = jnp.exp(self_scores - jnp.max(self_scores, axis=2, keepdims=True))
    self_weight = self_exp / jnp.sum(self_exp, axis=2, keepdims=True)
    self_low = self_weight.astype(b16)
    self_mix = matmul("hij,jhe->ihe", self_low, value_heads).reshape(total_rows, width).astype(b16)
    after_self = after_ffn + matmul("id,de->ie", self_mix, square[7]) + vecf[13]
    norm_e, unit_e, inv_e = layer_norm(after_self, vecf[14], vecf[15], 1)
    low_e = norm_e.astype(b16)
    out_pre = matmul("id,de->ie", low_e, square[8]) + vecf[16]
    out_act = jax.nn.gelu(out_pre).astype(b16)
    final = (after_self + matmul("id,de->ie", out_act, square[9]) + vecf[17]).astype(b16)

    def own_rows(array):
        mine = lax.dynamic_slice_in_dim(array, place * rows, rows, 0)
        theirs = lax.dynamic_slice_in_dim(array, (place ^ 1) * rows, rows, 0)
        return ordered(mine[None], swap(theirs, 1)[None], parity, 0)

    latents_out = own_rows(final)

    def share(a):
        parts = [lax.dynamic_slice_in_dim(a, s * n * own_w + pair * 2 * own_w, 2 * own_w, a.ndim - 1) for s in range(2)]
        return jnp.stack(parts, axis=0)

    def settle(x, axis):
        x = pick(x, core) + swap_core(pick(x, 1 - core))
        mine = lax.dynamic_slice_in_dim(x, parity * own_w, own_w, axis)
        theirs = lax.dynamic_slice_in_dim(x, (1 - parity) * own_w, own_w, axis)
        return mine + swap(theirs, 1)

    def weight_grad(a, r):
        return matmul("sia,ie->sae", jnp.moveaxis(share(a), 0, 0), r)

    def sums(x):
        return jnp.sum(x.astype(f32), axis=0)

    d_final = cot.astype(f32)
    round_nine = cot
    part9 = weight_grad(out_act, round_nine)
    d_out_pre = gelu_back(out_pre, matmul("ie,de->id", round_nine, square[9])).astype(b16)
    part8 = weight_grad(low_e, d_out_pre)
    d_norm_e = matmul("ie,de->id", d_out_pre, square[8])
    d_after_self = d_final + norm_back(d_norm_e, unit_e, inv_e, vecf[14], 1)
    round_seven = d_after_self.astype(b16)
    part7 = weight_grad(self_mix, round_seven)
    d_mix = matmul("ie,de->id", round_seven, square[7]).astype(b16)
    d_mix_heads = heads(d_mix)
    d_self_weight = matmul("ihe,jhe->hij", d_mix_heads, value_heads)
    d_self_scores = (
        self_weight * (d_self_weight - jnp.sum(d_self_weight * self_weight, axis=2, keepdims=True))
    ).astype(b16)
    d_self_query = (matmul("hij,jhe->ihe", d_self_scores, key_heads) * scale_self).reshape(total_rows, width).astype(b16)
    d_self_keys = (matmul("hij,ihe->jhe", d_self_scores, query_heads) * scale_self).reshape(total_rows, width).astype(b16)
    d_self_values = matmul("hij,ihe->jhe", self_low, d_mix_heads).reshape(total_rows, width).astype(b16)
    part4 = weight_grad(low_c, d_self_query)
    part5 = weight_grad(low_c, d_self_keys)
    part6 = weight_grad(low_c, d_self_values)
    d_norm_c = (
        matmul("ie,de->id", d_self_query, square[4])
        + matmul("ie,de->id", d_self_keys, square[5])
        + matmul("ie,de->id", d_self_values, square[6])
    )
    d_after_ffn = d_after_self + norm_back(d_norm_c, unit_c, inv_c, vecf[9], 1)
    round_three = d_after_ffn.astype(b16)
    part3 = weight_grad(ffn_act, round_three)
    d_ffn_pre = gelu_back(ffn_pre, matmul("ie,de->id", round_three, square[3])).astype(b16)
    part2 = weight_grad(low_b, d_ffn_pre)
    d_norm_b = matmul("ie,de->id", d_ffn_pre, square[2])
    d_after_cross = d_after_ffn + norm_back(d_norm_b, unit_b, inv_b, vecf[5], 1)
    round_one = d_after_cross.astype(b16)
    part1 = weight_grad(attended, round_one)
    d_attended = matmul("ie,de->id", round_one, square[1]).astype(b16)

    pull = matmul("dc,id->ci", v_val, d_attended).astype(b16)
    delta = jnp.sum(pull.astype(f32) * mean_x, axis=0)
    pieces = split_two(top_all) + split_two(total_all) + split_two(delta)
    sent = write(pull, pieces)
    sents = ordered(sent[None], swap(sent, 1)[None], parity, 0)
    pulls = sents
    side = sents[:, channels : channels + 6].astype(f32)
    top_q = side[:, 0] + side[:, 1]
    total_q = side[:, 2] + side[:, 3]
    delta_q = side[:, 4] + side[:, 5]
    scores_again = matmul("qci,qcj->qij", gates, low_x)
    weight = jnp.where(valid, jnp.exp(scores_again - top_q[..., None]), 0.0) / total_q[..., None]
    d_weight = matmul("qci,qcj->qij", pulls, low_x)
    d_scores = (weight * (d_weight - delta_q[..., None])).astype(b16)
    weight_low = weight.astype(b16)
    force = matmul("qij,qcj->qci", d_scores, low_x).astype(b16)
    d_in_norm = (matmul("qci,qij->qcj", gates, d_scores) + matmul("qci,qij->qcj", pulls, weight_low))[:, :channels]
    grad_pixels = norm_back(d_in_norm, unit_x, inv_x, gain_in[0][:, None], 1)
    grad_vc = jnp.stack([jnp.sum(d_in_norm * unit_x, axis=(0, 2)), jnp.sum(d_in_norm, axis=(0, 2))])
    grad_vc = grad_vc + swap_core(grad_vc)
    for bit in [1, 2] + wide:
        grad_vc = grad_vc + swap(grad_vc, bit)

    force_sum = pick(force, parity).astype(f32) + swap(pick(force, 1 - parity), 1).astype(f32)
    for bit in [2] + wide:
        mine = force_sum.astype(b16)
        force_sum = mine.astype(f32) + swap(mine, bit).astype(f32)
    force_low = (force_sum * scale).astype(b16)
    d_query = matmul("ci,dc->id", force_low, v_key).astype(b16)
    part0 = weight_grad(low_a, d_query)
    d_norm_a = matmul("ie,de->id", d_query, square[0])
    grad_lat = d_after_cross + norm_back(d_norm_a, unit_a, inv_a, vecf[0], 1)
    grad_latents = own_rows(grad_lat)

    share_q = share(query)
    share_att = share(d_attended)
    part_in = jnp.stack(
        [matmul("sia,ci->sac", share_q, force_low), matmul("sia,ci->sac", share_att, mean_low)], axis=1
    )[..., :channels]
    grad_input = settle(part_in, 1)
    vec_part = jnp.stack(
        [
            sums(d_norm_a * unit_a),
            sums(d_norm_a),
            sums(d_query),
            sums(d_attended),
            sums(round_one),
            sums(d_norm_b * unit_b),
            sums(d_norm_b),
            sums(d_ffn_pre),
            sums(round_three),
            sums(d_norm_c * unit_c),
            sums(d_norm_c),
            sums(d_self_query),
            sums(d_self_values),
            sums(round_seven),
            sums(d_norm_e * unit_e),
            sums(d_norm_e),
            sums(d_out_pre),
            sums(round_nine),
        ]
    )
    grad_vec = settle(share(vec_part), 1)
    late = settle(part0, 0)[None]
    mid = settle(jnp.stack([part1, part2, part3], axis=1), 1)
    heads_part = settle(jnp.stack([part4, part5, part6], axis=1), 1)
    early = settle(jnp.stack([part7, part8, part9], axis=1), 1)
    grad_square = jnp.concatenate([late, mid, heads_part, early], axis=0)
    return (latents_out, grad_latents, grad_pixels, grad_square, grad_input, grad_vec, grad_vc)


def solution(mesh):
    placed = (
        P("seq", None, "ctx"),
        P("seq"),
        P("seq", "ctx", None),
        P(None, ("seq", "ctx"), None),
        P(None, ("seq", "ctx"), None),
        P(None, ("seq", "ctx")),
        P(),
        P("seq", "ctx", None),
    )
    return jax.shard_map(
        body,
        mesh=mesh,
        in_specs=placed,
        out_specs=(
            P("seq", "ctx", None),
            P("seq", "ctx", None),
            P("seq", None, "ctx"),
            P(None, ("seq", "ctx"), None),
            P(None, ("seq", "ctx"), None),
            P(None, ("seq", "ctx")),
            P(),
        ),
        check_vma=False,
    )
```

```python
import math

import jax
import jax.numpy as jnp
from jax import lax
from jax.sharding import PartitionSpec as P

H = 8
epsilon = 1e-05
f32 = jnp.float32
b16 = jnp.bfloat16


def matmul(form, left, right):
    return jnp.einsum(form, left, right, preferred_element_type=f32)


def layer_norm(value, gain, shift, axis):
    center = value - jnp.mean(value, axis=axis, keepdims=True)
    spread = jnp.mean(center * center, axis=axis, keepdims=True)
    inverse = lax.rsqrt(spread + epsilon)
    unit = center * inverse
    return (unit * gain + shift, unit, inverse)


def norm_back(grad, unit, inverse, gain, axis):
    scaled = grad * gain
    inner = (
        scaled
        - jnp.mean(scaled, axis=axis, keepdims=True)
        - unit * jnp.mean(scaled * unit, axis=axis, keepdims=True)
    )
    return inner * inverse


def gelu_back(value, grad):
    unused, pull = jax.vjp(jax.nn.gelu, value)
    return pull(grad)[0]


def split_two(value):
    high = value.astype(b16)
    low = (value - high.astype(f32)).astype(b16)
    return high, low


def after(value, *needed):
    return lax.optimization_barrier((value,) + needed)[0]


def pick(array, index):
    return lax.dynamic_index_in_dim(array, index, 0, keepdims=False)


def body(pixels, lengths, latents, w_square, w_input, vec_d, vec_c, cotangent):
    n = lax.axis_size("ctx")
    bits_all = n.bit_length() - 1
    rows = latents.shape[1]
    width = latents.shape[2]
    own_w = w_square.shape[1]
    channels = pixels.shape[1]
    slots = pixels.shape[2]
    total_rows = rows * n
    head_size = width // H
    scale = 1.0 / math.sqrt(width)
    scale_self = 1.0 / math.sqrt(head_size)
    core = lax.axis_index("seq")
    place = lax.axis_index("ctx")
    parity = place & 1
    pair = place >> 1
    wide = [4 << i for i in range(bits_all - 2)]

    def swap(x, bit):
        return lax.ppermute(x, "ctx", [(i, i ^ bit) for i in range(n)])

    def swap_core(x):
        return lax.ppermute(x, "seq", [(0, 1), (1, 0)])

    def ordered(mine, other, flag, axis):
        first = jnp.where(flag == 0, mine, other)
        second = jnp.where(flag == 0, other, mine)
        return jnp.concatenate([first, second], axis=axis)

    def gather(x, order, low_bit, ties=()):
        levels = bits_all - low_bit
        m, r, c = x.shape
        x = x.reshape((m,) + (1,) * levels + (r, c))
        for step, bit in enumerate(order):
            if step < len(ties):
                x = after(x, ties[step])
            level = bit.bit_length() - 1 - low_bit
            axis = 1 + (levels - 1 - level)
            other = swap(x, bit)
            x = ordered(x, other, (place // bit) & 1, axis)
        return x.reshape(m, (n >> low_bit) * r, c)

    def both(x):
        return ordered(x, swap_core(x), core, 1)

    order_a = wide + [2, 1]

    def own_sequence(array, order, ties=()):
        mine = pick(array, parity)
        theirs = swap(pick(array, 1 - parity), 1)
        block = ordered(mine, theirs, parity, 0)
        return gather(block[None], order, 1, ties)[0]

    lanes = 384
    packed = jnp.concatenate(
        [
            w_square[0],
            jnp.pad(w_input[0], ((0, 0), (0, lanes - channels))),
            w_input[1],
            vec_d.T,
            jnp.zeros((own_w, lanes - channels - vec_d.shape[0]), b16),
        ],
        axis=1,
    )
    packed = both(gather(packed[None], order_a, 0))[0]
    square_first = packed[:, :width]
    packed = packed[:, width:]
    tall = (channels + 6 + 15) // 16 * 16
    v_key = packed[:, :tall]
    v_val = jnp.where(jnp.arange(tall) < channels, packed[:, lanes : lanes + tall], jnp.zeros((), b16))
    vecf = packed[:, lanes + channels : lanes + channels + vec_d.shape[0]].T.astype(f32)
    lat = own_sequence(latents, wide + [2])
    late_squares = lax.all_gather(w_square[1:], ("seq", "ctx"), axis=1, tiled=True)
    square = [square_first] + [late_squares[k] for k in range(9)]

    latent = lat.astype(f32)
    norm_a, unit_a, inv_a = layer_norm(latent, vecf[0], vecf[1], 1)
    low_a = norm_a.astype(b16)
    query = (matmul("id,de->ie", low_a, square[0]) + vecf[2]).astype(b16)
    gate = (matmul("dc,id->ci", v_key, query) * scale).astype(b16)
    gates = ordered(gate[None], swap(gate, 1)[None], parity, 0)

    gain_in = vec_c.astype(f32)
    norm_x, unit_x, inv_x = layer_norm(pixels.astype(f32), gain_in[0][:, None], gain_in[1][:, None], 1)
    low_x = jnp.pad(norm_x.astype(b16), ((0, 0), (0, tall - channels), (0, 0)))
    position = place * slots + jnp.arange(slots, dtype=jnp.int32)
    valid = (position[None, :] < lengths[:, None])[:, None, :]
    scores = matmul("qci,qcj->qij", gates, low_x)
    top = jnp.max(jnp.where(valid, scores, -1e30), axis=2)
    top_hi, top_lo = split_two(top)
    shift = top_hi.astype(f32) + top_lo.astype(f32)
    expo = jnp.where(valid, jnp.exp(scores - shift[..., None]), 0.0)
    total_hi, total_lo = split_two(jnp.sum(expo, axis=2))
    mixed = matmul("qij,qcj->qci", expo.astype(b16), low_x).astype(b16)
    row = jnp.arange(tall)[:, None]

    def write(v, parts):
        for k, part in enumerate(parts):
            v = jnp.where(row == channels + k, part[..., None, :], v)
        return v

    pay = write(mixed, [top_hi, top_lo, total_hi, total_lo])

    def opened(p):
        s = p[channels : channels + 4].astype(f32)
        return p.astype(f32), s[0] + s[1], s[2] + s[3]

    def merge(a, b):
        va, ta, la = opened(a)
        vb, tb, lb = opened(b)
        t = jnp.maximum(ta, tb)
        ea = jnp.exp(ta - t)
        eb = jnp.exp(tb - t)
        return va * ea + vb * eb, t, la * ea + lb * eb

    def closed(v, t, l):
        return write(v.astype(b16), split_two(t) + split_two(l))

    state = merge(pick(pay, parity), swap(pick(pay, 1 - parity), 1))
    for bit in [2] + wide:
        mine = closed(*state)
        state = merge(mine, swap(mine, bit))
    mix_sum, top_all, total_all = state
    mean_x = jnp.where(row < channels, mix_sum / total_all, 0.0)
    mean_low = mean_x.astype(b16)

    attended = (matmul("ci,dc->id", mean_low, v_val) + vecf[3]).astype(b16)
    after_cross = latent + matmul("id,de->ie", attended, square[1]) + vecf[4]
    norm_b, unit_b, inv_b = layer_norm(after_cross, vecf[5], vecf[6], 1)
    low_b = norm_b.astype(b16)
    ffn_pre = matmul("id,de->ie", low_b, square[2]) + vecf[7]
    ffn_act = jax.nn.gelu(ffn_pre).astype(b16)
    after_ffn = after_cross + matmul("id,de->ie", ffn_act, square[3]) + vecf[8]
    norm_c, unit_c, inv_c = layer_norm(after_ffn, vecf[9], vecf[10], 1)
    low_c = norm_c.astype(b16)

    def heads(x):
        return x.reshape(total_rows, H, head_size)

    self_query = (matmul("id,de->ie", low_c, square[4]) + vecf[11]).astype(b16)
    self_keys = matmul("id,de->ie", low_c, square[5]).astype(b16)
    self_values = (matmul("id,de->ie", low_c, square[6]) + vecf[12]).astype(b16)
    query_heads, key_heads, value_heads = heads(self_query), heads(self_keys), heads(self_values)
    self_scores = matmul("ihe,jhe->hij", query_heads, key_heads) * scale_self
    self_exp = jnp.exp(self_scores - jnp.max(self_scores, axis=2, keepdims=True))
    self_weight = self_exp / jnp.sum(self_exp, axis=2, keepdims=True)
    self_low = self_weight.astype(b16)
    self_mix = matmul("hij,jhe->ihe", self_low, value_heads).reshape(total_rows, width).astype(b16)
    after_self = after_ffn + matmul("id,de->ie", self_mix, square[7]) + vecf[13]
    norm_e, unit_e, inv_e = layer_norm(after_self, vecf[14], vecf[15], 1)
    low_e = norm_e.astype(b16)
    out_pre = matmul("id,de->ie", low_e, square[8]) + vecf[16]
    out_act = jax.nn.gelu(out_pre).astype(b16)
    final = (after_self + matmul("id,de->ie", out_act, square[9]) + vecf[17]).astype(b16)

    def own_rows(array):
        mine = lax.dynamic_slice_in_dim(array, place * rows, rows, 0)
        theirs = lax.dynamic_slice_in_dim(array, (place ^ 1) * rows, rows, 0)
        return ordered(mine[None], swap(theirs, 1)[None], parity, 0)

    latents_out = own_rows(final)

    cot = own_sequence(after(cotangent, low_b), wide + [2], (low_c, self_keys, self_mix))

    def share(a):
        parts = [lax.dynamic_slice_in_dim(a, s * n * own_w + pair * 2 * own_w, 2 * own_w, a.ndim - 1) for s in range(2)]
        return jnp.stack(parts, axis=0)

    def settle(x, axis):
        x = pick(x, core) + swap_core(pick(x, 1 - core))
        mine = lax.dynamic_slice_in_dim(x, parity * own_w, own_w, axis)
        theirs = lax.dynamic_slice_in_dim(x, (1 - parity) * own_w, own_w, axis)
        return mine + swap(theirs, 1)

    def weight_grad(a, r):
        return matmul("sia,ie->sae", jnp.moveaxis(share(a), 0, 0), r)

    def sums(x):
        return jnp.sum(x.astype(f32), axis=0)

    d_final = cot.astype(f32)
    round_nine = cot
    part9 = weight_grad(out_act, round_nine)
    d_out_pre = gelu_back(out_pre, matmul("ie,de->id", round_nine, square[9])).astype(b16)
    part8 = weight_grad(low_e, d_out_pre)
    d_norm_e = matmul("ie,de->id", d_out_pre, square[8])
    d_after_self = d_final + norm_back(d_norm_e, unit_e, inv_e, vecf[14], 1)
    round_seven = d_after_self.astype(b16)
    part7 = weight_grad(self_mix, round_seven)
    d_mix = matmul("ie,de->id", round_seven, square[7]).astype(b16)
    d_mix_heads = heads(d_mix)
    d_self_weight = matmul("ihe,jhe->hij", d_mix_heads, value_heads)
    d_self_scores = (
        self_weight * (d_self_weight - jnp.sum(d_self_weight * self_weight, axis=2, keepdims=True))
    ).astype(b16)
    d_self_query = (matmul("hij,jhe->ihe", d_self_scores, key_heads) * scale_self).reshape(total_rows, width).astype(b16)
    d_self_keys = (matmul("hij,ihe->jhe", d_self_scores, query_heads) * scale_self).reshape(total_rows, width).astype(b16)
    d_self_values = matmul("hij,ihe->jhe", self_low, d_mix_heads).reshape(total_rows, width).astype(b16)
    part4 = weight_grad(low_c, d_self_query)
    part5 = weight_grad(low_c, d_self_keys)
    part6 = weight_grad(low_c, d_self_values)
    d_norm_c = (
        matmul("ie,de->id", d_self_query, square[4])
        + matmul("ie,de->id", d_self_keys, square[5])
        + matmul("ie,de->id", d_self_values, square[6])
    )
    d_after_ffn = d_after_self + norm_back(d_norm_c, unit_c, inv_c, vecf[9], 1)
    round_three = d_after_ffn.astype(b16)
    part3 = weight_grad(ffn_act, round_three)
    d_ffn_pre = gelu_back(ffn_pre, matmul("ie,de->id", round_three, square[3])).astype(b16)
    part2 = weight_grad(low_b, d_ffn_pre)
    d_norm_b = matmul("ie,de->id", d_ffn_pre, square[2])
    d_after_cross = d_after_ffn + norm_back(d_norm_b, unit_b, inv_b, vecf[5], 1)
    round_one = d_after_cross.astype(b16)
    part1 = weight_grad(attended, round_one)
    d_attended = matmul("ie,de->id", round_one, square[1]).astype(b16)

    pull = matmul("dc,id->ci", v_val, d_attended).astype(b16)
    delta = jnp.sum(pull.astype(f32) * mean_x, axis=0)
    pieces = split_two(top_all) + split_two(total_all) + split_two(delta)
    sent = write(pull, pieces)
    sents = ordered(sent[None], swap(sent, 1)[None], parity, 0)
    pulls = sents
    side = sents[:, channels : channels + 6].astype(f32)
    top_q = side[:, 0] + side[:, 1]
    total_q = side[:, 2] + side[:, 3]
    delta_q = side[:, 4] + side[:, 5]
    scores_again = matmul("qci,qcj->qij", gates, low_x)
    weight = jnp.where(valid, jnp.exp(scores_again - top_q[..., None]), 0.0) / total_q[..., None]
    d_weight = matmul("qci,qcj->qij", pulls, low_x)
    d_scores = (weight * (d_weight - delta_q[..., None])).astype(b16)
    weight_low = weight.astype(b16)
    force = matmul("qij,qcj->qci", d_scores, low_x).astype(b16)
    d_in_norm = (matmul("qci,qij->qcj", gates, d_scores) + matmul("qci,qij->qcj", pulls, weight_low))[:, :channels]
    grad_pixels = norm_back(d_in_norm, unit_x, inv_x, gain_in[0][:, None], 1)
    grad_vc = jnp.stack([jnp.sum(d_in_norm * unit_x, axis=(0, 2)), jnp.sum(d_in_norm, axis=(0, 2))])
    grad_vc = grad_vc + swap_core(grad_vc)
    for bit in [1, 2] + wide:
        grad_vc = grad_vc + swap(grad_vc, bit)

    force_sum = pick(force, parity).astype(f32) + swap(pick(force, 1 - parity), 1).astype(f32)
    for bit in [2] + wide:
        mine = force_sum.astype(b16)
        force_sum = mine.astype(f32) + swap(mine, bit).astype(f32)
    force_low = (force_sum * scale).astype(b16)
    d_query = matmul("ci,dc->id", force_low, v_key).astype(b16)
    part0 = weight_grad(low_a, d_query)
    d_norm_a = matmul("ie,de->id", d_query, square[0])
    grad_lat = d_after_cross + norm_back(d_norm_a, unit_a, inv_a, vecf[0], 1)
    grad_latents = own_rows(grad_lat)

    share_q = share(query)
    share_att = share(d_attended)
    part_in = jnp.stack(
        [matmul("sia,ci->sac", share_q, force_low), matmul("sia,ci->sac", share_att, mean_low)], axis=1
    )[..., :channels]
    grad_input = settle(part_in, 1)
    vec_part = jnp.stack(
        [
            sums(d_norm_a * unit_a),
            sums(d_norm_a),
            sums(d_query),
            sums(d_attended),
            sums(round_one),
            sums(d_norm_b * unit_b),
            sums(d_norm_b),
            sums(d_ffn_pre),
            sums(round_three),
            sums(d_norm_c * unit_c),
            sums(d_norm_c),
            sums(d_self_query),
            sums(d_self_values),
            sums(round_seven),
            sums(d_norm_e * unit_e),
            sums(d_norm_e),
            sums(d_out_pre),
            sums(round_nine),
        ]
    )
    grad_vec = settle(share(vec_part), 1)
    late = settle(part0, 0)[None]
    mid = settle(jnp.stack([part1, part2, part3], axis=1), 1)
    heads_part = settle(jnp.stack([part4, part5, part6], axis=1), 1)
    early = settle(jnp.stack([part7, part8, part9], axis=1), 1)
    grad_square = jnp.concatenate([late, mid, heads_part, early], axis=0)
    return (latents_out, grad_latents, grad_pixels, grad_square, grad_input, grad_vec, grad_vc)


def solution(mesh):
    placed = (
        P("seq", None, "ctx"),
        P("seq"),
        P("seq", "ctx", None),
        P(None, ("seq", "ctx"), None),
        P(None, ("seq", "ctx"), None),
        P(None, ("seq", "ctx")),
        P(),
        P("seq", "ctx", None),
    )
    return jax.shard_map(
        body,
        mesh=mesh,
        in_specs=placed,
        out_specs=(
            P("seq", "ctx", None),
            P("seq", "ctx", None),
            P("seq", None, "ctx"),
            P(None, ("seq", "ctx"), None),
            P(None, ("seq", "ctx"), None),
            P(None, ("seq", "ctx")),
            P(),
        ),
        check_vma=False,
    )
```

```python
import math

import jax
import jax.numpy as jnp
from jax import lax
from jax.sharding import PartitionSpec as P

H = 8
epsilon = 1e-05
f32 = jnp.float32
b16 = jnp.bfloat16


def matmul(form, left, right):
    return jnp.einsum(form, left, right, preferred_element_type=f32)


def layer_norm(value, gain, shift, axis):
    center = value - jnp.mean(value, axis=axis, keepdims=True)
    spread = jnp.mean(center * center, axis=axis, keepdims=True)
    inverse = lax.rsqrt(spread + epsilon)
    unit = center * inverse
    return (unit * gain + shift, unit, inverse)


def norm_back(grad, unit, inverse, gain, axis):
    scaled = grad * gain
    inner = (
        scaled
        - jnp.mean(scaled, axis=axis, keepdims=True)
        - unit * jnp.mean(scaled * unit, axis=axis, keepdims=True)
    )
    return inner * inverse


def gelu_back(value, grad):
    unused, pull = jax.vjp(jax.nn.gelu, value)
    return pull(grad)[0]


def split_two(value):
    high = value.astype(b16)
    low = (value - high.astype(f32)).astype(b16)
    return high, low


def after(value, *needed):
    return lax.optimization_barrier((value,) + needed)[0]


def pick(array, index):
    return lax.dynamic_index_in_dim(array, index, 0, keepdims=False)


def body(pixels, lengths, latents, w_square, w_input, vec_d, vec_c, cotangent):
    n = lax.axis_size("ctx")
    bits_all = n.bit_length() - 1
    rows = latents.shape[1]
    width = latents.shape[2]
    own_w = w_square.shape[1]
    channels = pixels.shape[1]
    slots = pixels.shape[2]
    total_rows = rows * n
    head_size = width // H
    scale = 1.0 / math.sqrt(width)
    scale_self = 1.0 / math.sqrt(head_size)
    core = lax.axis_index("seq")
    place = lax.axis_index("ctx")
    parity = place & 1
    pair = place >> 1
    wide = [4 << i for i in range(bits_all - 2)]

    def swap(x, bit):
        return lax.ppermute(x, "ctx", [(i, i ^ bit) for i in range(n)])

    def swap_core(x):
        return lax.ppermute(x, "seq", [(0, 1), (1, 0)])

    def ordered(mine, other, flag, axis):
        first = jnp.where(flag == 0, mine, other)
        second = jnp.where(flag == 0, other, mine)
        return jnp.concatenate([first, second], axis=axis)

    def quad(x, low, high, axis):
        one, two, three = swap(x, low), swap(x, high), swap(x, low | high)
        bit_low, bit_high = (place // low) & 1, (place // high) & 1
        near = ordered(x, one, bit_low, axis)
        far = ordered(two, three, bit_low, axis)
        return ordered(near, far, bit_high, axis)

    def both(x):
        return ordered(x, swap_core(x), core, 1)

    def gather_wide(x):
        rest = list(wide)
        x = x[None]
        while len(rest) > 1:
            x = quad(x[None], rest[0], rest[1], 0)
            x = x.reshape((-1,) + x.shape[2:])
            rest = rest[2:]
        for bit in rest:
            x = ordered(x[None], swap(x[None], bit), (place // bit) & 1, 0)
            x = x.reshape((-1,) + x.shape[2:])
        return x

    def own_steps(array):
        other = yield swap(pick(array, 1 - parity), 1)
        x = ordered(pick(array, parity), other, parity, 0)[None]
        for bit in wide:
            other = yield swap(x, bit)
            x = ordered(x, other, (place // bit) & 1, 0)
        other = yield swap(x, 2)
        x = ordered(x[:, None], other[:, None], (place // 2) & 1, 1)
        return x.reshape(total_rows, width)

    lanes = 384
    packed = jnp.concatenate(
        [
            w_square[0],
            jnp.pad(w_input[0], ((0, 0), (0, lanes - channels))),
            w_input[1],
            vec_d.T,
            jnp.zeros((own_w, lanes - channels - vec_d.shape[0]), b16),
        ],
        axis=1,
    )
    packed = gather_wide(packed[None])[:, 0]
    packed = quad(packed[:, None], 1, 2, 1)
    packed = both(packed.reshape(1, n * own_w, -1))[0]
    square_first = packed[:, :width]
    packed = lax.optimization_barrier(packed[:, width:])
    tall = (channels + 6 + 15) // 16 * 16
    v_key = packed[:, :tall]
    v_val = jnp.where(jnp.arange(tall) < channels, packed[:, lanes : lanes + tall], jnp.zeros((), b16))
    vecf = packed[:, lanes + channels : lanes + channels + vec_d.shape[0]].T.astype(f32)
    lat = ordered(pick(latents, parity), swap(pick(latents, 1 - parity), 1), parity, 0)
    lat = gather_wide(lat[None])
    lat = ordered(lat, swap(lat, 2), (place // 2) & 1, 1).reshape(total_rows, width)
    late_squares = lax.all_gather(w_square[1:], ("seq", "ctx"), axis=1, tiled=True)
    square = [square_first] + [late_squares[k] for k in range(9)]

    latent = lat.astype(f32)
    norm_a, unit_a, inv_a = layer_norm(latent, vecf[0], vecf[1], 1)
    low_a = norm_a.astype(b16)
    query = (matmul("id,de->ie", low_a, square[0]) + vecf[2]).astype(b16)
    gate = (matmul("dc,id->ci", v_key, query) * scale).astype(b16)
    gates = ordered(gate[None], swap(gate, 1)[None], parity, 0)

    gain_in = vec_c.astype(f32)
    norm_x, unit_x, inv_x = layer_norm(pixels.astype(f32), gain_in[0][:, None], gain_in[1][:, None], 1)
    low_x = jnp.pad(norm_x.astype(b16), ((0, 0), (0, tall - channels), (0, 0)))
    position = place * slots + jnp.arange(slots, dtype=jnp.int32)
    valid = (position[None, :] < lengths[:, None])[:, None, :]
    scores = matmul("qci,qcj->qij", gates, low_x)
    top = jnp.max(jnp.where(valid, scores, -1e30), axis=2)
    top_hi, top_lo = split_two(top)
    shift = top_hi.astype(f32) + top_lo.astype(f32)
    expo = jnp.where(valid, jnp.exp(scores - shift[..., None]), 0.0)
    total_hi, total_lo = split_two(jnp.sum(expo, axis=2))
    mixed = matmul("qij,qcj->qci", expo.astype(b16), low_x).astype(b16)
    row = jnp.arange(tall)[:, None]

    def write(v, parts):
        for k, part in enumerate(parts):
            v = jnp.where(row == channels + k, part[..., None, :], v)
        return v

    pay = write(mixed, [top_hi, top_lo, total_hi, total_lo])

    def opened(p):
        s = p[channels : channels + 4].astype(f32)
        return p.astype(f32), s[0] + s[1], s[2] + s[3]

    def merge(a, b):
        va, ta, la = opened(a)
        vb, tb, lb = opened(b)
        t = jnp.maximum(ta, tb)
        ea = jnp.exp(ta - t)
        eb = jnp.exp(tb - t)
        return va * ea + vb * eb, t, la * ea + lb * eb

    def closed(v, t, l):
        return write(v.astype(b16), split_two(t) + split_two(l))

    state = merge(pick(pay, parity), swap(pick(pay, 1 - parity), 1))
    for bit in [2] + wide:
        mine = closed(*state)
        state = merge(mine, swap(mine, bit))
    mix_sum, top_all, total_all = state
    mean_x = jnp.where(row < channels, mix_sum / total_all, 0.0)
    mean_low = mean_x.astype(b16)

    attended = (matmul("ci,dc->id", mean_low, v_val) + vecf[3]).astype(b16)
    steps = own_steps(after(cotangent, attended))
    hanging = [next(steps)]
    gathered = []

    def pace(value):
        if not hanging:
            return value
        value, other = lax.optimization_barrier((value, hanging.pop()))
        try:
            hanging.append(steps.send(other))
        except StopIteration as stop:
            gathered.append(stop.value)
        return value

    after_cross = latent + matmul("id,de->ie", attended, square[1]) + vecf[4]
    norm_b, unit_b, inv_b = layer_norm(after_cross, vecf[5], vecf[6], 1)
    low_b = norm_b.astype(b16)
    ffn_pre = matmul("id,de->ie", low_b, square[2]) + vecf[7]
    ffn_act = pace(jax.nn.gelu(ffn_pre).astype(b16))
    after_ffn = after_cross + matmul("id,de->ie", ffn_act, square[3]) + vecf[8]
    norm_c, unit_c, inv_c = layer_norm(after_ffn, vecf[9], vecf[10], 1)
    low_c = pace(norm_c.astype(b16))

    def heads(x):
        return x.reshape(total_rows, H, head_size)

    self_query = (matmul("id,de->ie", low_c, square[4]) + vecf[11]).astype(b16)
    self_keys = matmul("id,de->ie", low_c, square[5]).astype(b16)
    self_values = (matmul("id,de->ie", low_c, square[6]) + vecf[12]).astype(b16)
    query_heads, key_heads, value_heads = heads(self_query), heads(self_keys), heads(self_values)
    self_scores = matmul("ihe,jhe->hij", query_heads, key_heads) * scale_self
    self_exp = jnp.exp(self_scores - jnp.max(self_scores, axis=2, keepdims=True))
    self_weight = self_exp / jnp.sum(self_exp, axis=2, keepdims=True)
    self_low = self_weight.astype(b16)
    self_mix = matmul("hij,jhe->ihe", self_low, value_heads).reshape(total_rows, width).astype(b16)
    self_mix = pace(self_mix)
    after_self = after_ffn + matmul("id,de->ie", self_mix, square[7]) + vecf[13]
    norm_e, unit_e, inv_e = layer_norm(after_self, vecf[14], vecf[15], 1)
    low_e = norm_e.astype(b16)
    out_pre = matmul("id,de->ie", low_e, square[8]) + vecf[16]
    out_act = pace(jax.nn.gelu(out_pre).astype(b16))
    final = (after_self + matmul("id,de->ie", out_act, square[9]) + vecf[17]).astype(b16)

    def own_rows(array):
        mine = lax.dynamic_slice_in_dim(array, place * rows, rows, 0)
        theirs = lax.dynamic_slice_in_dim(array, (place ^ 1) * rows, rows, 0)
        return ordered(mine[None], swap(theirs, 1)[None], parity, 0)

    latents_out = own_rows(final)

    part_rows = 2 * own_w
    aligned = max(part_rows, 128)
    base = pair * part_rows // aligned * aligned
    inner = pair * part_rows - base

    def share(a):
        return jnp.concatenate([lax.dynamic_slice_in_dim(a, s * n * own_w + base, aligned, 1) for s in range(2)], axis=1)

    def weight_grad(a, r):
        return matmul("ia,ie->ae", share(a), r)

    def window(part, which):
        return lax.dynamic_slice_in_dim(part, which * aligned + inner, part_rows, 0)

    def halves(x, which):
        return lax.dynamic_slice_in_dim(x, which * own_w, own_w, x.ndim - 2)

    def settle(parts):
        other = swap_core(jnp.stack([window(p, 1 - core) for p in parts]))
        return jnp.stack([window(p, core) for p in parts]) + other

    def settle_last(x):
        return halves(x, parity) + swap(halves(x, 1 - parity), 1)

    def sums(x):
        return jnp.sum(x.astype(f32), axis=0, keepdims=True)

    while hanging:
        pace(out_act)
    cot = gathered[0]
    d_final = cot.astype(f32)
    round_nine = cot
    d_out_pre = gelu_back(out_pre, matmul("ie,de->id", round_nine, square[9])).astype(b16)
    d_norm_e = matmul("ie,de->id", d_out_pre, square[8])
    d_after_self = d_final + norm_back(d_norm_e, unit_e, inv_e, vecf[14], 1)
    round_seven = d_after_self.astype(b16)
    d_mix = matmul("ie,de->id", round_seven, square[7]).astype(b16)
    d_mix_heads = heads(d_mix)
    d_self_weight = matmul("ihe,jhe->hij", d_mix_heads, value_heads)
    d_self_scores = (
        self_weight * (d_self_weight - jnp.sum(d_self_weight * self_weight, axis=2, keepdims=True))
    ).astype(b16)
    d_self_query = (matmul("hij,jhe->ihe", d_self_scores, key_heads) * scale_self).reshape(total_rows, width).astype(b16)
    d_self_keys = (matmul("hij,ihe->jhe", d_self_scores, query_heads) * scale_self).reshape(total_rows, width).astype(b16)
    d_self_values = matmul("hij,ihe->jhe", self_low, d_mix_heads).reshape(total_rows, width).astype(b16)
    d_norm_c = (
        matmul("ie,de->id", d_self_query, square[4])
        + matmul("ie,de->id", d_self_keys, square[5])
        + matmul("ie,de->id", d_self_values, square[6])
    )
    d_after_ffn = d_after_self + norm_back(d_norm_c, unit_c, inv_c, vecf[9], 1)
    round_three = d_after_ffn.astype(b16)
    d_ffn_pre = gelu_back(ffn_pre, matmul("ie,de->id", round_three, square[3])).astype(b16)
    d_norm_b = matmul("ie,de->id", d_ffn_pre, square[2])
    d_after_cross = d_after_ffn + norm_back(d_norm_b, unit_b, inv_b, vecf[5], 1)
    round_one = d_after_cross.astype(b16)
    d_attended = matmul("ie,de->id", round_one, square[1]).astype(b16)

    pull = matmul("dc,id->ci", v_val, d_attended).astype(b16)
    delta = jnp.sum(pull.astype(f32) * mean_x, axis=0)
    pieces = split_two(top_all) + split_two(total_all) + split_two(delta)
    sent = write(pull, pieces)
    other = swap(sent, 1)
    part9 = weight_grad(after(out_act, sent), round_nine)
    part8 = weight_grad(after(low_e, sent), d_out_pre)
    other = after(other, part9, part8)
    sents = ordered(sent[None], other[None], parity, 0)
    pulls = sents
    side = sents[:, channels : channels + 6].astype(f32)
    top_q = side[:, 0] + side[:, 1]
    total_q = side[:, 2] + side[:, 3]
    delta_q = side[:, 4] + side[:, 5]
    scores_again = matmul("qci,qcj->qij", gates, low_x)
    weight = jnp.where(valid, jnp.exp(scores_again - top_q[..., None]), 0.0) / total_q[..., None]
    d_weight = matmul("qci,qcj->qij", pulls, low_x)
    d_scores = (weight * (d_weight - delta_q[..., None])).astype(b16)
    weight_low = weight.astype(b16)
    force = matmul("qij,qcj->qci", d_scores, low_x).astype(b16)
    mine = pick(force, parity)
    other = swap(pick(force, 1 - parity), 1)
    held = after(d_scores, force)
    d_in_norm = (matmul("qci,qij->qcj", gates, held) + matmul("qci,qij->qcj", pulls, weight_low))[:, :channels]
    grad_pixels = norm_back(d_in_norm, unit_x, inv_x, gain_in[0][:, None], 1)
    grad_vc = [jnp.sum(d_in_norm * unit_x, axis=(0, 2)), jnp.sum(d_in_norm, axis=(0, 2))]
    grad_vc = jnp.pad(jnp.stack(grad_vc), ((0, 0), (0, total_rows - channels)))
    other = after(other, grad_vc)
    force_sum = mine.astype(f32) + other.astype(f32)
    work = [
        lambda t: [weight_grad(after(self_mix, t), round_seven), weight_grad(after(low_c, t), d_self_values)],
        lambda t: [weight_grad(after(low_c, t), d_self_keys), weight_grad(after(low_c, t), d_self_query)],
        lambda t: [
            weight_grad(after(ffn_act, t), round_three),
            weight_grad(after(low_b, t), d_ffn_pre),
            weight_grad(after(attended, t), round_one),
        ],
    ]
    ready = []
    for step, bit in enumerate([2] + wide):
        mine = write(force_sum.astype(b16), split_two(grad_vc[0]) + split_two(grad_vc[1]))
        other = swap(mine, bit)
        if step < len(work):
            ready.append(work[step](mine))
            other = after(other, *ready[-1])
        force_sum = mine.astype(f32) + other.astype(f32)
        grad_vc = jnp.stack([force_sum[channels] + force_sum[channels + 1], force_sum[channels + 2] + force_sum[channels + 3]])
    while len(ready) < len(work):
        ready.append(work[len(ready)](force_sum))
    part7, part6 = ready[0]
    part5, part4 = ready[1]
    part3, part2, part1 = ready[2]
    force_low = jnp.where(row < channels, force_sum * scale, 0.0).astype(b16)
    d_query = matmul("ci,dc->id", force_low, v_key).astype(b16)
    part0 = weight_grad(low_a, d_query)
    d_norm_a = matmul("ie,de->id", d_query, square[0])
    grad_lat = d_after_cross + norm_back(d_norm_a, unit_a, inv_a, vecf[0], 1)
    grad_latents = own_rows(grad_lat)

    part_q = matmul("ia,ci->ac", share(query), force_low)
    part_att = matmul("ia,ci->ac", share(d_attended), mean_low)
    pad_lanes = lanes - tall
    wide_all = width + 2 * lanes

    def gradients(which):
        full = [window(part0, which)]
        for part in (part_q, part_att):
            full.append(jnp.pad(window(part, which), ((0, 0), (0, pad_lanes))))
        return jnp.concatenate(full, axis=1)

    late_vec = jnp.concatenate([sums(d_norm_a * unit_a), sums(d_norm_a), sums(d_query), jnp.pad(grad_vc, ((0, 0), (0, width - total_rows)))], axis=0)
    early_vec = jnp.concatenate(
        [
            sums(d_attended),
            sums(round_one),
            sums(d_norm_b * unit_b),
            sums(d_norm_b),
            sums(d_ffn_pre),
            sums(round_three),
            sums(d_norm_c * unit_c),
            sums(d_norm_c),
            sums(d_self_query),
            sums(d_self_values),
            sums(round_seven),
            sums(d_norm_e * unit_e),
            sums(d_norm_e),
            sums(d_out_pre),
            sums(round_nine),
        ],
        axis=0,
    )
    vectors = jnp.concatenate([late_vec, early_vec, jnp.zeros((4, width), f32)], axis=0)
    tail = jnp.pad(vectors, ((0, 0), (0, wide_all - width)))
    own = jnp.concatenate([gradients(core), tail], axis=0)
    own = own + swap_core(jnp.concatenate([gradients(1 - core), tail], axis=0))

    def reduced(which):
        return jnp.concatenate([halves(own[:part_rows], which), own[part_rows:]], axis=0)

    own = reduced(parity) + swap(reduced(1 - parity), 1)
    late = own[None, :own_w, :width]
    grad_input = jnp.stack([own[:own_w, width : width + channels], own[:own_w, width + lanes : width + lanes + channels]])
    tail = own[own_w:, :width]
    grad_vc = tail[3:5, :channels]
    grad_vec = lax.dynamic_slice_in_dim(tail, core * n * own_w + place * own_w, own_w, 1)
    grad_vec = jnp.concatenate([grad_vec[:3], grad_vec[5 : 2 + vec_d.shape[0]]], axis=0)
    early = settle_last(settle([part7, part8, part9]))
    heads_part = settle_last(settle([part4, part5, part6]))
    mid = settle_last(settle([part1, part2, part3]))
    grad_square = jnp.concatenate([late, mid, heads_part, early], axis=0)
    return (latents_out, grad_latents, grad_pixels, grad_square, grad_input, grad_vec, grad_vc)


def solution(mesh):
    placed = (
        P("seq", None, "ctx"),
        P("seq"),
        P("seq", "ctx", None),
        P(None, ("seq", "ctx"), None),
        P(None, ("seq", "ctx"), None),
        P(None, ("seq", "ctx")),
        P(),
        P("seq", "ctx", None),
    )
    return jax.shard_map(
        body,
        mesh=mesh,
        in_specs=placed,
        out_specs=(
            P("seq", "ctx", None),
            P("seq", "ctx", None),
            P("seq", None, "ctx"),
            P(None, ("seq", "ctx"), None),
            P(None, ("seq", "ctx"), None),
            P(None, ("seq", "ctx")),
            P(),
        ),
        check_vma=False,
    )
```

```python
import math

import jax
import jax.numpy as jnp
from jax import lax
from jax.sharding import PartitionSpec as P

H = 8
epsilon = 1e-05
f32 = jnp.float32
b16 = jnp.bfloat16


def matmul(form, left, right):
    return jnp.einsum(form, left, right, preferred_element_type=f32)


def layer_norm(value, gain, shift, axis):
    center = value - jnp.mean(value, axis=axis, keepdims=True)
    spread = jnp.mean(center * center, axis=axis, keepdims=True)
    inverse = lax.rsqrt(spread + epsilon)
    unit = center * inverse
    return (unit * gain + shift, unit, inverse)


def norm_back(grad, unit, inverse, gain, axis):
    scaled = grad * gain
    inner = (
        scaled
        - jnp.mean(scaled, axis=axis, keepdims=True)
        - unit * jnp.mean(scaled * unit, axis=axis, keepdims=True)
    )
    return inner * inverse


def gelu_back(value, grad):
    unused, pull = jax.vjp(jax.nn.gelu, value)
    return pull(grad)[0]


def split_two(value):
    high = value.astype(b16)
    low = (value - high.astype(f32)).astype(b16)
    return high, low


def after(value, *needed):
    return lax.optimization_barrier((value,) + needed)[0]


def pick(array, index):
    return lax.dynamic_index_in_dim(array, index, 0, keepdims=False)


def body(pixels, lengths, latents, w_square, w_input, vec_d, vec_c, cotangent):
    n = lax.axis_size("ctx")
    bits_all = n.bit_length() - 1
    rows = latents.shape[1]
    width = latents.shape[2]
    own_w = w_square.shape[1]
    channels = pixels.shape[1]
    slots = pixels.shape[2]
    total_rows = rows * n
    head_size = width // H
    scale = 1.0 / math.sqrt(width)
    scale_self = 1.0 / math.sqrt(head_size)
    core = lax.axis_index("seq")
    place = lax.axis_index("ctx")
    parity = place & 1
    pair = place >> 1
    wide = [4 << i for i in range(bits_all - 2)]

    def swap(x, bit):
        return lax.ppermute(x, "ctx", [(i, i ^ bit) for i in range(n)])

    def swap_core(x):
        return lax.ppermute(x, "seq", [(0, 1), (1, 0)])

    def ordered(mine, other, flag, axis):
        first = jnp.where(flag == 0, mine, other)
        second = jnp.where(flag == 0, other, mine)
        return jnp.concatenate([first, second], axis=axis)

    def quad(x, low, high, axis):
        one, two, three = swap(x, low), swap(x, high), swap(x, low | high)
        bit_low, bit_high = (place // low) & 1, (place // high) & 1
        near = ordered(x, one, bit_low, axis)
        far = ordered(two, three, bit_low, axis)
        return ordered(near, far, bit_high, axis)

    def both(x):
        return ordered(x, swap_core(x), core, 1)

    def gather_wide(x):
        rest = list(wide)
        x = x[None]
        while len(rest) > 1:
            x = quad(x[None], rest[0], rest[1], 0)
            x = x.reshape((-1,) + x.shape[2:])
            rest = rest[2:]
        for bit in rest:
            x = ordered(x[None], swap(x[None], bit), (place // bit) & 1, 0)
            x = x.reshape((-1,) + x.shape[2:])
        return x

    def own_steps(array):
        other = yield swap(pick(array, 1 - parity), 1)
        x = ordered(pick(array, parity), other, parity, 0)[None]
        for bit in wide:
            other = yield swap(x, bit)
            x = ordered(x, other, (place // bit) & 1, 0)
        other = yield swap(x, 2)
        x = ordered(x[:, None], other[:, None], (place // 2) & 1, 1)
        return x.reshape(total_rows, width)

    lanes = 384
    packed = jnp.concatenate(
        [
            w_square[0],
            jnp.pad(w_input[0], ((0, 0), (0, lanes - channels))),
            w_input[1],
            vec_d.T,
            jnp.zeros((own_w, lanes - channels - vec_d.shape[0]), b16),
        ],
        axis=1,
    )
    packed = gather_wide(packed[None])[:, 0]
    packed = quad(packed[:, None], 1, 2, 1)
    packed = both(packed.reshape(1, n * own_w, -1))[0]
    square_first = packed[:, :width]
    packed = lax.optimization_barrier(packed[:, width:])
    tall = (channels + 6 + 15) // 16 * 16
    v_key = packed[:, :tall]
    v_val = jnp.where(jnp.arange(tall) < channels, packed[:, lanes : lanes + tall], jnp.zeros((), b16))
    vecf = packed[:, lanes + channels : lanes + channels + vec_d.shape[0]].T.astype(f32)
    lat = ordered(pick(latents, parity), swap(pick(latents, 1 - parity), 1), parity, 0)
    lat = gather_wide(lat[None])
    lat = ordered(lat, swap(lat, 2), (place // 2) & 1, 1).reshape(total_rows, width)
    late_squares = lax.all_gather(w_square[1:], ("seq", "ctx"), axis=1, tiled=True)
    square = [square_first] + [late_squares[k] for k in range(9)]

    latent = lat.astype(f32)
    norm_a, unit_a, inv_a = layer_norm(latent, vecf[0], vecf[1], 1)
    low_a = norm_a.astype(b16)
    query = (matmul("id,de->ie", low_a, square[0]) + vecf[2]).astype(b16)
    gate = (matmul("dc,id->ci", v_key, query) * scale).astype(b16)
    gates = ordered(gate[None], swap(gate, 1)[None], parity, 0)

    gain_in = vec_c.astype(f32)
    norm_x, unit_x, inv_x = layer_norm(pixels.astype(f32), gain_in[0][:, None], gain_in[1][:, None], 1)
    low_x = jnp.pad(norm_x.astype(b16), ((0, 0), (0, tall - channels), (0, 0)))
    position = place * slots + jnp.arange(slots, dtype=jnp.int32)
    valid = (position[None, :] < lengths[:, None])[:, None, :]
    scores = matmul("qci,qcj->qij", gates, low_x)
    top = jnp.max(jnp.where(valid, scores, -1e30), axis=2)
    top_hi, top_lo = split_two(top)
    shift = top_hi.astype(f32) + top_lo.astype(f32)
    expo = jnp.where(valid, jnp.exp(scores - shift[..., None]), 0.0)
    total_hi, total_lo = split_two(jnp.sum(expo, axis=2))
    mixed = matmul("qij,qcj->qci", expo.astype(b16), low_x).astype(b16)
    row = jnp.arange(tall)[:, None]

    def write(v, parts):
        for k, part in enumerate(parts):
            v = jnp.where(row == channels + k, part[..., None, :], v)
        return v

    pay = write(mixed, [top_hi, top_lo, total_hi, total_lo])

    def opened(p):
        s = p[channels : channels + 4].astype(f32)
        return p.astype(f32), s[0] + s[1], s[2] + s[3]

    def merge(a, b):
        va, ta, la = opened(a)
        vb, tb, lb = opened(b)
        t = jnp.maximum(ta, tb)
        ea = jnp.exp(ta - t)
        eb = jnp.exp(tb - t)
        return va * ea + vb * eb, t, la * ea + lb * eb

    def closed(v, t, l):
        return write(v.astype(b16), split_two(t) + split_two(l))

    state = merge(pick(pay, parity), swap(pick(pay, 1 - parity), 1))
    for bit in [2] + wide:
        mine = closed(*state)
        state = merge(mine, swap(mine, bit))
    mix_sum, top_all, total_all = state
    mean_x = jnp.where(row < channels, mix_sum / total_all, 0.0)
    mean_low = mean_x.astype(b16)

    attended = (matmul("ci,dc->id", mean_low, v_val) + vecf[3]).astype(b16)
    steps = own_steps(after(cotangent, attended))
    hanging = [next(steps)]
    gathered = []

    def pace(value):
        if not hanging:
            return value
        value, other = lax.optimization_barrier((value, hanging.pop()))
        try:
            hanging.append(steps.send(other))
        except StopIteration as stop:
            gathered.append(stop.value)
        return value

    after_cross = latent + matmul("id,de->ie", attended, square[1]) + vecf[4]
    norm_b, unit_b, inv_b = layer_norm(after_cross, vecf[5], vecf[6], 1)
    low_b = norm_b.astype(b16)
    ffn_pre = matmul("id,de->ie", low_b, square[2]) + vecf[7]
    ffn_act = pace(jax.nn.gelu(ffn_pre).astype(b16))
    after_ffn = after_cross + matmul("id,de->ie", ffn_act, square[3]) + vecf[8]
    norm_c, unit_c, inv_c = layer_norm(after_ffn, vecf[9], vecf[10], 1)
    low_c = pace(norm_c.astype(b16))

    def heads(x):
        return x.reshape(total_rows, H, head_size)

    self_query = (matmul("id,de->ie", low_c, square[4]) + vecf[11]).astype(b16)
    self_keys = matmul("id,de->ie", low_c, square[5]).astype(b16)
    self_values = (matmul("id,de->ie", low_c, square[6]) + vecf[12]).astype(b16)
    query_heads, key_heads, value_heads = heads(self_query), heads(self_keys), heads(self_values)
    self_scores = matmul("ihe,jhe->hij", query_heads, key_heads) * scale_self
    self_exp = jnp.exp(self_scores - jnp.max(self_scores, axis=2, keepdims=True))
    self_weight = self_exp / jnp.sum(self_exp, axis=2, keepdims=True)
    self_low = self_weight.astype(b16)
    self_mix = matmul("hij,jhe->ihe", self_low, value_heads).reshape(total_rows, width).astype(b16)
    self_mix = pace(self_mix)
    after_self = after_ffn + matmul("id,de->ie", self_mix, square[7]) + vecf[13]
    norm_e, unit_e, inv_e = layer_norm(after_self, vecf[14], vecf[15], 1)
    low_e = norm_e.astype(b16)
    out_pre = matmul("id,de->ie", low_e, square[8]) + vecf[16]
    out_act = pace(jax.nn.gelu(out_pre).astype(b16))
    final = (after_self + matmul("id,de->ie", out_act, square[9]) + vecf[17]).astype(b16)

    def own_rows(array):
        mine = lax.dynamic_slice_in_dim(array, place * rows, rows, 0)
        theirs = lax.dynamic_slice_in_dim(array, (place ^ 1) * rows, rows, 0)
        return ordered(mine[None], swap(theirs, 1)[None], parity, 0)

    latents_out = own_rows(final)

    part_rows = 2 * own_w
    aligned = max(part_rows, 128)
    base = pair * part_rows // aligned * aligned
    inner = pair * part_rows - base

    def share(a):
        return jnp.concatenate([lax.dynamic_slice_in_dim(a, s * n * own_w + base, aligned, 1) for s in range(2)], axis=1)

    def weight_grad(a, r):
        return matmul("ia,ie->ae", share(a), r)

    def window(part, which):
        return lax.dynamic_slice_in_dim(part, which * aligned + inner, part_rows, 0)

    def halves(x, which):
        return lax.dynamic_slice_in_dim(x, which * own_w, own_w, x.ndim - 2)

    def settle(parts, extra=()):
        return swap_core(jnp.concatenate([window(p, 1 - core) for p in parts] + list(extra), axis=0))

    def settled(parts, other, extra=()):
        return jnp.concatenate([window(p, core) for p in parts] + list(extra), axis=0) + other

    def halved(x, count, which):
        top = x[: count * part_rows].reshape(count, part_rows, -1)
        top = halves(top, which).reshape(count * own_w, -1)
        return jnp.concatenate([top, x[count * part_rows :]], axis=0)

    def sums(x):
        return jnp.sum(x.astype(f32), axis=0, keepdims=True)

    while hanging:
        pace(out_act)
    cot = gathered[0]
    d_final = cot.astype(f32)
    round_nine = cot
    d_out_pre = gelu_back(out_pre, matmul("ie,de->id", round_nine, square[9])).astype(b16)
    d_norm_e = matmul("ie,de->id", d_out_pre, square[8])
    d_after_self = d_final + norm_back(d_norm_e, unit_e, inv_e, vecf[14], 1)
    round_seven = d_after_self.astype(b16)
    d_mix = matmul("ie,de->id", round_seven, square[7]).astype(b16)
    d_mix_heads = heads(d_mix)
    d_self_weight = matmul("ihe,jhe->hij", d_mix_heads, value_heads)
    d_self_scores = (
        self_weight * (d_self_weight - jnp.sum(d_self_weight * self_weight, axis=2, keepdims=True))
    ).astype(b16)
    d_self_query = (matmul("hij,jhe->ihe", d_self_scores, key_heads) * scale_self).reshape(total_rows, width).astype(b16)
    d_self_keys = (matmul("hij,ihe->jhe", d_self_scores, query_heads) * scale_self).reshape(total_rows, width).astype(b16)
    d_self_values = matmul("hij,ihe->jhe", self_low, d_mix_heads).reshape(total_rows, width).astype(b16)
    d_norm_c = (
        matmul("ie,de->id", d_self_query, square[4])
        + matmul("ie,de->id", d_self_keys, square[5])
        + matmul("ie,de->id", d_self_values, square[6])
    )
    d_after_ffn = d_after_self + norm_back(d_norm_c, unit_c, inv_c, vecf[9], 1)
    round_three = d_after_ffn.astype(b16)
    d_ffn_pre = gelu_back(ffn_pre, matmul("ie,de->id", round_three, square[3])).astype(b16)
    d_norm_b = matmul("ie,de->id", d_ffn_pre, square[2])
    d_after_cross = d_after_ffn + norm_back(d_norm_b, unit_b, inv_b, vecf[5], 1)
    round_one = d_after_cross.astype(b16)
    d_attended = matmul("ie,de->id", round_one, square[1]).astype(b16)

    pull = matmul("dc,id->ci", v_val, d_attended).astype(b16)
    delta = jnp.sum(pull.astype(f32) * mean_x, axis=0)
    pieces = split_two(top_all) + split_two(total_all) + split_two(delta)
    sent = write(pull, pieces)
    other = swap(sent, 1)
    part9 = weight_grad(after(out_act, sent), round_nine)
    part8 = weight_grad(after(low_e, sent), d_out_pre)
    other = after(other, part9, part8)
    sents = ordered(sent[None], other[None], parity, 0)
    pulls = sents
    side = sents[:, channels : channels + 6].astype(f32)
    top_q = side[:, 0] + side[:, 1]
    total_q = side[:, 2] + side[:, 3]
    delta_q = side[:, 4] + side[:, 5]
    scores_again = matmul("qci,qcj->qij", gates, low_x)
    weight = jnp.where(valid, jnp.exp(scores_again - top_q[..., None]), 0.0) / total_q[..., None]
    d_weight = matmul("qci,qcj->qij", pulls, low_x)
    d_scores = (weight * (d_weight - delta_q[..., None])).astype(b16)
    weight_low = weight.astype(b16)
    force = matmul("qij,qcj->qci", d_scores, low_x).astype(b16)
    mine = pick(force, parity)
    other = swap(pick(force, 1 - parity), 1)
    held = after(d_scores, force)
    d_in_norm = (matmul("qci,qij->qcj", gates, held) + matmul("qci,qij->qcj", pulls, weight_low))[:, :channels]
    grad_pixels = norm_back(d_in_norm, unit_x, inv_x, gain_in[0][:, None], 1)
    grad_vc = [jnp.sum(d_in_norm * unit_x, axis=(0, 2)), jnp.sum(d_in_norm, axis=(0, 2))]
    grad_vc = jnp.pad(jnp.stack(grad_vc), ((0, 0), (0, total_rows - channels)))
    other = after(other, grad_vc)
    early_vec = lambda: jnp.concatenate(
        [
            sums(d_attended),
            sums(round_one),
            sums(d_norm_b * unit_b),
            sums(d_norm_b),
            sums(d_ffn_pre),
            sums(round_three),
            sums(d_norm_c * unit_c),
            sums(d_norm_c),
            sums(d_self_query),
            sums(d_self_values),
            sums(round_seven),
            sums(d_norm_e * unit_e),
            sums(d_norm_e),
            sums(d_out_pre),
            sums(round_nine),
            jnp.zeros((1, width), f32),
        ],
        axis=0,
    )
    store = {"first": [part9, part8]}

    def work_one(t):
        store["first"] += [weight_grad(after(self_mix, t), round_seven), weight_grad(after(low_c, t), d_self_values)]
        return store["first"][2:]

    def work_two(t):
        held = after(store["first"][0], t)
        store["first"][0] = held
        got = settle(store["first"])
        store["second"] = [
            weight_grad(after(low_c, t), d_self_keys),
            weight_grad(after(low_c, t), d_self_query),
            weight_grad(after(ffn_act, t), round_three),
        ]
        store["vec"] = early_vec()
        store["first"] = settled(store["first"], got)
        return store["second"] + [store["first"], store["vec"]]

    def work_three(t):
        mine = after(store["first"], t)
        got = swap(halved(mine, 4, 1 - parity), 1)
        other = settle([after(store["second"][0], t)] + store["second"][1:], [store["vec"]])
        store["third"] = [weight_grad(after(low_b, t), d_ffn_pre), weight_grad(after(attended, t), round_one)]
        store["second"] = settled(store["second"], other, [store["vec"]])
        store["first"] = halved(mine, 4, parity) + got
        return store["third"] + [store["first"], store["second"]]

    def work_four(t):
        mine = after(store["second"], t)
        got = swap(halved(mine, 3, 1 - parity), 1)
        other = settle([after(store["third"][0], t)] + store["third"][1:])
        store["third"] = settled(store["third"], other)
        store["second"] = halved(mine, 3, parity) + got
        return [store["second"], store["third"]]

    work = [work_one, work_two, work_three, work_four]
    other = after(other, *work[0](force))
    force_sum = mine.astype(f32) + other.astype(f32)
    done = 1
    for step, bit in enumerate([2] + wide):
        mine = write(force_sum.astype(b16), split_two(grad_vc[0]) + split_two(grad_vc[1]))
        other = swap(mine, bit)
        if done < len(work):
            other = after(other, *work[done](mine))
            done += 1
        force_sum = mine.astype(f32) + other.astype(f32)
        grad_vc = jnp.stack([force_sum[channels] + force_sum[channels + 1], force_sum[channels + 2] + force_sum[channels + 3]])
    while done < len(work):
        work[done](force_sum)
        done += 1
    mine = after(store["third"], force_sum)
    third_other = swap(halved(mine, 2, 1 - parity), 1)
    third = halved(mine, 2, parity) + third_other
    force_low = jnp.where(row < channels, force_sum * scale, 0.0).astype(b16)
    d_query = matmul("ci,dc->id", force_low, v_key).astype(b16)
    part0 = weight_grad(low_a, d_query)
    d_norm_a = matmul("ie,de->id", d_query, square[0])
    grad_lat = d_after_cross + norm_back(d_norm_a, unit_a, inv_a, vecf[0], 1)
    grad_latents = own_rows(grad_lat)

    part_q = matmul("ia,ci->ac", share(query), force_low)
    part_att = matmul("ia,ci->ac", share(d_attended), mean_low)
    pad_lanes = lanes - tall
    wide_all = width + 2 * lanes

    def gradients(which):
        full = [window(part0, which)]
        for part in (part_q, part_att):
            full.append(jnp.pad(window(part, which), ((0, 0), (0, pad_lanes))))
        return jnp.concatenate(full, axis=1)

    late_vec = jnp.concatenate([sums(d_norm_a * unit_a), sums(d_norm_a), sums(d_query), jnp.pad(grad_vc, ((0, 0), (0, width - total_rows)))], axis=0)
    vectors = jnp.concatenate([late_vec, jnp.zeros((3, width), f32)], axis=0)
    tail = jnp.pad(vectors, ((0, 0), (0, wide_all - width)))
    own = jnp.concatenate([gradients(core), tail], axis=0)
    own = own + swap_core(jnp.concatenate([gradients(1 - core), tail], axis=0))

    def reduced(which):
        return jnp.concatenate([halves(own[:part_rows], which), own[part_rows:]], axis=0)

    own = reduced(parity) + swap(reduced(1 - parity), 1)
    late = own[None, :own_w, :width]
    grad_input = jnp.stack([own[:own_w, width : width + channels], own[:own_w, width + lanes : width + lanes + channels]])
    tail = own[own_w:, :width]
    grad_vc = tail[3:5, :channels]
    vectors = jnp.concatenate([tail[:3], store["second"][3 * own_w :]], axis=0)
    grad_vec = lax.dynamic_slice_in_dim(vectors, core * n * own_w + place * own_w, own_w, 1)[: vec_d.shape[0]]
    nine, eight, seven, six = store["first"].reshape(4, own_w, width)
    five, four, three = store["second"][: 3 * own_w].reshape(3, own_w, width)
    two, one = third.reshape(2, own_w, width)
    grad_square = jnp.stack([late[0], one, two, three, four, five, six, seven, eight, nine])
    return (latents_out, grad_latents, grad_pixels, grad_square, grad_input, grad_vec, grad_vc)


def solution(mesh):
    placed = (
        P("seq", None, "ctx"),
        P("seq"),
        P("seq", "ctx", None),
        P(None, ("seq", "ctx"), None),
        P(None, ("seq", "ctx"), None),
        P(None, ("seq", "ctx")),
        P(),
        P("seq", "ctx", None),
    )
    return jax.shard_map(
        body,
        mesh=mesh,
        in_specs=placed,
        out_specs=(
            P("seq", "ctx", None),
            P("seq", "ctx", None),
            P("seq", None, "ctx"),
            P(None, ("seq", "ctx"), None),
            P(None, ("seq", "ctx"), None),
            P(None, ("seq", "ctx")),
            P(),
        ),
        check_vma=False,
    )
```

```python
import math

import jax
import jax.numpy as jnp
from jax import lax
from jax.experimental import pallas as pl
from jax.experimental.pallas import tpu as pltpu
from jax.sharding import PartitionSpec as P

H = 8
epsilon = 1e-05
f32 = jnp.float32
b16 = jnp.bfloat16


def matmul(form, left, right):
    return jnp.einsum(form, left, right, preferred_element_type=f32)


def layer_norm(value, gain, shift, axis):
    center = value - jnp.mean(value, axis=axis, keepdims=True)
    spread = jnp.mean(center * center, axis=axis, keepdims=True)
    inverse = lax.rsqrt(spread + epsilon)
    unit = center * inverse
    return (unit * gain + shift, unit, inverse)


def norm_back(grad, unit, inverse, gain, axis):
    scaled = grad * gain
    inner = (
        scaled
        - jnp.mean(scaled, axis=axis, keepdims=True)
        - unit * jnp.mean(scaled * unit, axis=axis, keepdims=True)
    )
    return inner * inverse


def split_two(value):
    high = value.astype(b16)
    low = (value - high.astype(f32)).astype(b16)
    return high, low


def after(value, *needed):
    return lax.optimization_barrier((value,) + needed)[0]


def pick(array, index):
    return lax.dynamic_index_in_dim(array, index, 0, keepdims=False)


def latent_part(attended, lat, vectors, planes, numbers, part_rows, aligned, scale_self):
    total, width = lat.shape
    head = width // H
    extra = vectors.shape[0]
    out_rows = 9 * part_rows + extra
    shares = 2 * aligned
    stacked = shares + 16
    chunk = 32
    block = 256
    part = 128
    cubic = 0.044715
    root = math.sqrt(2.0 / math.pi)

    def kernel(
        num, att, lat_ref, vec, planes_ref, final, d_att, stream_out, keep, send,
        w, cot, low_b, act_b, low_c, q, k, v, mix, low_e, act_e, weights,
        unit_b, unit_c, unit_e, pre_b, pre_e, inv_b, inv_c, inv_e, stream, t, r, small, lhs, sems,
    ):
        parity, core, inner = num[0], num[1], num[4]

        def load(plane, slot, sem):
            return pltpu.make_async_copy(planes_ref.at[plane], w.at[slot], sems.at[sem])

        cot_copy = pltpu.make_async_copy(
            planes_ref.at[9 + parity, pl.ds(pl.multiple_of(core * total, total), total), :], cot, sems.at[11]
        )
        copies = [load(i, i, i) for i in range(7)]
        for copy in copies:
            copy.start()
        cot_copy.start()
        row_eight, row_nine = load(7, 0, 7), load(8, 1, 8)
        again_two, again_one = load(1, 1, 9), load(0, 0, 10)

        lhs[pl.ds(shares, 16), :] = jnp.ones((16, total), b16)

        def each(size, body, carry=None):
            def step(i, c):
                return body(pl.ds(pl.multiple_of(i * size, size), size), c)

            return lax.fori_loop(0, total // size, step, 0 if carry is None else carry)

        def product(a, slot, flip):
            dims = (((1,), (1 if flip else 0,)), ((), ()))
            return lax.dot_general(a, w[slot], dims, preferred_element_type=f32)

        def into_t(a_ref, slot, flip=False, add=False):
            def body(rows, c):
                o = product(a_ref[rows, :], slot, flip)
                t[rows, :] = t[rows, :] + o if add else o
                return c

            each(block, body)

        def into_low(a_ref, slot, out, flip=False, bias=None):
            def body(rows, c):
                o = product(a_ref[rows, :], slot, flip)
                if bias is not None:
                    o = o + vec[bias : bias + 1, :]
                out[rows, :] = o.astype(b16)
                return c

            each(block, body)

        def row_of(i):
            return vec[i : i + 1, :]

        def residual(before, bias, unit, inv, low, gain):
            def body(rows, c):
                x = before[rows, :].astype(f32) + t[rows, :] + row_of(bias)
                stream[rows, :] = x
                center = x - jnp.mean(x, axis=1, keepdims=True)
                inverse = lax.rsqrt(jnp.mean(center * center, axis=1, keepdims=True) + epsilon)
                u = center * inverse
                unit[rows, :] = u
                inv[rows, :] = jnp.broadcast_to(inverse, (chunk, 128))
                low[rows, :] = (u * row_of(gain) + row_of(gain + 1)).astype(b16)
                return c

            each(chunk, body)

        def activate(bias, pre, act):
            def body(rows, c):
                x = t[rows, :] + row_of(bias)
                pre[rows, :] = x
                act[rows, :] = (0.5 * x * (1.0 + jnp.tanh(root * (x + cubic * (x * x * x))))).astype(b16)
                return c

            each(chunk, body)

        def activate_back(pre):
            def body(rows, c):
                x = pre[rows, :]
                square = x * x
                h = jnp.tanh(root * (x + cubic * (square * x)))
                slope = 0.5 * (1.0 + h) + 0.5 * x * (1.0 - h * h) * (root * (1.0 + 3.0 * cubic * square))
                r[rows, :] = (t[rows, :] * slope).astype(b16)
                return c

            each(chunk, body)

        def norm_grad(before, unit, inv, gain, place):
            def body(rows, c):
                g, u = t[rows, :], unit[rows, :]
                scaled = g * row_of(gain)
                inner_grad = (
                    scaled
                    - jnp.mean(scaled, axis=1, keepdims=True)
                    - u * jnp.mean(scaled * u, axis=1, keepdims=True)
                )
                x = before[rows, :].astype(f32) + inner_grad * inv[rows, 0:1]
                stream[rows, :] = x
                r[rows, :] = x.astype(b16)
                first = c[0] + jnp.sum((g * u).reshape(chunk // 8, 8, width), axis=0)
                second = c[1] + jnp.sum(g.reshape(chunk // 8, 8, width), axis=0)
                return first, second

            zero = jnp.zeros((8, width), f32)
            first, second = each(chunk, body, (zero, zero))
            put_sum(place, jnp.sum(first, axis=0, keepdims=True))
            put_sum(place + 1, jnp.sum(second, axis=0, keepdims=True))

        def put_sum(place, value):
            keep[pl.ds(9 * part_rows + place, 1), :] = value
            send[pl.ds(9 * part_rows + place, 1), :] = value

        def gradient(index, a_ref, r_ref, place=None):
            for s in range(2):
                columns = a_ref[:, pl.ds(pl.multiple_of(num[2 + s], 128), aligned)]
                lhs[pl.ds(s * aligned, aligned), :] = columns.T
            t[pl.ds(0, stacked), :] = jnp.dot(lhs[...], r_ref[...], preferred_element_type=f32)
            near = pl.multiple_of(core * aligned + inner, 8)
            far = pl.multiple_of((1 - core) * aligned + inner, 8)
            keep[pl.ds(index * part_rows, part_rows), :] = t[pl.ds(near, part_rows), :]
            send[pl.ds(index * part_rows, part_rows), :] = t[pl.ds(far, part_rows), :]
            if place is not None:
                put_sum(place, t[pl.ds(shares, 1), :])

        for place in (keep, send):
            place[pl.ds(9 * part_rows, extra), :] = jnp.zeros((extra, width), f32)

        copies[0].wait()
        into_t(att, 0)
        row_eight.start()
        residual(lat_ref, 4, unit_b, inv_b, low_b, 5)
        copies[1].wait()
        into_t(low_b, 1)
        row_nine.start()
        activate(7, pre_b, act_b)
        copies[2].wait()
        into_t(act_b, 2)
        residual(stream, 8, unit_c, inv_c, low_c, 9)
        copies[3].wait()
        into_low(low_c, 3, q, bias=11)
        copies[4].wait()
        into_low(low_c, 4, k)
        copies[5].wait()
        into_low(low_c, 5, v, bias=12)
        for h in range(H):
            cols = slice(h * head, (h + 1) * head)

            def attend(rows, c):
                s = scale_self * lax.dot_general(
                    q[rows, cols], k[:, cols], (((1,), (1,)), ((), ())), preferred_element_type=f32
                )
                e = jnp.exp(s - jnp.max(s, axis=1, keepdims=True))
                low = (e / jnp.sum(e, axis=1, keepdims=True)).astype(b16)
                weights[h, rows, :] = low
                mix[rows, cols] = jnp.dot(low, v[:, cols], preferred_element_type=f32).astype(b16)
                return c

            each(part, attend)
        copies[6].wait()
        into_t(mix, 6)
        residual(stream, 13, unit_e, inv_e, low_e, 14)
        row_eight.wait()
        into_t(low_e, 0)
        activate(16, pre_e, act_e)
        row_nine.wait()
        into_t(act_e, 1)

        def finish(rows, c):
            final[rows, :] = (stream[rows, :] + t[rows, :] + row_of(17)).astype(b16)
            return c

        each(chunk, finish)

        cot_copy.wait()
        into_t(cot, 1, flip=True)
        again_two.start()
        activate_back(pre_e)
        gradient(8, act_e, cot, 17)
        gradient(7, low_e, r, 16)
        into_t(r, 0, flip=True)
        again_one.start()
        norm_grad(cot, unit_e, inv_e, 14, 14)
        gradient(6, mix, r, 13)
        into_low(r, 6, d_att, flip=True)
        for h in range(H):
            cols = slice(h * head, (h + 1) * head)
            turned = (((0,), (0,)), ((), ()))
            small[...] = lax.dot_general(weights[h], d_att[:, cols], turned, preferred_element_type=f32).astype(b16)

            def attend_back(rows, c):
                d_weight = lax.dot_general(
                    d_att[rows, cols], v[:, cols], (((1,), (1,)), ((), ())), preferred_element_type=f32
                )
                weight = weights[h, rows, :].astype(f32)
                d_scores = weight * (d_weight - jnp.sum(d_weight * weight, axis=1, keepdims=True))
                d_scores = d_scores.astype(b16)
                weights[h, rows, :] = d_scores
                d_query = jnp.dot(d_scores, k[:, cols], preferred_element_type=f32) * scale_self
                d_att[rows, cols] = d_query.astype(b16)
                return c

            each(part, attend_back)
            d_keys = lax.dot_general(weights[h], q[:, cols], turned, preferred_element_type=f32) * scale_self
            k[:, cols] = d_keys.astype(b16)
            v[:, cols] = small[...]
        gradient(5, low_c, v, 12)
        gradient(4, low_c, k)
        gradient(3, low_c, d_att, 11)
        into_t(d_att, 3, flip=True)
        into_t(k, 4, flip=True, add=True)
        into_t(v, 5, flip=True, add=True)
        norm_grad(stream, unit_c, inv_c, 9, 9)
        gradient(2, act_b, r, 8)
        into_t(r, 2, flip=True)
        activate_back(pre_b)
        gradient(1, low_b, r, 7)
        again_two.wait()
        into_t(r, 1, flip=True)
        norm_grad(stream, unit_b, inv_b, 5, 5)
        gradient(0, att, r, 4)
        again_one.wait()
        into_low(r, 0, d_att, flip=True)
        put_sum(3, jnp.dot(jnp.ones((16, total), b16), d_att[...], preferred_element_type=f32)[0:1, :])

        def leave(rows, c):
            stream_out[rows, :] = stream[rows, :]
            return c

        each(chunk, leave)

    whole = pl.BlockSpec(memory_space=pltpu.VMEM)
    low = pltpu.VMEM((total, width), b16)
    high = pltpu.VMEM((total, width), f32)
    narrow = pltpu.VMEM((total, 128), f32)
    return pl.pallas_call(
        kernel,
        name="latent_part",
        in_specs=[pl.BlockSpec(memory_space=pltpu.SMEM), whole, whole, whole, pl.BlockSpec(memory_space=pl.ANY)],
        out_specs=[whole] * 5,
        out_shape=[
            jax.ShapeDtypeStruct((total, width), b16),
            jax.ShapeDtypeStruct((total, width), b16),
            jax.ShapeDtypeStruct((total, width), f32),
            jax.ShapeDtypeStruct((out_rows, width), f32),
            jax.ShapeDtypeStruct((out_rows, width), f32),
        ],
        scratch_shapes=[
            pltpu.VMEM((7, width, width), b16),
            low, low, low, low, low, low, low, low, low, low,
            pltpu.VMEM((H, total, total), b16),
            high, high, high, high, high, narrow, narrow, narrow, high, high, low,
            pltpu.VMEM((total, head), b16),
            pltpu.VMEM((stacked, total), b16),
            pltpu.SemaphoreType.DMA((12,)),
        ],
        compiler_params=pltpu.CompilerParams(vmem_limit_bytes=62 * 1024 * 1024),
    )(numbers, attended, lat, vectors, planes)


def body(pixels, lengths, latents, w_square, w_input, vec_d, vec_c, cotangent):
    n = lax.axis_size("ctx")
    bits_all = n.bit_length() - 1
    rows = latents.shape[1]
    width = latents.shape[2]
    own_w = w_square.shape[1]
    channels = pixels.shape[1]
    slots = pixels.shape[2]
    total_rows = rows * n
    head_size = width // H
    scale = 1.0 / math.sqrt(width)
    scale_self = 1.0 / math.sqrt(head_size)
    core = lax.axis_index("seq")
    place = lax.axis_index("ctx")
    parity = place & 1
    pair = place >> 1
    wide = [4 << i for i in range(bits_all - 2)]

    def swap(x, bit):
        return lax.ppermute(x, "ctx", [(i, i ^ bit) for i in range(n)])

    def swap_core(x):
        return lax.ppermute(x, "seq", [(0, 1), (1, 0)])

    def ordered(mine, other, flag, axis):
        first = jnp.where(flag == 0, mine, other)
        second = jnp.where(flag == 0, other, mine)
        return jnp.concatenate([first, second], axis=axis)

    def quad(x, low, high, axis):
        one, two, three = swap(x, low), swap(x, high), swap(x, low | high)
        bit_low, bit_high = (place // low) & 1, (place // high) & 1
        near = ordered(x, one, bit_low, axis)
        far = ordered(two, three, bit_low, axis)
        return ordered(near, far, bit_high, axis)

    def both(x):
        return ordered(x, swap_core(x), core, 1)

    def gather_wide(x):
        rest = list(wide)
        x = x[None]
        while len(rest) > 1:
            x = quad(x[None], rest[0], rest[1], 0)
            x = x.reshape((-1,) + x.shape[2:])
            rest = rest[2:]
        for bit in rest:
            x = ordered(x[None], swap(x[None], bit), (place // bit) & 1, 0)
            x = x.reshape((-1,) + x.shape[2:])
        return x

    lanes = 384
    packed = jnp.concatenate(
        [
            w_square[0],
            jnp.pad(w_input[0], ((0, 0), (0, lanes - channels))),
            w_input[1],
            vec_d.T,
            jnp.zeros((own_w, lanes - channels - vec_d.shape[0]), b16),
        ],
        axis=1,
    )
    packed = gather_wide(packed[None])[:, 0]
    packed = quad(packed[:, None], 1, 2, 1)
    packed = both(packed.reshape(1, n * own_w, -1))[0]
    square_first = packed[:, :width]
    packed = lax.optimization_barrier(packed[:, width:])
    tall = (channels + 6 + 15) // 16 * 16
    v_key = packed[:, :tall]
    v_val = jnp.where(jnp.arange(tall) < channels, packed[:, lanes : lanes + tall], jnp.zeros((), b16))
    vecf = packed[:, lanes + channels : lanes + channels + vec_d.shape[0]].T.astype(f32)
    lat = ordered(pick(latents, parity), swap(pick(latents, 1 - parity), 1), parity, 0)
    lat = gather_wide(lat[None])
    lat = ordered(lat, swap(lat, 2), (place // 2) & 1, 1).reshape(total_rows, width)
    planes = lax.all_gather(jnp.concatenate([w_square[1:], cotangent], axis=0), ("seq", "ctx"), axis=1, tiled=True)

    latent = lat.astype(f32)
    norm_a, unit_a, inv_a = layer_norm(latent, vecf[0], vecf[1], 1)
    low_a = norm_a.astype(b16)
    query = (matmul("id,de->ie", low_a, square_first) + vecf[2]).astype(b16)
    gate = (matmul("dc,id->ci", v_key, query) * scale).astype(b16)
    gates = ordered(gate[None], swap(gate, 1)[None], parity, 0)

    gain_in = vec_c.astype(f32)
    norm_x, unit_x, inv_x = layer_norm(pixels.astype(f32), gain_in[0][:, None], gain_in[1][:, None], 1)
    low_x = jnp.pad(norm_x.astype(b16), ((0, 0), (0, tall - channels), (0, 0)))
    position = place * slots + jnp.arange(slots, dtype=jnp.int32)
    valid = (position[None, :] < lengths[:, None])[:, None, :]
    scores = matmul("qci,qcj->qij", gates, low_x)
    top = jnp.max(jnp.where(valid, scores, -1e30), axis=2)
    top_hi, top_lo = split_two(top)
    shift = top_hi.astype(f32) + top_lo.astype(f32)
    expo = jnp.where(valid, jnp.exp(scores - shift[..., None]), 0.0)
    total_hi, total_lo = split_two(jnp.sum(expo, axis=2))
    mixed = matmul("qij,qcj->qci", expo.astype(b16), low_x).astype(b16)
    row = jnp.arange(tall)[:, None]

    def write(v, parts):
        for k, part in enumerate(parts):
            v = jnp.where(row == channels + k, part[..., None, :], v)
        return v

    pay = write(mixed, [top_hi, top_lo, total_hi, total_lo])

    def opened(p):
        s = p[channels : channels + 4].astype(f32)
        return p.astype(f32), s[0] + s[1], s[2] + s[3]

    def merge(a, b):
        va, ta, la = opened(a)
        vb, tb, lb = opened(b)
        t = jnp.maximum(ta, tb)
        ea = jnp.exp(ta - t)
        eb = jnp.exp(tb - t)
        return va * ea + vb * eb, t, la * ea + lb * eb

    def closed(v, t, l):
        return write(v.astype(b16), split_two(t) + split_two(l))

    state = merge(pick(pay, parity), swap(pick(pay, 1 - parity), 1))
    for bit in [2] + wide:
        mine = closed(*state)
        state = merge(mine, swap(mine, bit))
    mix_sum, top_all, total_all = state
    mean_x = jnp.where(row < channels, mix_sum / total_all, 0.0)
    mean_low = mean_x.astype(b16)

    attended = (matmul("ci,dc->id", mean_low, v_val) + vecf[3]).astype(b16)
    part_rows = 2 * own_w
    aligned = max(part_rows, 128)
    base = pair * part_rows // aligned * aligned
    inner = pair * part_rows - base
    vectors = jnp.pad(vecf, ((0, 24 - vecf.shape[0]), (0, 0)))
    numbers = jnp.stack([parity, core, base, n * own_w + base, inner]).astype(jnp.int32)
    final, d_attended, d_after_cross, keep, send = latent_part(
        attended, lat, vectors, planes, numbers, part_rows, aligned, scale_self
    )

    def own_rows(array):
        mine = lax.dynamic_slice_in_dim(array, place * rows, rows, 0)
        theirs = lax.dynamic_slice_in_dim(array, (place ^ 1) * rows, rows, 0)
        return ordered(mine[None], swap(theirs, 1)[None], parity, 0)

    latents_out = own_rows(final)

    def share(a):
        return jnp.concatenate([lax.dynamic_slice_in_dim(a, s * n * own_w + base, aligned, 1) for s in range(2)], axis=1)

    def weight_grad(a, r):
        return matmul("ia,ie->ae", share(a), r)

    def window(part, which):
        return lax.dynamic_slice_in_dim(part, which * aligned + inner, part_rows, 0)

    def halves(x, which):
        return lax.dynamic_slice_in_dim(x, which * own_w, own_w, x.ndim - 2)

    def halved(x, which):
        top = halves(x[: 9 * part_rows].reshape(9, part_rows, width), which).reshape(9 * own_w, width)
        return jnp.concatenate([top, x[9 * part_rows :]], axis=0)

    def sums(x):
        return jnp.sum(x.astype(f32), axis=0, keepdims=True)

    pull = matmul("dc,id->ci", v_val, d_attended).astype(b16)
    delta = jnp.sum(pull.astype(f32) * mean_x, axis=0)
    pieces = split_two(top_all) + split_two(total_all) + split_two(delta)
    sent = write(pull, pieces)
    other = swap(sent, 1)
    core_sums = swap_core(after(send, sent))
    sents = ordered(sent[None], other[None], parity, 0)
    pulls = sents
    side = sents[:, channels : channels + 6].astype(f32)
    top_q = side[:, 0] + side[:, 1]
    total_q = side[:, 2] + side[:, 3]
    delta_q = side[:, 4] + side[:, 5]
    scores_again = matmul("qci,qcj->qij", gates, low_x)
    weight = jnp.where(valid, jnp.exp(scores_again - top_q[..., None]), 0.0) / total_q[..., None]
    d_weight = matmul("qci,qcj->qij", pulls, low_x)
    d_scores = (weight * (d_weight - delta_q[..., None])).astype(b16)
    weight_low = weight.astype(b16)
    force = matmul("qij,qcj->qci", d_scores, low_x).astype(b16)
    mine = pick(force, parity)
    other = swap(pick(force, 1 - parity), 1)
    held = after(d_scores, force)
    d_in_norm = (matmul("qci,qij->qcj", gates, held) + matmul("qci,qij->qcj", pulls, weight_low))[:, :channels]
    grad_pixels = norm_back(d_in_norm, unit_x, inv_x, gain_in[0][:, None], 1)
    grad_vc = [jnp.sum(d_in_norm * unit_x, axis=(0, 2)), jnp.sum(d_in_norm, axis=(0, 2))]
    grad_vc = jnp.pad(jnp.stack(grad_vc), ((0, 0), (0, total_rows - channels)))
    other = after(other, grad_vc)
    force_sum = mine.astype(f32) + other.astype(f32)
    chip_sums = None
    for bit in [2] + wide:
        mine = write(force_sum.astype(b16), split_two(grad_vc[0]) + split_two(grad_vc[1]))
        other = swap(mine, bit)
        if chip_sums is None:
            core_sums = after(keep, mine) + core_sums
            chip_sums = swap(halved(core_sums, 1 - parity), 1)
            part_att = matmul("ia,ci->ac", share(d_attended), mean_low)
            other = after(other, part_att)
        force_sum = mine.astype(f32) + other.astype(f32)
        grad_vc = jnp.stack([force_sum[channels] + force_sum[channels + 1], force_sum[channels + 2] + force_sum[channels + 3]])
    force_low = jnp.where(row < channels, force_sum * scale, 0.0).astype(b16)
    d_query = matmul("ci,dc->id", force_low, v_key).astype(b16)
    part0 = weight_grad(low_a, d_query)
    d_norm_a = matmul("ie,de->id", d_query, square_first)
    grad_lat = d_after_cross + norm_back(d_norm_a, unit_a, inv_a, vecf[0], 1)
    grad_latents = own_rows(grad_lat)

    part_q = matmul("ia,ci->ac", share(query), force_low)
    pad_lanes = lanes - tall
    wide_all = width + 2 * lanes

    def gradients(which):
        full = [window(part0, which)]
        for part in (part_q, part_att):
            full.append(jnp.pad(window(part, which), ((0, 0), (0, pad_lanes))))
        return jnp.concatenate(full, axis=1)

    late_vec = jnp.concatenate([sums(d_norm_a * unit_a), sums(d_norm_a), sums(d_query), jnp.pad(grad_vc, ((0, 0), (0, width - total_rows)))], axis=0)
    vectors = jnp.concatenate([late_vec, jnp.zeros((3, width), f32)], axis=0)
    tail = jnp.pad(vectors, ((0, 0), (0, wide_all - width)))
    own = jnp.concatenate([gradients(core), tail], axis=0)
    own = own + swap_core(jnp.concatenate([gradients(1 - core), tail], axis=0))

    def reduced(which):
        return jnp.concatenate([halves(own[:part_rows], which), own[part_rows:]], axis=0)

    own = reduced(parity) + swap(reduced(1 - parity), 1)
    late = own[None, :own_w, :width]
    chip_sums = halved(core_sums, parity) + chip_sums
    grad_input = jnp.stack([own[:own_w, width : width + channels], own[:own_w, width + lanes : width + lanes + channels]])
    tail = own[own_w:, :width]
    grad_vc = tail[3:5, :channels]
    vectors = jnp.concatenate([tail[:3], chip_sums[9 * own_w + 3 :]], axis=0)
    grad_vec = lax.dynamic_slice_in_dim(vectors, core * n * own_w + place * own_w, own_w, 1)[: vec_d.shape[0]]
    grad_square = jnp.concatenate([late, chip_sums[: 9 * own_w].reshape(9, own_w, width)], axis=0)
    return (latents_out, grad_latents, grad_pixels, grad_square, grad_input, grad_vec, grad_vc)


def solution(mesh):
    placed = (
        P("seq", None, "ctx"),
        P("seq"),
        P("seq", "ctx", None),
        P(None, ("seq", "ctx"), None),
        P(None, ("seq", "ctx"), None),
        P(None, ("seq", "ctx")),
        P(),
        P("seq", "ctx", None),
    )
    return jax.shard_map(
        body,
        mesh=mesh,
        in_specs=placed,
        out_specs=(
            P("seq", "ctx", None),
            P("seq", "ctx", None),
            P("seq", None, "ctx"),
            P(None, ("seq", "ctx"), None),
            P(None, ("seq", "ctx"), None),
            P(None, ("seq", "ctx")),
            P(),
        ),
        check_vma=False,
    )
```

```python
import math

import jax
import jax.numpy as jnp
from jax import lax
from jax.experimental import pallas as pl
from jax.experimental.pallas import tpu as pltpu
from jax.sharding import PartitionSpec as P

H = 8
epsilon = 1e-05
f32 = jnp.float32
b16 = jnp.bfloat16


def matmul(form, left, right):
    return jnp.einsum(form, left, right, preferred_element_type=f32)


def layer_norm(value, gain, shift, axis):
    center = value - jnp.mean(value, axis=axis, keepdims=True)
    spread = jnp.mean(center * center, axis=axis, keepdims=True)
    inverse = lax.rsqrt(spread + epsilon)
    unit = center * inverse
    return (unit * gain + shift, unit, inverse)


def norm_back(grad, unit, inverse, gain, axis):
    scaled = grad * gain
    inner = (
        scaled
        - jnp.mean(scaled, axis=axis, keepdims=True)
        - unit * jnp.mean(scaled * unit, axis=axis, keepdims=True)
    )
    return inner * inverse


def split_two(value):
    high = value.astype(b16)
    low = (value - high.astype(f32)).astype(b16)
    return high, low


def after(value, *needed):
    return lax.optimization_barrier((value,) + needed)[0]


def pick(array, index):
    return lax.dynamic_index_in_dim(array, index, 0, keepdims=False)


def latent_part(attended, lat, vectors, planes, cotangent, numbers, part_rows, aligned, scale_self):
    total, width = lat.shape
    head = width // H
    extra = vectors.shape[0]
    out_rows = 9 * part_rows + extra
    shares = 2 * aligned
    stacked = shares + 16
    chunk = 32
    block = 256
    part = 128
    cubic = 0.044715
    root = math.sqrt(2.0 / math.pi)

    def kernel(
        num, att, lat_ref, vec, planes_ref, cot_ref, final, d_att, stream_out, keep, send,
        w, cot, low_b, act_b, low_c, q, k, v, mix, low_e, act_e, weights,
        unit_b, unit_c, unit_e, pre_b, pre_e, inv_b, inv_c, inv_e, stream, t, r, small, lhs, sems,
    ):
        core, inner = num[0], num[3]

        def load(plane, slot, sem):
            return pltpu.make_async_copy(planes_ref.at[plane], w.at[slot], sems.at[sem])

        cot_copy = pltpu.make_async_copy(cot_ref, cot, sems.at[11])
        copies = [load(i, i, i) for i in range(7)]
        for copy in copies:
            copy.start()
        cot_copy.start()
        row_eight, row_nine = load(7, 0, 7), load(8, 1, 8)
        again_two, again_one = load(1, 1, 9), load(0, 0, 10)

        lhs[pl.ds(shares, 16), :] = jnp.ones((16, total), b16)

        def each(size, body, carry=None):
            def step(i, c):
                return body(pl.ds(pl.multiple_of(i * size, size), size), c)

            return lax.fori_loop(0, total // size, step, 0 if carry is None else carry)

        def product(a, slot, flip):
            dims = (((1,), (1 if flip else 0,)), ((), ()))
            return lax.dot_general(a, w[slot], dims, preferred_element_type=f32)

        def into_t(a_ref, slot, flip=False, add=False):
            def body(rows, c):
                o = product(a_ref[rows, :], slot, flip)
                t[rows, :] = t[rows, :] + o if add else o
                return c

            each(block, body)

        def into_low(a_ref, slot, out, flip=False, bias=None):
            def body(rows, c):
                o = product(a_ref[rows, :], slot, flip)
                if bias is not None:
                    o = o + vec[bias : bias + 1, :]
                out[rows, :] = o.astype(b16)
                return c

            each(block, body)

        def row_of(i):
            return vec[i : i + 1, :]

        def residual(before, bias, unit, inv, low, gain):
            def body(rows, c):
                x = before[rows, :].astype(f32) + t[rows, :] + row_of(bias)
                stream[rows, :] = x
                center = x - jnp.mean(x, axis=1, keepdims=True)
                inverse = lax.rsqrt(jnp.mean(center * center, axis=1, keepdims=True) + epsilon)
                u = center * inverse
                unit[rows, :] = u
                inv[rows, :] = jnp.broadcast_to(inverse, (chunk, 128))
                low[rows, :] = (u * row_of(gain) + row_of(gain + 1)).astype(b16)
                return c

            each(chunk, body)

        def activate(bias, pre, act):
            def body(rows, c):
                x = t[rows, :] + row_of(bias)
                pre[rows, :] = x
                act[rows, :] = (0.5 * x * (1.0 + jnp.tanh(root * (x + cubic * (x * x * x))))).astype(b16)
                return c

            each(chunk, body)

        def activate_back(pre):
            def body(rows, c):
                x = pre[rows, :]
                square = x * x
                h = jnp.tanh(root * (x + cubic * (square * x)))
                slope = 0.5 * (1.0 + h) + 0.5 * x * (1.0 - h * h) * (root * (1.0 + 3.0 * cubic * square))
                r[rows, :] = (t[rows, :] * slope).astype(b16)
                return c

            each(chunk, body)

        def norm_grad(before, unit, inv, gain, place):
            def body(rows, c):
                g, u = t[rows, :], unit[rows, :]
                scaled = g * row_of(gain)
                inner_grad = (
                    scaled
                    - jnp.mean(scaled, axis=1, keepdims=True)
                    - u * jnp.mean(scaled * u, axis=1, keepdims=True)
                )
                x = before[rows, :].astype(f32) + inner_grad * inv[rows, 0:1]
                stream[rows, :] = x
                r[rows, :] = x.astype(b16)
                first = c[0] + jnp.sum((g * u).reshape(chunk // 8, 8, width), axis=0)
                second = c[1] + jnp.sum(g.reshape(chunk // 8, 8, width), axis=0)
                return first, second

            zero = jnp.zeros((8, width), f32)
            first, second = each(chunk, body, (zero, zero))
            put_sum(place, jnp.sum(first, axis=0, keepdims=True))
            put_sum(place + 1, jnp.sum(second, axis=0, keepdims=True))

        def put_sum(place, value):
            keep[pl.ds(9 * part_rows + place, 1), :] = value
            send[pl.ds(9 * part_rows + place, 1), :] = value

        def gradient(index, a_ref, r_ref, place=None):
            for s in range(2):
                columns = a_ref[:, pl.ds(pl.multiple_of(num[1 + s], 128), aligned)]
                lhs[pl.ds(s * aligned, aligned), :] = columns.T
            t[pl.ds(0, stacked), :] = jnp.dot(lhs[...], r_ref[...], preferred_element_type=f32)
            near = pl.multiple_of(core * aligned + inner, 8)
            far = pl.multiple_of((1 - core) * aligned + inner, 8)
            keep[pl.ds(index * part_rows, part_rows), :] = t[pl.ds(near, part_rows), :]
            send[pl.ds(index * part_rows, part_rows), :] = t[pl.ds(far, part_rows), :]
            if place is not None:
                put_sum(place, t[pl.ds(shares, 1), :])

        for place in (keep, send):
            place[pl.ds(9 * part_rows, extra), :] = jnp.zeros((extra, width), f32)

        copies[0].wait()
        into_t(att, 0)
        row_eight.start()
        residual(lat_ref, 4, unit_b, inv_b, low_b, 5)
        copies[1].wait()
        into_t(low_b, 1)
        row_nine.start()
        activate(7, pre_b, act_b)
        copies[2].wait()
        into_t(act_b, 2)
        residual(stream, 8, unit_c, inv_c, low_c, 9)
        copies[3].wait()
        into_low(low_c, 3, q, bias=11)
        copies[4].wait()
        into_low(low_c, 4, k)
        copies[5].wait()
        into_low(low_c, 5, v, bias=12)
        for h in range(H):
            cols = slice(h * head, (h + 1) * head)

            def attend(rows, c):
                s = scale_self * lax.dot_general(
                    q[rows, cols], k[:, cols], (((1,), (1,)), ((), ())), preferred_element_type=f32
                )
                e = jnp.exp(s - jnp.max(s, axis=1, keepdims=True))
                low = (e / jnp.sum(e, axis=1, keepdims=True)).astype(b16)
                weights[h, rows, :] = low
                mix[rows, cols] = jnp.dot(low, v[:, cols], preferred_element_type=f32).astype(b16)
                return c

            each(part, attend)
        copies[6].wait()
        into_t(mix, 6)
        residual(stream, 13, unit_e, inv_e, low_e, 14)
        row_eight.wait()
        into_t(low_e, 0)
        activate(16, pre_e, act_e)
        row_nine.wait()
        into_t(act_e, 1)

        def finish(rows, c):
            final[rows, :] = (stream[rows, :] + t[rows, :] + row_of(17)).astype(b16)
            return c

        each(chunk, finish)

        cot_copy.wait()
        into_t(cot, 1, flip=True)
        again_two.start()
        activate_back(pre_e)
        gradient(8, act_e, cot, 17)
        gradient(7, low_e, r, 16)
        into_t(r, 0, flip=True)
        again_one.start()
        norm_grad(cot, unit_e, inv_e, 14, 14)
        gradient(6, mix, r, 13)
        into_low(r, 6, d_att, flip=True)
        for h in range(H):
            cols = slice(h * head, (h + 1) * head)
            turned = (((0,), (0,)), ((), ()))
            small[...] = lax.dot_general(weights[h], d_att[:, cols], turned, preferred_element_type=f32).astype(b16)

            def attend_back(rows, c):
                d_weight = lax.dot_general(
                    d_att[rows, cols], v[:, cols], (((1,), (1,)), ((), ())), preferred_element_type=f32
                )
                weight = weights[h, rows, :].astype(f32)
                d_scores = weight * (d_weight - jnp.sum(d_weight * weight, axis=1, keepdims=True))
                d_scores = d_scores.astype(b16)
                weights[h, rows, :] = d_scores
                d_query = jnp.dot(d_scores, k[:, cols], preferred_element_type=f32) * scale_self
                d_att[rows, cols] = d_query.astype(b16)
                return c

            each(part, attend_back)
            d_keys = lax.dot_general(weights[h], q[:, cols], turned, preferred_element_type=f32) * scale_self
            k[:, cols] = d_keys.astype(b16)
            v[:, cols] = small[...]
        gradient(5, low_c, v, 12)
        gradient(4, low_c, k)
        gradient(3, low_c, d_att, 11)
        into_t(d_att, 3, flip=True)
        into_t(k, 4, flip=True, add=True)
        into_t(v, 5, flip=True, add=True)
        norm_grad(stream, unit_c, inv_c, 9, 9)
        gradient(2, act_b, r, 8)
        into_t(r, 2, flip=True)
        activate_back(pre_b)
        gradient(1, low_b, r, 7)
        again_two.wait()
        into_t(r, 1, flip=True)
        norm_grad(stream, unit_b, inv_b, 5, 5)
        gradient(0, att, r, 4)
        again_one.wait()
        into_low(r, 0, d_att, flip=True)
        put_sum(3, jnp.dot(jnp.ones((16, total), b16), d_att[...], preferred_element_type=f32)[0:1, :])

        def leave(rows, c):
            stream_out[rows, :] = stream[rows, :]
            return c

        each(chunk, leave)

    whole = pl.BlockSpec(memory_space=pltpu.VMEM)
    low = pltpu.VMEM((total, width), b16)
    high = pltpu.VMEM((total, width), f32)
    narrow = pltpu.VMEM((total, 128), f32)
    return pl.pallas_call(
        kernel,
        name="latent_part",
        in_specs=[pl.BlockSpec(memory_space=pltpu.SMEM), whole, whole, whole] + [pl.BlockSpec(memory_space=pl.ANY)] * 2,
        out_specs=[whole] * 5,
        out_shape=[
            jax.ShapeDtypeStruct((total, width), b16),
            jax.ShapeDtypeStruct((total, width), b16),
            jax.ShapeDtypeStruct((total, width), f32),
            jax.ShapeDtypeStruct((out_rows, width), f32),
            jax.ShapeDtypeStruct((out_rows, width), f32),
        ],
        scratch_shapes=[
            pltpu.VMEM((7, width, width), b16),
            low, low, low, low, low, low, low, low, low, low,
            pltpu.VMEM((H, total, total), b16),
            high, high, high, high, high, narrow, narrow, narrow, high, high, low,
            pltpu.VMEM((total, head), b16),
            pltpu.VMEM((stacked, total), b16),
            pltpu.SemaphoreType.DMA((12,)),
        ],
        compiler_params=pltpu.CompilerParams(vmem_limit_bytes=62 * 1024 * 1024),
    )(numbers, attended, lat, vectors, planes, cotangent)


def body(pixels, lengths, latents, w_square, w_input, vec_d, vec_c, cotangent):
    n = lax.axis_size("ctx")
    bits_all = n.bit_length() - 1
    rows = latents.shape[1]
    width = latents.shape[2]
    own_w = w_square.shape[1]
    channels = pixels.shape[1]
    slots = pixels.shape[2]
    total_rows = rows * n
    head_size = width // H
    scale = 1.0 / math.sqrt(width)
    scale_self = 1.0 / math.sqrt(head_size)
    core = lax.axis_index("seq")
    place = lax.axis_index("ctx")
    parity = place & 1
    pair = place >> 1
    wide = [4 << i for i in range(bits_all - 2)]

    def swap(x, bit):
        return lax.ppermute(x, "ctx", [(i, i ^ bit) for i in range(n)])

    def swap_core(x):
        return lax.ppermute(x, "seq", [(0, 1), (1, 0)])

    def ordered(mine, other, flag, axis):
        first = jnp.where(flag == 0, mine, other)
        second = jnp.where(flag == 0, other, mine)
        return jnp.concatenate([first, second], axis=axis)

    def quad(x, low, high, axis):
        one, two, three = swap(x, low), swap(x, high), swap(x, low | high)
        bit_low, bit_high = (place // low) & 1, (place // high) & 1
        near = ordered(x, one, bit_low, axis)
        far = ordered(two, three, bit_low, axis)
        return ordered(near, far, bit_high, axis)

    def both(x):
        return ordered(x, swap_core(x), core, 1)

    def gather_wide(x):
        rest = list(wide)
        x = x[None]
        while len(rest) > 1:
            x = quad(x[None], rest[0], rest[1], 0)
            x = x.reshape((-1,) + x.shape[2:])
            rest = rest[2:]
        for bit in rest:
            x = ordered(x[None], swap(x[None], bit), (place // bit) & 1, 0)
            x = x.reshape((-1,) + x.shape[2:])
        return x

    def own_steps(array):
        other = yield swap(pick(array, 1 - parity), 1)
        x = ordered(pick(array, parity), other, parity, 0)[None]
        for bit in wide:
            other = yield swap(x, bit)
            x = ordered(x, other, (place // bit) & 1, 0)
        other = yield swap(x, 2)
        x = ordered(x[:, None], other[:, None], (place // 2) & 1, 1)
        return x.reshape(total_rows, width)

    lanes = 384
    packed = jnp.concatenate(
        [
            w_square[0],
            jnp.pad(w_input[0], ((0, 0), (0, lanes - channels))),
            w_input[1],
            vec_d.T,
            jnp.zeros((own_w, lanes - channels - vec_d.shape[0]), b16),
        ],
        axis=1,
    )
    packed = gather_wide(packed[None])[:, 0]
    packed = quad(packed[:, None], 1, 2, 1)
    packed = both(packed.reshape(1, n * own_w, -1))[0]
    square_first = packed[:, :width]
    packed = lax.optimization_barrier(packed[:, width:])
    tall = (channels + 6 + 15) // 16 * 16
    v_key = packed[:, :tall]
    v_val = jnp.where(jnp.arange(tall) < channels, packed[:, lanes : lanes + tall], jnp.zeros((), b16))
    vecf = packed[:, lanes + channels : lanes + channels + vec_d.shape[0]].T.astype(f32)
    lat = ordered(pick(latents, parity), swap(pick(latents, 1 - parity), 1), parity, 0)
    lat = gather_wide(lat[None])
    lat = ordered(lat, swap(lat, 2), (place // 2) & 1, 1).reshape(total_rows, width)
    planes = lax.all_gather(w_square[1:], ("seq", "ctx"), axis=1, tiled=True)

    latent = lat.astype(f32)
    norm_a, unit_a, inv_a = layer_norm(latent, vecf[0], vecf[1], 1)
    low_a = norm_a.astype(b16)
    query = (matmul("id,de->ie", low_a, square_first) + vecf[2]).astype(b16)
    gate = (matmul("dc,id->ci", v_key, query) * scale).astype(b16)
    steps = own_steps(after(cotangent, gate))
    hanging = [next(steps)]
    gathered = []

    def pace(value):
        if not hanging:
            return value
        value, other = lax.optimization_barrier((value, hanging.pop()))
        try:
            hanging.append(steps.send(other))
        except StopIteration as stop:
            gathered.append(stop.value)
        return value

    gates = ordered(gate[None], pace(swap(gate, 1))[None], parity, 0)

    gain_in = vec_c.astype(f32)
    norm_x, unit_x, inv_x = layer_norm(pixels.astype(f32), gain_in[0][:, None], gain_in[1][:, None], 1)
    low_x = jnp.pad(norm_x.astype(b16), ((0, 0), (0, tall - channels), (0, 0)))
    position = place * slots + jnp.arange(slots, dtype=jnp.int32)
    valid = (position[None, :] < lengths[:, None])[:, None, :]
    scores = matmul("qci,qcj->qij", gates, low_x)
    top = jnp.max(jnp.where(valid, scores, -1e30), axis=2)
    top_hi, top_lo = split_two(top)
    shift = top_hi.astype(f32) + top_lo.astype(f32)
    expo = jnp.where(valid, jnp.exp(scores - shift[..., None]), 0.0)
    total_hi, total_lo = split_two(jnp.sum(expo, axis=2))
    mixed = matmul("qij,qcj->qci", expo.astype(b16), low_x).astype(b16)
    row = jnp.arange(tall)[:, None]

    def write(v, parts):
        for k, part in enumerate(parts):
            v = jnp.where(row == channels + k, part[..., None, :], v)
        return v

    pay = write(mixed, [top_hi, top_lo, total_hi, total_lo])

    def opened(p):
        s = p[channels : channels + 4].astype(f32)
        return p.astype(f32), s[0] + s[1], s[2] + s[3]

    def merge(a, b):
        va, ta, la = opened(a)
        vb, tb, lb = opened(b)
        t = jnp.maximum(ta, tb)
        ea = jnp.exp(ta - t)
        eb = jnp.exp(tb - t)
        return va * ea + vb * eb, t, la * ea + lb * eb

    def closed(v, t, l):
        return write(v.astype(b16), split_two(t) + split_two(l))

    state = merge(pick(pay, parity), pace(swap(pick(pay, 1 - parity), 1)))
    for bit in [2] + wide:
        mine = closed(*state)
        state = merge(mine, pace(swap(mine, bit)))
    while hanging:
        pace(state[0])
    cot = gathered[0]
    mix_sum, top_all, total_all = state
    mean_x = jnp.where(row < channels, mix_sum / total_all, 0.0)
    mean_low = mean_x.astype(b16)

    attended = (matmul("ci,dc->id", mean_low, v_val) + vecf[3]).astype(b16)
    part_rows = 2 * own_w
    aligned = max(part_rows, 128)
    base = pair * part_rows // aligned * aligned
    inner = pair * part_rows - base
    vectors = jnp.pad(vecf, ((0, 24 - vecf.shape[0]), (0, 0)))
    numbers = jnp.stack([core, base, n * own_w + base, inner]).astype(jnp.int32)
    final, d_attended, d_after_cross, keep, send = latent_part(
        attended, lat, vectors, planes, cot, numbers, part_rows, aligned, scale_self
    )

    def own_rows(array):
        mine = lax.dynamic_slice_in_dim(array, place * rows, rows, 0)
        theirs = lax.dynamic_slice_in_dim(array, (place ^ 1) * rows, rows, 0)
        return ordered(mine[None], swap(theirs, 1)[None], parity, 0)

    latents_out = own_rows(final)

    def share(a):
        return jnp.concatenate([lax.dynamic_slice_in_dim(a, s * n * own_w + base, aligned, 1) for s in range(2)], axis=1)

    def weight_grad(a, r):
        return matmul("ia,ie->ae", share(a), r)

    def window(part, which):
        return lax.dynamic_slice_in_dim(part, which * aligned + inner, part_rows, 0)

    def halves(x, which):
        return lax.dynamic_slice_in_dim(x, which * own_w, own_w, x.ndim - 2)

    def halved(x, which):
        top = halves(x[: 9 * part_rows].reshape(9, part_rows, width), which).reshape(9 * own_w, width)
        return jnp.concatenate([top, x[9 * part_rows :]], axis=0)

    def sums(x):
        return jnp.sum(x.astype(f32), axis=0, keepdims=True)

    pull = matmul("dc,id->ci", v_val, d_attended).astype(b16)
    delta = jnp.sum(pull.astype(f32) * mean_x, axis=0)
    pieces = split_two(top_all) + split_two(total_all) + split_two(delta)
    sent = write(pull, pieces)
    other = swap(sent, 1)
    core_sums = swap_core(after(send, sent))
    sents = ordered(sent[None], other[None], parity, 0)
    pulls = sents
    side = sents[:, channels : channels + 6].astype(f32)
    top_q = side[:, 0] + side[:, 1]
    total_q = side[:, 2] + side[:, 3]
    delta_q = side[:, 4] + side[:, 5]
    scores_again = matmul("qci,qcj->qij", gates, low_x)
    weight = jnp.where(valid, jnp.exp(scores_again - top_q[..., None]), 0.0) / total_q[..., None]
    d_weight = matmul("qci,qcj->qij", pulls, low_x)
    d_scores = (weight * (d_weight - delta_q[..., None])).astype(b16)
    weight_low = weight.astype(b16)
    force = matmul("qij,qcj->qci", d_scores, low_x).astype(b16)
    mine = pick(force, parity)
    other = swap(pick(force, 1 - parity), 1)
    held = after(d_scores, force)
    d_in_norm = (matmul("qci,qij->qcj", gates, held) + matmul("qci,qij->qcj", pulls, weight_low))[:, :channels]
    grad_pixels = norm_back(d_in_norm, unit_x, inv_x, gain_in[0][:, None], 1)
    grad_vc = [jnp.sum(d_in_norm * unit_x, axis=(0, 2)), jnp.sum(d_in_norm, axis=(0, 2))]
    grad_vc = jnp.pad(jnp.stack(grad_vc), ((0, 0), (0, total_rows - channels)))
    other = after(other, grad_vc)
    force_sum = mine.astype(f32) + other.astype(f32)
    chip_sums = None
    for bit in [2] + wide:
        mine = write(force_sum.astype(b16), split_two(grad_vc[0]) + split_two(grad_vc[1]))
        other = swap(mine, bit)
        if chip_sums is None:
            core_sums = after(keep, mine) + core_sums
            other, core_sums = lax.optimization_barrier((other, core_sums))
            chip_sums = swap(halved(core_sums, 1 - parity).astype(b16), 1)
            part_att = matmul("ia,ci->ac", share(d_attended), mean_low)
            other = after(other, part_att)
        elif bit == wide[-1]:
            other, chip_sums = lax.optimization_barrier((other, chip_sums))
        force_sum = mine.astype(f32) + other.astype(f32)
        grad_vc = jnp.stack([force_sum[channels] + force_sum[channels + 1], force_sum[channels + 2] + force_sum[channels + 3]])
    force_low = jnp.where(row < channels, force_sum * scale, 0.0).astype(b16)
    d_query = matmul("ci,dc->id", force_low, v_key).astype(b16)
    part0 = weight_grad(low_a, d_query)
    d_norm_a = matmul("ie,de->id", d_query, square_first)
    grad_lat = d_after_cross + norm_back(d_norm_a, unit_a, inv_a, vecf[0], 1)
    grad_latents = own_rows(grad_lat)

    part_q = matmul("ia,ci->ac", share(query), force_low)
    pad_lanes = lanes - tall
    wide_all = width + 2 * lanes

    def gradients(which):
        full = [window(part0, which)]
        for part in (part_q, part_att):
            full.append(jnp.pad(window(part, which), ((0, 0), (0, pad_lanes))))
        return jnp.concatenate(full, axis=1)

    late_vec = jnp.concatenate([sums(d_norm_a * unit_a), sums(d_norm_a), sums(d_query), jnp.pad(grad_vc, ((0, 0), (0, width - total_rows)))], axis=0)
    vectors = jnp.concatenate([late_vec, jnp.zeros((3, width), f32)], axis=0)
    tail = jnp.pad(vectors, ((0, 0), (0, wide_all - width)))
    own = jnp.concatenate([gradients(core), tail], axis=0)
    own = own + swap_core(jnp.concatenate([gradients(1 - core), tail], axis=0))

    def reduced(which):
        return jnp.concatenate([halves(own[:part_rows], which), own[part_rows:]], axis=0)

    own = reduced(parity) + swap(reduced(1 - parity), 1)
    late = own[None, :own_w, :width]
    chip_sums = halved(core_sums, parity) + chip_sums.astype(f32)
    grad_input = jnp.stack([own[:own_w, width : width + channels], own[:own_w, width + lanes : width + lanes + channels]])
    tail = own[own_w:, :width]
    grad_vc = tail[3:5, :channels]
    vectors = jnp.concatenate([tail[:3], chip_sums[9 * own_w + 3 :]], axis=0)
    grad_vec = lax.dynamic_slice_in_dim(vectors, core * n * own_w + place * own_w, own_w, 1)[: vec_d.shape[0]]
    grad_square = jnp.concatenate([late, chip_sums[: 9 * own_w].reshape(9, own_w, width)], axis=0)
    return (latents_out, grad_latents, grad_pixels, grad_square, grad_input, grad_vec, grad_vc)


def solution(mesh):
    placed = (
        P("seq", None, "ctx"),
        P("seq"),
        P("seq", "ctx", None),
        P(None, ("seq", "ctx"), None),
        P(None, ("seq", "ctx"), None),
        P(None, ("seq", "ctx")),
        P(),
        P("seq", "ctx", None),
    )
    return jax.shard_map(
        body,
        mesh=mesh,
        in_specs=placed,
        out_specs=(
            P("seq", "ctx", None),
            P("seq", "ctx", None),
            P("seq", None, "ctx"),
            P(None, ("seq", "ctx"), None),
            P(None, ("seq", "ctx"), None),
            P(None, ("seq", "ctx")),
            P(),
        ),
        check_vma=False,
    )
```

```python
import math

import jax
import jax.numpy as jnp
from jax import lax
from jax.experimental import pallas as pl
from jax.experimental.pallas import tpu as pltpu
from jax.sharding import PartitionSpec as P

H = 8
epsilon = 1e-05
f32 = jnp.float32
b16 = jnp.bfloat16


def matmul(form, left, right):
    return jnp.einsum(form, left, right, preferred_element_type=f32)


def layer_norm(value, gain, shift, axis):
    center = value - jnp.mean(value, axis=axis, keepdims=True)
    spread = jnp.mean(center * center, axis=axis, keepdims=True)
    inverse = lax.rsqrt(spread + epsilon)
    unit = center * inverse
    return (unit * gain + shift, unit, inverse)


def norm_back(grad, unit, inverse, gain, axis):
    scaled = grad * gain
    inner = (
        scaled
        - jnp.mean(scaled, axis=axis, keepdims=True)
        - unit * jnp.mean(scaled * unit, axis=axis, keepdims=True)
    )
    return inner * inverse


def split_two(value):
    high = value.astype(b16)
    low = (value - high.astype(f32)).astype(b16)
    return high, low


def after(value, *needed):
    return lax.optimization_barrier((value,) + needed)[0]


def pick(array, index):
    return lax.dynamic_index_in_dim(array, index, 0, keepdims=False)


def latent_part(attended, lat, vectors, planes, cotangent, numbers, part_rows, aligned, scale_self):
    total, width = lat.shape
    head = width // H
    extra = vectors.shape[0]
    out_rows = 9 * part_rows + extra
    shares = 2 * aligned
    stacked = shares + 16
    chunk = 128
    block = 512
    part = 512
    cubic = 0.044715
    root = math.sqrt(2.0 / math.pi)

    def kernel(
        num, att, lat_ref, vec, planes_ref, cot_ref, final, d_att, stream_out, keep, send,
        w, cot, low_b, act_b, low_c, q, k, v, mix, low_e, act_e, weights,
        unit_b, unit_c, unit_e, pre_b, pre_e, inv_b, inv_c, inv_e, stream, t, r, small, lhs, sems,
    ):
        core, inner = num[0], num[3]

        def load(plane, slot, sem):
            return pltpu.make_async_copy(planes_ref.at[plane], w.at[slot], sems.at[sem])

        cot_copy = pltpu.make_async_copy(cot_ref, cot, sems.at[11])
        copies = [load(i, i, i) for i in range(7)]
        for copy in copies:
            copy.start()
        cot_copy.start()
        row_eight, row_nine = load(7, 0, 7), load(8, 1, 8)
        again_two, again_one = load(1, 1, 9), load(0, 0, 10)

        lhs[pl.ds(shares, 16), :] = jnp.ones((16, total), b16)

        def each(size, body, carry=None):
            def step(i, c):
                return body(pl.ds(pl.multiple_of(i * size, size), size), c)

            return lax.fori_loop(0, total // size, step, 0 if carry is None else carry)

        def product(a, slot, flip):
            dims = (((1,), (1 if flip else 0,)), ((), ()))
            return lax.dot_general(a, w[slot], dims, preferred_element_type=f32)

        def into_t(a_ref, slot, flip=False, add=False):
            def body(rows, c):
                o = product(a_ref[rows, :], slot, flip)
                t[rows, :] = t[rows, :] + o if add else o
                return c

            each(block, body)

        def into_low(a_ref, slot, out, flip=False, bias=None):
            def body(rows, c):
                o = product(a_ref[rows, :], slot, flip)
                if bias is not None:
                    o = o + vec[bias : bias + 1, :]
                out[rows, :] = o.astype(b16)
                return c

            each(block, body)

        def row_of(i):
            return vec[i : i + 1, :]

        def residual(before, bias, unit, inv, low, gain):
            def body(rows, c):
                x = before[rows, :].astype(f32) + t[rows, :] + row_of(bias)
                stream[rows, :] = x
                center = x - jnp.mean(x, axis=1, keepdims=True)
                inverse = lax.rsqrt(jnp.mean(center * center, axis=1, keepdims=True) + epsilon)
                u = center * inverse
                unit[rows, :] = u
                inv[rows, :] = jnp.broadcast_to(inverse, (chunk, 128))
                low[rows, :] = (u * row_of(gain) + row_of(gain + 1)).astype(b16)
                return c

            each(chunk, body)

        def activate(bias, pre, act):
            def body(rows, c):
                x = t[rows, :] + row_of(bias)
                pre[rows, :] = x
                act[rows, :] = (0.5 * x * (1.0 + jnp.tanh(root * (x + cubic * (x * x * x))))).astype(b16)
                return c

            each(chunk, body)

        def activate_back(pre):
            def body(rows, c):
                x = pre[rows, :]
                square = x * x
                h = jnp.tanh(root * (x + cubic * (square * x)))
                slope = 0.5 * (1.0 + h) + 0.5 * x * (1.0 - h * h) * (root * (1.0 + 3.0 * cubic * square))
                r[rows, :] = (t[rows, :] * slope).astype(b16)
                return c

            each(chunk, body)

        def norm_grad(before, unit, inv, gain, place):
            def body(rows, c):
                g, u = t[rows, :], unit[rows, :]
                scaled = g * row_of(gain)
                inner_grad = (
                    scaled
                    - jnp.mean(scaled, axis=1, keepdims=True)
                    - u * jnp.mean(scaled * u, axis=1, keepdims=True)
                )
                x = before[rows, :].astype(f32) + inner_grad * inv[rows, 0:1]
                stream[rows, :] = x
                r[rows, :] = x.astype(b16)
                first = c[0] + jnp.sum((g * u).reshape(chunk // 8, 8, width), axis=0)
                second = c[1] + jnp.sum(g.reshape(chunk // 8, 8, width), axis=0)
                return first, second

            zero = jnp.zeros((8, width), f32)
            first, second = each(chunk, body, (zero, zero))
            put_sum(place, jnp.sum(first, axis=0, keepdims=True))
            put_sum(place + 1, jnp.sum(second, axis=0, keepdims=True))

        def put_sum(place, value):
            keep[pl.ds(9 * part_rows + place, 1), :] = value
            send[pl.ds(9 * part_rows + place, 1), :] = value

        def gradient(index, a_ref, r_ref, place=None):
            for s in range(2):
                columns = a_ref[:, pl.ds(pl.multiple_of(num[1 + s], 128), aligned)]
                lhs[pl.ds(s * aligned, aligned), :] = columns.T
            t[pl.ds(0, stacked), :] = jnp.dot(lhs[...], r_ref[...], preferred_element_type=f32)
            near = pl.multiple_of(core * aligned + inner, 8)
            far = pl.multiple_of((1 - core) * aligned + inner, 8)
            keep[pl.ds(index * part_rows, part_rows), :] = t[pl.ds(near, part_rows), :]
            send[pl.ds(index * part_rows, part_rows), :] = t[pl.ds(far, part_rows), :]
            if place is not None:
                put_sum(place, t[pl.ds(shares, 1), :])

        for place in (keep, send):
            place[pl.ds(9 * part_rows, extra), :] = jnp.zeros((extra, width), f32)

        copies[0].wait()
        into_t(att, 0)
        row_eight.start()
        residual(lat_ref, 4, unit_b, inv_b, low_b, 5)
        copies[1].wait()
        into_t(low_b, 1)
        row_nine.start()
        activate(7, pre_b, act_b)
        copies[2].wait()
        into_t(act_b, 2)
        residual(stream, 8, unit_c, inv_c, low_c, 9)
        copies[3].wait()
        into_low(low_c, 3, q, bias=11)
        copies[4].wait()
        into_low(low_c, 4, k)
        copies[5].wait()
        into_low(low_c, 5, v, bias=12)
        for h in range(H):
            cols = slice(h * head, (h + 1) * head)

            def attend(rows, c):
                s = scale_self * lax.dot_general(
                    q[rows, cols], k[:, cols], (((1,), (1,)), ((), ())), preferred_element_type=f32
                )
                e = jnp.exp(s - jnp.max(s, axis=1, keepdims=True))
                low = (e / jnp.sum(e, axis=1, keepdims=True)).astype(b16)
                weights[h, rows, :] = low
                mix[rows, cols] = jnp.dot(low, v[:, cols], preferred_element_type=f32).astype(b16)
                return c

            each(part, attend)
        copies[6].wait()
        into_t(mix, 6)
        residual(stream, 13, unit_e, inv_e, low_e, 14)
        row_eight.wait()
        into_t(low_e, 0)
        activate(16, pre_e, act_e)
        row_nine.wait()
        into_t(act_e, 1)

        def finish(rows, c):
            final[rows, :] = (stream[rows, :] + t[rows, :] + row_of(17)).astype(b16)
            return c

        each(chunk, finish)

        cot_copy.wait()
        into_t(cot, 1, flip=True)
        again_two.start()
        activate_back(pre_e)
        gradient(8, act_e, cot, 17)
        gradient(7, low_e, r, 16)
        into_t(r, 0, flip=True)
        again_one.start()
        norm_grad(cot, unit_e, inv_e, 14, 14)
        gradient(6, mix, r, 13)
        into_low(r, 6, d_att, flip=True)
        for h in range(H):
            cols = slice(h * head, (h + 1) * head)
            turned = (((0,), (0,)), ((), ()))
            small[...] = lax.dot_general(weights[h], d_att[:, cols], turned, preferred_element_type=f32).astype(b16)

            def attend_back(rows, c):
                d_weight = lax.dot_general(
                    d_att[rows, cols], v[:, cols], (((1,), (1,)), ((), ())), preferred_element_type=f32
                )
                weight = weights[h, rows, :].astype(f32)
                d_scores = weight * (d_weight - jnp.sum(d_weight * weight, axis=1, keepdims=True))
                d_scores = d_scores.astype(b16)
                weights[h, rows, :] = d_scores
                d_query = jnp.dot(d_scores, k[:, cols], preferred_element_type=f32) * scale_self
                d_att[rows, cols] = d_query.astype(b16)
                return c

            each(part, attend_back)
            d_keys = lax.dot_general(weights[h], q[:, cols], turned, preferred_element_type=f32) * scale_self
            k[:, cols] = d_keys.astype(b16)
            v[:, cols] = small[...]
        gradient(5, low_c, v, 12)
        gradient(4, low_c, k)
        gradient(3, low_c, d_att, 11)
        into_t(d_att, 3, flip=True)
        into_t(k, 4, flip=True, add=True)
        into_t(v, 5, flip=True, add=True)
        norm_grad(stream, unit_c, inv_c, 9, 9)
        gradient(2, act_b, r, 8)
        into_t(r, 2, flip=True)
        activate_back(pre_b)
        gradient(1, low_b, r, 7)
        again_two.wait()
        into_t(r, 1, flip=True)
        norm_grad(stream, unit_b, inv_b, 5, 5)
        gradient(0, att, r, 4)
        again_one.wait()
        into_low(r, 0, d_att, flip=True)
        put_sum(3, jnp.dot(jnp.ones((16, total), b16), d_att[...], preferred_element_type=f32)[0:1, :])

        def leave(rows, c):
            stream_out[rows, :] = stream[rows, :]
            return c

        each(chunk, leave)

    whole = pl.BlockSpec(memory_space=pltpu.VMEM)
    low = pltpu.VMEM((total, width), b16)
    high = pltpu.VMEM((total, width), f32)
    narrow = pltpu.VMEM((total, 128), f32)
    return pl.pallas_call(
        kernel,
        name="latent_part",
        in_specs=[pl.BlockSpec(memory_space=pltpu.SMEM), whole, whole, whole] + [pl.BlockSpec(memory_space=pl.ANY)] * 2,
        out_specs=[whole] * 5,
        out_shape=[
            jax.ShapeDtypeStruct((total, width), b16),
            jax.ShapeDtypeStruct((total, width), b16),
            jax.ShapeDtypeStruct((total, width), f32),
            jax.ShapeDtypeStruct((out_rows, width), f32),
            jax.ShapeDtypeStruct((out_rows, width), f32),
        ],
        scratch_shapes=[
            pltpu.VMEM((7, width, width), b16),
            low, low, low, low, low, low, low, low, low, low,
            pltpu.VMEM((H, total, total), b16),
            high, high, high, high, high, narrow, narrow, narrow, high, high, low,
            pltpu.VMEM((total, head), b16),
            pltpu.VMEM((stacked, total), b16),
            pltpu.SemaphoreType.DMA((12,)),
        ],
        compiler_params=pltpu.CompilerParams(vmem_limit_bytes=62 * 1024 * 1024),
    )(numbers, attended, lat, vectors, planes, cotangent)


def body(pixels, lengths, latents, w_square, w_input, vec_d, vec_c, cotangent):
    n = lax.axis_size("ctx")
    bits_all = n.bit_length() - 1
    rows = latents.shape[1]
    width = latents.shape[2]
    own_w = w_square.shape[1]
    channels = pixels.shape[1]
    slots = pixels.shape[2]
    total_rows = rows * n
    head_size = width // H
    scale = 1.0 / math.sqrt(width)
    scale_self = 1.0 / math.sqrt(head_size)
    core = lax.axis_index("seq")
    place = lax.axis_index("ctx")
    parity = place & 1
    pair = place >> 1
    wide = [4 << i for i in range(bits_all - 2)]

    def swap(x, bit):
        return lax.ppermute(x, "ctx", [(i, i ^ bit) for i in range(n)])

    def swap_core(x):
        return lax.ppermute(x, "seq", [(0, 1), (1, 0)])

    def ordered(mine, other, flag, axis):
        first = jnp.where(flag == 0, mine, other)
        second = jnp.where(flag == 0, other, mine)
        return jnp.concatenate([first, second], axis=axis)

    def quad(x, low, high, axis):
        one, two, three = swap(x, low), swap(x, high), swap(x, low | high)
        bit_low, bit_high = (place // low) & 1, (place // high) & 1
        near = ordered(x, one, bit_low, axis)
        far = ordered(two, three, bit_low, axis)
        return ordered(near, far, bit_high, axis)

    def both(x):
        return ordered(x, swap_core(x), core, 1)

    def gather_wide(x):
        rest = list(wide)
        x = x[None]
        while len(rest) > 1:
            x = quad(x[None], rest[0], rest[1], 0)
            x = x.reshape((-1,) + x.shape[2:])
            rest = rest[2:]
        for bit in rest:
            x = ordered(x[None], swap(x[None], bit), (place // bit) & 1, 0)
            x = x.reshape((-1,) + x.shape[2:])
        return x

    def own_steps(array):
        other = yield swap(pick(array, 1 - parity), 1)
        x = ordered(pick(array, parity), other, parity, 0)[None]
        for bit in wide:
            other = yield swap(x, bit)
            x = ordered(x, other, (place // bit) & 1, 0)
        other = yield swap(x, 2)
        x = ordered(x[:, None], other[:, None], (place // 2) & 1, 1)
        return x.reshape(total_rows, width)

    lanes = 384
    packed = jnp.concatenate(
        [
            w_square[0],
            jnp.pad(w_input[0], ((0, 0), (0, lanes - channels))),
            w_input[1],
            vec_d.T,
            jnp.zeros((own_w, lanes - channels - vec_d.shape[0]), b16),
        ],
        axis=1,
    )
    packed = gather_wide(packed[None])[:, 0]
    packed = quad(packed[:, None], 1, 2, 1)
    packed = both(packed.reshape(1, n * own_w, -1))[0]
    square_first = packed[:, :width]
    packed = lax.optimization_barrier(packed[:, width:])
    tall = (channels + 6 + 15) // 16 * 16
    v_key = packed[:, :tall]
    v_val = jnp.where(jnp.arange(tall) < channels, packed[:, lanes : lanes + tall], jnp.zeros((), b16))
    vecf = packed[:, lanes + channels : lanes + channels + vec_d.shape[0]].T.astype(f32)
    lat = ordered(pick(latents, parity), swap(pick(latents, 1 - parity), 1), parity, 0)
    lat = gather_wide(lat[None])
    lat = ordered(lat, swap(lat, 2), (place // 2) & 1, 1).reshape(total_rows, width)
    planes = lax.all_gather(w_square[1:], ("seq", "ctx"), axis=1, tiled=True)

    latent = lat.astype(f32)
    norm_a, unit_a, inv_a = layer_norm(latent, vecf[0], vecf[1], 1)
    low_a = norm_a.astype(b16)
    query = (matmul("id,de->ie", low_a, square_first) + vecf[2]).astype(b16)
    gate = (matmul("dc,id->ci", v_key, query) * scale).astype(b16)
    steps = own_steps(after(cotangent, gate))
    hanging = [next(steps)]
    gathered = []

    def pace(value):
        if not hanging:
            return value
        value, other = lax.optimization_barrier((value, hanging.pop()))
        try:
            hanging.append(steps.send(other))
        except StopIteration as stop:
            gathered.append(stop.value)
        return value

    gates = ordered(gate[None], pace(swap(gate, 1))[None], parity, 0)

    gain_in = vec_c.astype(f32)
    norm_x, unit_x, inv_x = layer_norm(pixels.astype(f32), gain_in[0][:, None], gain_in[1][:, None], 1)
    low_x = jnp.pad(norm_x.astype(b16), ((0, 0), (0, tall - channels), (0, 0)))
    position = place * slots + jnp.arange(slots, dtype=jnp.int32)
    valid = (position[None, :] < lengths[:, None])[:, None, :]
    scores = matmul("qci,qcj->qij", gates, low_x)
    top = jnp.max(jnp.where(valid, scores, -1e30), axis=2)
    top_hi, top_lo = split_two(top)
    shift = top_hi.astype(f32) + top_lo.astype(f32)
    expo = jnp.where(valid, jnp.exp(scores - shift[..., None]), 0.0)
    total_hi, total_lo = split_two(jnp.sum(expo, axis=2))
    mixed = matmul("qij,qcj->qci", expo.astype(b16), low_x).astype(b16)
    row = jnp.arange(tall)[:, None]

    def write(v, parts):
        for k, part in enumerate(parts):
            v = jnp.where(row == channels + k, part[..., None, :], v)
        return v

    pay = write(mixed, [top_hi, top_lo, total_hi, total_lo])

    def opened(p):
        s = p[channels : channels + 4].astype(f32)
        return p.astype(f32), s[0] + s[1], s[2] + s[3]

    def merge(a, b):
        va, ta, la = opened(a)
        vb, tb, lb = opened(b)
        t = jnp.maximum(ta, tb)
        ea = jnp.exp(ta - t)
        eb = jnp.exp(tb - t)
        return va * ea + vb * eb, t, la * ea + lb * eb

    def closed(v, t, l):
        return write(v.astype(b16), split_two(t) + split_two(l))

    state = merge(pick(pay, parity), pace(swap(pick(pay, 1 - parity), 1)))
    for bit in [2] + wide:
        mine = closed(*state)
        state = merge(mine, pace(swap(mine, bit)))
    while hanging:
        pace(state[0])
    cot = gathered[0]
    mix_sum, top_all, total_all = state
    mean_x = jnp.where(row < channels, mix_sum / total_all, 0.0)
    mean_low = mean_x.astype(b16)

    attended = (matmul("ci,dc->id", mean_low, v_val) + vecf[3]).astype(b16)
    part_rows = 2 * own_w
    aligned = max(part_rows, 128)
    base = pair * part_rows // aligned * aligned
    inner = pair * part_rows - base
    vectors = jnp.pad(vecf, ((0, 24 - vecf.shape[0]), (0, 0)))
    numbers = jnp.stack([core, base, n * own_w + base, inner]).astype(jnp.int32)
    final, d_attended, d_after_cross, keep, send = latent_part(
        attended, lat, vectors, planes, cot, numbers, part_rows, aligned, scale_self
    )

    def own_rows(array):
        mine = lax.dynamic_slice_in_dim(array, place * rows, rows, 0)
        theirs = lax.dynamic_slice_in_dim(array, (place ^ 1) * rows, rows, 0)
        return ordered(mine[None], swap(theirs, 1)[None], parity, 0)

    def share(a):
        return jnp.concatenate([lax.dynamic_slice_in_dim(a, s * n * own_w + base, aligned, 1) for s in range(2)], axis=1)

    def weight_grad(a, r):
        return matmul("ia,ie->ae", share(a), r)

    def window(part, which):
        return lax.dynamic_slice_in_dim(part, which * aligned + inner, part_rows, 0)

    def halves(x, which):
        return lax.dynamic_slice_in_dim(x, which * own_w, own_w, x.ndim - 2)

    def halved(x, which):
        top = halves(x[: 9 * part_rows].reshape(9, part_rows, width), which).reshape(9 * own_w, width)
        return jnp.concatenate([top, x[9 * part_rows :]], axis=0)

    def sums(x):
        return jnp.sum(x.astype(f32), axis=0, keepdims=True)

    pull = matmul("dc,id->ci", v_val, d_attended).astype(b16)
    delta = jnp.sum(pull.astype(f32) * mean_x, axis=0)
    pieces = split_two(top_all) + split_two(total_all) + split_two(delta)
    sent = write(pull, pieces)
    other = swap(sent, 1)
    core_sums = swap_core(after(send, sent))
    sents = ordered(sent[None], other[None], parity, 0)
    pulls = sents
    side = sents[:, channels : channels + 6].astype(f32)
    top_q = side[:, 0] + side[:, 1]
    total_q = side[:, 2] + side[:, 3]
    delta_q = side[:, 4] + side[:, 5]
    scores_again = matmul("qci,qcj->qij", gates, low_x)
    weight = jnp.where(valid, jnp.exp(scores_again - top_q[..., None]), 0.0) / total_q[..., None]
    d_weight = matmul("qci,qcj->qij", pulls, low_x)
    d_scores = (weight * (d_weight - delta_q[..., None])).astype(b16)
    weight_low = weight.astype(b16)
    force = matmul("qij,qcj->qci", d_scores, low_x).astype(b16)
    mine = pick(force, parity)
    other = swap(pick(force, 1 - parity), 1)
    held = after(d_scores, force)
    d_in_norm = (matmul("qci,qij->qcj", gates, held) + matmul("qci,qij->qcj", pulls, weight_low))[:, :channels]
    grad_pixels = norm_back(d_in_norm, unit_x, inv_x, gain_in[0][:, None], 1)
    grad_vc = [jnp.sum(d_in_norm * unit_x, axis=(0, 2)), jnp.sum(d_in_norm, axis=(0, 2))]
    grad_vc = jnp.pad(jnp.stack(grad_vc), ((0, 0), (0, total_rows - channels)))
    other = after(other, grad_vc)
    force_sum = mine.astype(f32) + other.astype(f32)
    chip_sums = None
    for bit in [2] + wide:
        mine = write(force_sum.astype(b16), split_two(grad_vc[0]) + split_two(grad_vc[1]))
        other = swap(mine, bit)
        if chip_sums is None:
            core_sums = after(keep, mine) + core_sums
            other, core_sums = lax.optimization_barrier((other, core_sums))
            latents_out = own_rows(after(final, mine))
            chip_sums = swap(halved(core_sums, 1 - parity).astype(b16), 1)
            part_att = matmul("ia,ci->ac", share(d_attended), mean_low)
            other = after(other, part_att)
        elif bit == wide[-1]:
            other, chip_sums = lax.optimization_barrier((other, chip_sums))
        force_sum = mine.astype(f32) + other.astype(f32)
        grad_vc = jnp.stack([force_sum[channels] + force_sum[channels + 1], force_sum[channels + 2] + force_sum[channels + 3]])
    force_low = jnp.where(row < channels, force_sum * scale, 0.0).astype(b16)
    d_query = matmul("ci,dc->id", force_low, v_key).astype(b16)
    part0 = weight_grad(low_a, d_query)
    d_norm_a = matmul("ie,de->id", d_query, square_first)
    grad_lat = d_after_cross + norm_back(d_norm_a, unit_a, inv_a, vecf[0], 1)
    grad_latents = own_rows(grad_lat)

    part_q = matmul("ia,ci->ac", share(query), force_low)
    pad_lanes = lanes - tall
    wide_all = width + 2 * lanes

    def gradients(which):
        full = [window(part0, which)]
        for part in (part_q, part_att):
            full.append(jnp.pad(window(part, which), ((0, 0), (0, pad_lanes))))
        return jnp.concatenate(full, axis=1)

    late_vec = jnp.concatenate([sums(d_norm_a * unit_a), sums(d_norm_a), sums(d_query), jnp.pad(grad_vc, ((0, 0), (0, width - total_rows)))], axis=0)
    vectors = jnp.concatenate([late_vec, jnp.zeros((3, width), f32)], axis=0)
    tail = jnp.pad(vectors, ((0, 0), (0, wide_all - width)))
    own = jnp.concatenate([gradients(core), tail], axis=0)
    own = own + swap_core(jnp.concatenate([gradients(1 - core), tail], axis=0))

    def reduced(which):
        return jnp.concatenate([halves(own[:part_rows], which), own[part_rows:]], axis=0)

    own = reduced(parity) + swap(reduced(1 - parity), 1)
    late = own[None, :own_w, :width]
    chip_sums = halved(core_sums, parity) + chip_sums.astype(f32)
    grad_input = jnp.stack([own[:own_w, width : width + channels], own[:own_w, width + lanes : width + lanes + channels]])
    tail = own[own_w:, :width]
    grad_vc = tail[3:5, :channels]
    vectors = jnp.concatenate([tail[:3], chip_sums[9 * own_w + 3 :]], axis=0)
    grad_vec = lax.dynamic_slice_in_dim(vectors, core * n * own_w + place * own_w, own_w, 1)[: vec_d.shape[0]]
    grad_square = jnp.concatenate([late, chip_sums[: 9 * own_w].reshape(9, own_w, width)], axis=0)
    return (latents_out, grad_latents, grad_pixels, grad_square, grad_input, grad_vec, grad_vc)


def solution(mesh):
    placed = (
        P("seq", None, "ctx"),
        P("seq"),
        P("seq", "ctx", None),
        P(None, ("seq", "ctx"), None),
        P(None, ("seq", "ctx"), None),
        P(None, ("seq", "ctx")),
        P(),
        P("seq", "ctx", None),
    )
    return jax.shard_map(
        body,
        mesh=mesh,
        in_specs=placed,
        out_specs=(
            P("seq", "ctx", None),
            P("seq", "ctx", None),
            P("seq", None, "ctx"),
            P(None, ("seq", "ctx"), None),
            P(None, ("seq", "ctx"), None),
            P(None, ("seq", "ctx")),
            P(),
        ),
        check_vma=False,
    )
```

```python
import math

import jax
import jax.numpy as jnp
from jax import lax
from jax.experimental import pallas as pl
from jax.experimental.pallas import tpu as pltpu
from jax.sharding import PartitionSpec as P

H = 8
epsilon = 1e-05
f32 = jnp.float32
b16 = jnp.bfloat16


def matmul(form, left, right):
    return jnp.einsum(form, left, right, preferred_element_type=f32)


def layer_norm(value, gain, shift, axis):
    center = value - jnp.mean(value, axis=axis, keepdims=True)
    spread = jnp.mean(center * center, axis=axis, keepdims=True)
    inverse = lax.rsqrt(spread + epsilon)
    unit = center * inverse
    return (unit * gain + shift, unit, inverse)


def norm_back(grad, unit, inverse, gain, axis):
    scaled = grad * gain
    inner = (
        scaled
        - jnp.mean(scaled, axis=axis, keepdims=True)
        - unit * jnp.mean(scaled * unit, axis=axis, keepdims=True)
    )
    return inner * inverse


def split_two(value):
    high = value.astype(b16)
    low = (value - high.astype(f32)).astype(b16)
    return high, low


def after(value, *needed):
    return lax.optimization_barrier((value,) + needed)[0]


def pick(array, index):
    return lax.dynamic_index_in_dim(array, index, 0, keepdims=False)


def latent_part(attended, lat, vectors, planes, cotangent, numbers, part_rows, aligned, scale_self):
    total, width = lat.shape
    head = width // H
    extra = vectors.shape[0]
    out_rows = 9 * part_rows + extra
    shares = 2 * aligned
    stacked = shares + 16
    chunk = 128
    block = 512
    part = 512
    cubic = 0.044715
    root = math.sqrt(2.0 / math.pi)

    def kernel(
        num, att, lat_ref, vec, planes_ref, cot_ref, final, d_att, stream_out, keep, send,
        w, cot, low_b, act_b, low_c, q, k, v, mix, low_e, act_e, weights,
        unit_b, unit_c, unit_e, pre_b, pre_e, inv_b, inv_c, inv_e, stream, t, r, small, lhs, sems,
    ):
        core, inner = num[0], num[3]

        def load(plane, slot, sem):
            return pltpu.make_async_copy(planes_ref.at[plane], w.at[slot], sems.at[sem])

        cot_copy = pltpu.make_async_copy(cot_ref, cot, sems.at[11])
        copies = [load(i, i, i) for i in range(7)]
        for copy in copies:
            copy.start()
        cot_copy.start()
        row_eight, row_nine = load(7, 0, 7), load(8, 1, 8)
        again_two, again_one = load(1, 1, 9), load(0, 0, 10)

        lhs[pl.ds(shares, 16), :] = jnp.ones((16, total), b16)

        def each(size, body, carry=None):
            def step(i, c):
                return body(pl.ds(pl.multiple_of(i * size, size), size), c)

            return lax.fori_loop(0, total // size, step, 0 if carry is None else carry)

        def product(a, slot, flip):
            dims = (((1,), (1 if flip else 0,)), ((), ()))
            return lax.dot_general(a, w[slot], dims, preferred_element_type=f32)

        def into_t(a_ref, slot, flip=False, add=False):
            def body(rows, c):
                o = product(a_ref[rows, :], slot, flip)
                t[rows, :] = t[rows, :] + o if add else o
                return c

            each(block, body)

        def into_low(a_ref, slot, out, flip=False, bias=None):
            def body(rows, c):
                o = product(a_ref[rows, :], slot, flip)
                if bias is not None:
                    o = o + vec[bias : bias + 1, :]
                out[rows, :] = o.astype(b16)
                return c

            each(block, body)

        def row_of(i):
            return vec[i : i + 1, :]

        def residual(before, bias, unit, inv, low, gain):
            def body(rows, c):
                x = before[rows, :].astype(f32) + t[rows, :] + row_of(bias)
                stream[rows, :] = x
                center = x - jnp.mean(x, axis=1, keepdims=True)
                inverse = lax.rsqrt(jnp.mean(center * center, axis=1, keepdims=True) + epsilon)
                u = center * inverse
                unit[rows, :] = u
                inv[rows, :] = jnp.broadcast_to(inverse, (chunk, 128))
                low[rows, :] = (u * row_of(gain) + row_of(gain + 1)).astype(b16)
                return c

            each(chunk, body)

        def activate(bias, pre, act):
            def body(rows, c):
                x = t[rows, :] + row_of(bias)
                pre[rows, :] = x
                act[rows, :] = (0.5 * x * (1.0 + jnp.tanh(root * (x + cubic * (x * x * x))))).astype(b16)
                return c

            each(chunk, body)

        def activate_back(pre):
            def body(rows, c):
                x = pre[rows, :]
                square = x * x
                h = jnp.tanh(root * (x + cubic * (square * x)))
                slope = 0.5 * (1.0 + h) + 0.5 * x * (1.0 - h * h) * (root * (1.0 + 3.0 * cubic * square))
                r[rows, :] = (t[rows, :] * slope).astype(b16)
                return c

            each(chunk, body)

        def norm_grad(before, unit, inv, gain, place):
            def body(rows, c):
                g, u = t[rows, :], unit[rows, :]
                scaled = g * row_of(gain)
                inner_grad = (
                    scaled
                    - jnp.mean(scaled, axis=1, keepdims=True)
                    - u * jnp.mean(scaled * u, axis=1, keepdims=True)
                )
                x = before[rows, :].astype(f32) + inner_grad * inv[rows, 0:1]
                stream[rows, :] = x
                r[rows, :] = x.astype(b16)
                first = c[0] + jnp.sum((g * u).reshape(chunk // 8, 8, width), axis=0)
                second = c[1] + jnp.sum(g.reshape(chunk // 8, 8, width), axis=0)
                return first, second

            zero = jnp.zeros((8, width), f32)
            first, second = each(chunk, body, (zero, zero))
            put_sum(place, jnp.sum(first, axis=0, keepdims=True))
            put_sum(place + 1, jnp.sum(second, axis=0, keepdims=True))

        def put_sum(place, value):
            keep[pl.ds(9 * part_rows + place, 1), :] = value
            send[pl.ds(9 * part_rows + place, 1), :] = value

        def gradient(index, a_ref, r_ref, place=None):
            for s in range(2):
                columns = a_ref[:, pl.ds(pl.multiple_of(num[1 + s], 128), aligned)]
                lhs[pl.ds(s * aligned, aligned), :] = columns.T
            t[pl.ds(0, stacked), :] = jnp.dot(lhs[...], r_ref[...], preferred_element_type=f32)
            near = pl.multiple_of(core * aligned + inner, 8)
            far = pl.multiple_of((1 - core) * aligned + inner, 8)
            keep[pl.ds(index * part_rows, part_rows), :] = t[pl.ds(near, part_rows), :]
            send[pl.ds(index * part_rows, part_rows), :] = t[pl.ds(far, part_rows), :]
            if place is not None:
                put_sum(place, t[pl.ds(shares, 1), :])

        for place in (keep, send):
            place[pl.ds(9 * part_rows, extra), :] = jnp.zeros((extra, width), f32)

        copies[0].wait()
        into_t(att, 0)
        row_eight.start()
        residual(lat_ref, 4, unit_b, inv_b, low_b, 5)
        copies[1].wait()
        into_t(low_b, 1)
        row_nine.start()
        activate(7, pre_b, act_b)
        copies[2].wait()
        into_t(act_b, 2)
        residual(stream, 8, unit_c, inv_c, low_c, 9)
        copies[3].wait()
        into_low(low_c, 3, q, bias=11)
        copies[4].wait()
        into_low(low_c, 4, k)
        copies[5].wait()
        into_low(low_c, 5, v, bias=12)
        for h in range(H):
            cols = slice(h * head, (h + 1) * head)

            def attend(rows, c):
                s = scale_self * lax.dot_general(
                    q[rows, cols], k[:, cols], (((1,), (1,)), ((), ())), preferred_element_type=f32
                )
                e = jnp.exp(s - jnp.max(s, axis=1, keepdims=True))
                low = (e / jnp.sum(e, axis=1, keepdims=True)).astype(b16)
                weights[h, rows, :] = low
                mix[rows, cols] = jnp.dot(low, v[:, cols], preferred_element_type=f32).astype(b16)
                return c

            each(part, attend)
        copies[6].wait()
        into_t(mix, 6)
        residual(stream, 13, unit_e, inv_e, low_e, 14)
        row_eight.wait()
        into_t(low_e, 0)
        activate(16, pre_e, act_e)
        row_nine.wait()
        into_t(act_e, 1)

        def finish(rows, c):
            final[rows, :] = (stream[rows, :] + t[rows, :] + row_of(17)).astype(b16)
            return c

        each(chunk, finish)

        cot_copy.wait()
        into_t(cot, 1, flip=True)
        again_two.start()
        activate_back(pre_e)
        gradient(8, act_e, cot, 17)
        gradient(7, low_e, r, 16)
        into_t(r, 0, flip=True)
        again_one.start()
        norm_grad(cot, unit_e, inv_e, 14, 14)
        gradient(6, mix, r, 13)
        into_low(r, 6, d_att, flip=True)
        for h in range(H):
            cols = slice(h * head, (h + 1) * head)
            turned = (((0,), (0,)), ((), ()))
            small[...] = lax.dot_general(weights[h], d_att[:, cols], turned, preferred_element_type=f32).astype(b16)

            def attend_back(rows, c):
                d_weight = lax.dot_general(
                    d_att[rows, cols], v[:, cols], (((1,), (1,)), ((), ())), preferred_element_type=f32
                )
                weight = weights[h, rows, :].astype(f32)
                d_scores = weight * (d_weight - jnp.sum(d_weight * weight, axis=1, keepdims=True))
                d_scores = d_scores.astype(b16)
                weights[h, rows, :] = d_scores
                d_query = jnp.dot(d_scores, k[:, cols], preferred_element_type=f32) * scale_self
                d_att[rows, cols] = d_query.astype(b16)
                return c

            each(part, attend_back)
            d_keys = lax.dot_general(weights[h], q[:, cols], turned, preferred_element_type=f32) * scale_self
            k[:, cols] = d_keys.astype(b16)
            v[:, cols] = small[...]
        gradient(5, low_c, v, 12)
        gradient(4, low_c, k)
        gradient(3, low_c, d_att, 11)
        into_t(d_att, 3, flip=True)
        into_t(k, 4, flip=True, add=True)
        into_t(v, 5, flip=True, add=True)
        norm_grad(stream, unit_c, inv_c, 9, 9)
        gradient(2, act_b, r, 8)
        into_t(r, 2, flip=True)
        activate_back(pre_b)
        gradient(1, low_b, r, 7)
        again_two.wait()
        into_t(r, 1, flip=True)
        norm_grad(stream, unit_b, inv_b, 5, 5)
        gradient(0, att, r, 4)
        again_one.wait()
        into_low(r, 0, d_att, flip=True)
        put_sum(3, jnp.dot(jnp.ones((16, total), b16), d_att[...], preferred_element_type=f32)[0:1, :])

        def leave(rows, c):
            stream_out[rows, :] = stream[rows, :]
            return c

        each(chunk, leave)

    whole = pl.BlockSpec(memory_space=pltpu.VMEM)
    low = pltpu.VMEM((total, width), b16)
    high = pltpu.VMEM((total, width), f32)
    narrow = pltpu.VMEM((total, 128), f32)
    return pl.pallas_call(
        kernel,
        name="latent_part",
        in_specs=[pl.BlockSpec(memory_space=pltpu.SMEM), whole, whole, whole] + [pl.BlockSpec(memory_space=pl.ANY)] * 2,
        out_specs=[whole] * 5,
        out_shape=[
            jax.ShapeDtypeStruct((total, width), b16),
            jax.ShapeDtypeStruct((total, width), b16),
            jax.ShapeDtypeStruct((total, width), f32),
            jax.ShapeDtypeStruct((out_rows, width), f32),
            jax.ShapeDtypeStruct((out_rows, width), f32),
        ],
        scratch_shapes=[
            pltpu.VMEM((7, width, width), b16),
            low, low, low, low, low, low, low, low, low, low,
            pltpu.VMEM((H, total, total), b16),
            high, high, high, high, high, narrow, narrow, narrow, high, high, low,
            pltpu.VMEM((total, head), b16),
            pltpu.VMEM((stacked, total), b16),
            pltpu.SemaphoreType.DMA((12,)),
        ],
        compiler_params=pltpu.CompilerParams(vmem_limit_bytes=62 * 1024 * 1024),
    )(numbers, attended, lat, vectors, planes, cotangent)


def body(pixels, lengths, latents, w_square, w_input, vec_d, vec_c, cotangent):
    n = lax.axis_size("ctx")
    bits_all = n.bit_length() - 1
    rows = latents.shape[1]
    width = latents.shape[2]
    own_w = w_square.shape[1]
    channels = pixels.shape[1]
    slots = pixels.shape[2]
    total_rows = rows * n
    head_size = width // H
    scale = 1.0 / math.sqrt(width)
    scale_self = 1.0 / math.sqrt(head_size)
    core = lax.axis_index("seq")
    place = lax.axis_index("ctx")
    parity = place & 1
    pair = place >> 1
    wide = [4 << i for i in range(bits_all - 2)]

    def swap(x, bit):
        return lax.ppermute(x, "ctx", [(i, i ^ bit) for i in range(n)])

    def swap_core(x):
        return lax.ppermute(x, "seq", [(0, 1), (1, 0)])

    def ordered(mine, other, flag, axis):
        first = jnp.where(flag == 0, mine, other)
        second = jnp.where(flag == 0, other, mine)
        return jnp.concatenate([first, second], axis=axis)

    def quad(x, low, high, axis):
        one, two, three = swap(x, low), swap(x, high), swap(x, low | high)
        bit_low, bit_high = (place // low) & 1, (place // high) & 1
        near = ordered(x, one, bit_low, axis)
        far = ordered(two, three, bit_low, axis)
        return ordered(near, far, bit_high, axis)

    def both(x):
        return ordered(x, swap_core(x), core, 1)

    def gather_wide(x):
        rest = list(wide)
        x = x[None]
        while len(rest) > 1:
            x = quad(x[None], rest[0], rest[1], 0)
            x = x.reshape((-1,) + x.shape[2:])
            rest = rest[2:]
        for bit in rest:
            x = ordered(x[None], swap(x[None], bit), (place // bit) & 1, 0)
            x = x.reshape((-1,) + x.shape[2:])
        return x

    def own_steps(array, other):
        x = ordered(pick(array, parity), other, parity, 0)[None]
        for bit in wide:
            other = yield swap(x, bit)
            x = ordered(x, other, (place // bit) & 1, 0)
        other = yield swap(x, 2)
        x = ordered(x[:, None], other[:, None], (place // 2) & 1, 1)
        return x.reshape(total_rows, width)

    lanes = 384
    tall = (channels + 6 + 15) // 16 * 16
    packed = jnp.concatenate(
        [
            w_square[0],
            jnp.pad(w_input[0], ((0, 0), (0, tall - channels))),
            vec_d.T,
            jnp.zeros((own_w, lanes - tall - vec_d.shape[0]), b16),
        ],
        axis=1,
    )
    packed = gather_wide(packed[None])[:, 0]
    packed = quad(packed[:, None], 1, 2, 1)
    packed = both(packed.reshape(1, n * own_w, -1))[0]
    square_first = packed[:, :width]
    packed = lax.optimization_barrier(packed[:, width:])
    v_key = packed[:, :tall]
    vecf = matmul("kc,dc->kd", jnp.eye(24, lanes - tall, dtype=b16), packed[:, tall:])
    away = jnp.concatenate([pick(latents, 1 - parity), pick(cotangent, 1 - parity)], axis=0)
    away = swap(away, 1)
    lat = ordered(pick(latents, parity), away[:rows], parity, 0)
    lat = gather_wide(lat[None])
    lat = ordered(lat, swap(lat, 2), (place // 2) & 1, 1).reshape(total_rows, width)
    values_plane = jnp.pad(w_input[1:], ((0, 0), (0, 0), (0, width - channels)))
    planes = jnp.concatenate([w_square[1:], values_plane], axis=0)
    planes = lax.all_gather(planes, ("seq", "ctx"), axis=1, tiled=True)
    v_val = planes[9, :, :tall]

    latent = lat.astype(f32)
    norm_a, unit_a, inv_a = layer_norm(latent, vecf[0], vecf[1], 1)
    low_a = norm_a.astype(b16)
    query = (matmul("id,de->ie", low_a, square_first) + vecf[2]).astype(b16)
    gate = (matmul("dc,id->ci", v_key, query) * scale).astype(b16)
    gates = ordered(gate[None], swap(gate, 1)[None], parity, 0)
    steps = own_steps(after(cotangent, gates), away[rows:])
    hanging = [next(steps)]
    gathered = []

    def pace(value):
        if not hanging:
            return value
        value, other = lax.optimization_barrier((value, hanging.pop()))
        try:
            hanging.append(steps.send(other))
        except StopIteration as stop:
            gathered.append(stop.value)
        return value


    gain_in = vec_c.astype(f32)
    norm_x, unit_x, inv_x = layer_norm(pixels.astype(f32), gain_in[0][:, None], gain_in[1][:, None], 1)
    low_x = jnp.pad(norm_x.astype(b16), ((0, 0), (0, tall - channels), (0, 0)))
    position = place * slots + jnp.arange(slots, dtype=jnp.int32)
    valid = (position[None, :] < lengths[:, None])[:, None, :]
    scores = matmul("qci,qcj->qij", gates, low_x)
    top = jnp.max(jnp.where(valid, scores, -1e30), axis=2)
    top_hi, top_lo = split_two(top)
    shift = top_hi.astype(f32) + top_lo.astype(f32)
    expo = jnp.where(valid, jnp.exp(scores - shift[..., None]), 0.0)
    total_hi, total_lo = split_two(jnp.sum(expo, axis=2))
    mixed = matmul("qij,qcj->qci", expo.astype(b16), low_x).astype(b16)
    row = jnp.arange(tall)[:, None]

    def write(v, parts):
        for k, part in enumerate(parts):
            v = jnp.where(row == channels + k, part[..., None, :], v)
        return v

    pay = write(mixed, [top_hi, top_lo, total_hi, total_lo])

    def opened(p):
        s = p[channels : channels + 4].astype(f32)
        return p.astype(f32), s[0] + s[1], s[2] + s[3]

    def merge(a, b):
        va, ta, la = opened(a)
        vb, tb, lb = opened(b)
        t = jnp.maximum(ta, tb)
        ea = jnp.exp(ta - t)
        eb = jnp.exp(tb - t)
        return va * ea + vb * eb, t, la * ea + lb * eb

    def closed(v, t, l):
        return write(v.astype(b16), split_two(t) + split_two(l))

    state = merge(pick(pay, parity), pace(swap(pick(pay, 1 - parity), 1)))
    for bit in [2] + wide:
        mine = closed(*state)
        state = merge(mine, pace(swap(mine, bit)))
    while hanging:
        pace(state[0])
    cot = gathered[0]
    mix_sum, top_all, total_all = state
    mean_x = jnp.where(row < channels, mix_sum / total_all, 0.0)
    mean_low = mean_x.astype(b16)

    attended = (matmul("ci,dc->id", mean_low, v_val) + vecf[3]).astype(b16)
    part_rows = 2 * own_w
    aligned = max(part_rows, 128)
    base = pair * part_rows // aligned * aligned
    inner = pair * part_rows - base
    numbers = jnp.stack([core, base, n * own_w + base, inner]).astype(jnp.int32)
    final, d_attended, d_after_cross, keep, send = latent_part(
        attended, lat, vecf, planes, cot, numbers, part_rows, aligned, scale_self
    )

    def own_rows(array):
        mine = lax.dynamic_slice_in_dim(array, place * rows, rows, 0)
        theirs = lax.dynamic_slice_in_dim(array, (place ^ 1) * rows, rows, 0)
        return ordered(mine[None], swap(theirs, 1)[None], parity, 0)

    def share(a):
        return jnp.concatenate([lax.dynamic_slice_in_dim(a, s * n * own_w + base, aligned, 1) for s in range(2)], axis=1)

    def weight_grad(a, r):
        return matmul("ia,ie->ae", share(a), r)

    def window(part, which):
        return lax.dynamic_slice_in_dim(part, which * aligned + inner, part_rows, 0)

    def halves(x, which):
        return lax.dynamic_slice_in_dim(x, which * own_w, own_w, x.ndim - 2)

    def halved(x, which):
        top = halves(x[: 9 * part_rows].reshape(9, part_rows, width), which).reshape(9 * own_w, width)
        return jnp.concatenate([top, x[9 * part_rows :]], axis=0)

    def sums(x):
        return jnp.sum(x.astype(f32), axis=0, keepdims=True)

    pull = matmul("dc,id->ci", v_val, d_attended).astype(b16)
    delta = jnp.sum(pull.astype(f32) * mean_x, axis=0)
    pieces = split_two(top_all) + split_two(total_all) + split_two(delta)
    sent = write(pull, pieces)
    other = swap(sent, 1)
    core_sums = swap_core(after(send, sent))
    sents = ordered(sent[None], other[None], parity, 0)
    pulls = sents
    side = sents[:, channels : channels + 6].astype(f32)
    top_q = side[:, 0] + side[:, 1]
    total_q = side[:, 2] + side[:, 3]
    delta_q = side[:, 4] + side[:, 5]
    scores_again = matmul("qci,qcj->qij", gates, low_x)
    weight = jnp.where(valid, jnp.exp(scores_again - top_q[..., None]), 0.0) / total_q[..., None]
    d_weight = matmul("qci,qcj->qij", pulls, low_x)
    d_scores = (weight * (d_weight - delta_q[..., None])).astype(b16)
    weight_low = weight.astype(b16)
    force = matmul("qij,qcj->qci", d_scores, low_x).astype(b16)
    mine = pick(force, parity)
    other = swap(pick(force, 1 - parity), 1)
    held = after(d_scores, force)
    d_in_norm = (matmul("qci,qij->qcj", gates, held) + matmul("qci,qij->qcj", pulls, weight_low))[:, :channels]
    grad_pixels = norm_back(d_in_norm, unit_x, inv_x, gain_in[0][:, None], 1)
    grad_vc = [jnp.sum(d_in_norm * unit_x, axis=(0, 2)), jnp.sum(d_in_norm, axis=(0, 2))]
    grad_vc = jnp.pad(jnp.stack(grad_vc), ((0, 0), (0, total_rows - channels)))
    other = after(other, grad_vc)
    force_sum = mine.astype(f32) + other.astype(f32)
    chip_sums = None
    for bit in [2] + wide:
        mine = write(force_sum.astype(b16), split_two(grad_vc[0]) + split_two(grad_vc[1]))
        other = swap(mine, bit)
        if chip_sums is None:
            core_sums = after(keep, mine) + core_sums
            other, core_sums = lax.optimization_barrier((other, core_sums))
            latents_out = own_rows(after(final, mine))
            chip_sums = swap(halved(core_sums, 1 - parity).astype(b16), 1)
            part_att = matmul("ia,ci->ac", share(d_attended), mean_low)
            other = after(other, part_att)
        elif bit == wide[-1]:
            other, chip_sums = lax.optimization_barrier((other, chip_sums))
        force_sum = mine.astype(f32) + other.astype(f32)
        grad_vc = jnp.stack([force_sum[channels] + force_sum[channels + 1], force_sum[channels + 2] + force_sum[channels + 3]])
    force_low = jnp.where(row < channels, force_sum * scale, 0.0).astype(b16)
    d_query = matmul("ci,dc->id", force_low, v_key).astype(b16)
    part0 = weight_grad(low_a, d_query)
    d_norm_a = matmul("ie,de->id", d_query, square_first)
    grad_lat = d_after_cross + norm_back(d_norm_a, unit_a, inv_a, vecf[0], 1)
    grad_latents = own_rows(grad_lat)

    part_q = matmul("ia,ci->ac", share(query), force_low)
    pad_lanes = lanes - tall
    wide_all = width + 2 * lanes

    def gradients(which):
        full = [window(part0, which)]
        for part in (part_q, part_att):
            full.append(jnp.pad(window(part, which), ((0, 0), (0, pad_lanes))))
        return jnp.concatenate(full, axis=1)

    late_vec = jnp.concatenate([sums(d_norm_a * unit_a), sums(d_norm_a), sums(d_query), jnp.pad(grad_vc, ((0, 0), (0, width - total_rows)))], axis=0)
    vectors = jnp.concatenate([late_vec, jnp.zeros((3, width), f32)], axis=0)
    tail = jnp.pad(vectors, ((0, 0), (0, wide_all - width)))
    own = jnp.concatenate([gradients(core), tail], axis=0)
    own = own + swap_core(jnp.concatenate([gradients(1 - core), tail], axis=0).astype(b16)).astype(f32)

    def reduced(which):
        return jnp.concatenate([halves(own[:part_rows], which), own[part_rows:]], axis=0)

    own = reduced(parity) + swap(reduced(1 - parity).astype(b16), 1).astype(f32)
    late = own[None, :own_w, :width]
    chip_sums = halved(core_sums, parity) + chip_sums.astype(f32)
    grad_input = jnp.stack([own[:own_w, width : width + channels], own[:own_w, width + lanes : width + lanes + channels]])
    tail = own[own_w:, :width]
    grad_vc = tail[3:5, :channels]
    vectors = jnp.concatenate([tail[:3], chip_sums[9 * own_w + 3 :]], axis=0)
    grad_vec = lax.dynamic_slice_in_dim(vectors, core * n * own_w + place * own_w, own_w, 1)[: vec_d.shape[0]]
    grad_square = jnp.concatenate([late, chip_sums[: 9 * own_w].reshape(9, own_w, width)], axis=0)
    return (latents_out, grad_latents, grad_pixels, grad_square, grad_input, grad_vec, grad_vc)


def solution(mesh):
    placed = (
        P("seq", None, "ctx"),
        P("seq"),
        P("seq", "ctx", None),
        P(None, ("seq", "ctx"), None),
        P(None, ("seq", "ctx"), None),
        P(None, ("seq", "ctx")),
        P(),
        P("seq", "ctx", None),
    )
    return jax.shard_map(
        body,
        mesh=mesh,
        in_specs=placed,
        out_specs=(
            P("seq", "ctx", None),
            P("seq", "ctx", None),
            P("seq", None, "ctx"),
            P(None, ("seq", "ctx"), None),
            P(None, ("seq", "ctx"), None),
            P(None, ("seq", "ctx")),
            P(),
        ),
        check_vma=False,
    )
```

```python
import math

import jax
import jax.numpy as jnp
from jax import lax
from jax.experimental import pallas as pl
from jax.experimental.pallas import tpu as pltpu
from jax.sharding import PartitionSpec as P

H = 8
epsilon = 1e-05
f32 = jnp.float32
b16 = jnp.bfloat16


def matmul(form, left, right):
    return jnp.einsum(form, left, right, preferred_element_type=f32)


def layer_norm(value, gain, shift, axis):
    center = value - jnp.mean(value, axis=axis, keepdims=True)
    spread = jnp.mean(center * center, axis=axis, keepdims=True)
    inverse = lax.rsqrt(spread + epsilon)
    unit = center * inverse
    return (unit * gain + shift, unit, inverse)


def norm_back(grad, unit, inverse, gain, axis):
    scaled = grad * gain
    inner = (
        scaled
        - jnp.mean(scaled, axis=axis, keepdims=True)
        - unit * jnp.mean(scaled * unit, axis=axis, keepdims=True)
    )
    return inner * inverse


def split_two(value):
    high = value.astype(b16)
    low = (value - high.astype(f32)).astype(b16)
    return high, low


def after(value, *needed):
    return lax.optimization_barrier((value,) + needed)[0]


def pick(array, index):
    return lax.dynamic_index_in_dim(array, index, 0, keepdims=False)


def latent_part(attended, lat, vectors, planes, cotangent, numbers, part_rows, aligned, scale_self):
    total, width = lat.shape
    head = width // H
    extra = vectors.shape[0]
    out_rows = 9 * part_rows + extra
    shares = 2 * aligned
    stacked = shares + 16
    chunk = 128
    block = 512
    part = 512
    cubic = 0.044715
    root = math.sqrt(2.0 / math.pi)

    def kernel(
        num, att, lat_ref, vec, planes_ref, cot_ref, final, d_att, stream_out, keep, send,
        w, cot, low_b, act_b, low_c, q, k, v, mix, low_e, act_e, weights,
        unit_b, unit_c, unit_e, pre_b, pre_e, inv_b, inv_c, inv_e, stream, t, r, small, lhs, sems,
    ):
        core, inner = num[0], num[3]

        def load(plane, slot, sem):
            return pltpu.make_async_copy(planes_ref.at[plane], w.at[slot], sems.at[sem])

        cot_copy = pltpu.make_async_copy(cot_ref, cot, sems.at[11])
        copies = [load(i, i, i) for i in range(7)]
        for copy in copies:
            copy.start()
        cot_copy.start()
        row_eight, row_nine = load(7, 0, 7), load(8, 1, 8)
        again_two, again_one = load(1, 1, 9), load(0, 0, 10)

        lhs[pl.ds(shares, 16), :] = jnp.ones((16, total), b16)

        def each(size, body, carry=None):
            def step(i, c):
                return body(pl.ds(pl.multiple_of(i * size, size), size), c)

            return lax.fori_loop(0, total // size, step, 0 if carry is None else carry)

        def product(a, slot, flip):
            dims = (((1,), (1 if flip else 0,)), ((), ()))
            return lax.dot_general(a, w[slot], dims, preferred_element_type=f32)

        def into_t(a_ref, slot, flip=False, add=False):
            def body(rows, c):
                o = product(a_ref[rows, :], slot, flip)
                t[rows, :] = t[rows, :] + o if add else o
                return c

            each(block, body)

        def into_low(a_ref, slot, out, flip=False, bias=None):
            def body(rows, c):
                o = product(a_ref[rows, :], slot, flip)
                if bias is not None:
                    o = o + vec[bias : bias + 1, :]
                out[rows, :] = o.astype(b16)
                return c

            each(block, body)

        def row_of(i):
            return vec[i : i + 1, :]

        def residual(before, bias, unit, inv, low, gain):
            def body(rows, c):
                x = before[rows, :].astype(f32) + t[rows, :] + row_of(bias)
                stream[rows, :] = x
                center = x - jnp.mean(x, axis=1, keepdims=True)
                inverse = lax.rsqrt(jnp.mean(center * center, axis=1, keepdims=True) + epsilon)
                u = center * inverse
                unit[rows, :] = u
                inv[rows, :] = jnp.broadcast_to(inverse, (chunk, 128))
                low[rows, :] = (u * row_of(gain) + row_of(gain + 1)).astype(b16)
                return c

            each(chunk, body)

        def activate(bias, pre, act):
            def body(rows, c):
                x = t[rows, :] + row_of(bias)
                pre[rows, :] = x
                act[rows, :] = (0.5 * x * (1.0 + jnp.tanh(root * (x + cubic * (x * x * x))))).astype(b16)
                return c

            each(chunk, body)

        def activate_back(pre):
            def body(rows, c):
                x = pre[rows, :]
                square = x * x
                h = jnp.tanh(root * (x + cubic * (square * x)))
                slope = 0.5 * (1.0 + h) + 0.5 * x * (1.0 - h * h) * (root * (1.0 + 3.0 * cubic * square))
                r[rows, :] = (t[rows, :] * slope).astype(b16)
                return c

            each(chunk, body)

        def norm_grad(before, unit, inv, gain, place):
            def body(rows, c):
                g, u = t[rows, :], unit[rows, :]
                scaled = g * row_of(gain)
                inner_grad = (
                    scaled
                    - jnp.mean(scaled, axis=1, keepdims=True)
                    - u * jnp.mean(scaled * u, axis=1, keepdims=True)
                )
                x = before[rows, :].astype(f32) + inner_grad * inv[rows, 0:1]
                stream[rows, :] = x
                r[rows, :] = x.astype(b16)
                first = c[0] + jnp.sum((g * u).reshape(chunk // 8, 8, width), axis=0)
                second = c[1] + jnp.sum(g.reshape(chunk // 8, 8, width), axis=0)
                return first, second

            zero = jnp.zeros((8, width), f32)
            first, second = each(chunk, body, (zero, zero))
            put_sum(place, jnp.sum(first, axis=0, keepdims=True))
            put_sum(place + 1, jnp.sum(second, axis=0, keepdims=True))

        def put_sum(place, value):
            keep[pl.ds(9 * part_rows + place, 1), :] = value
            send[pl.ds(9 * part_rows + place, 1), :] = value

        def gradient(index, a_ref, r_ref, place=None):
            for s in range(2):
                columns = a_ref[:, pl.ds(pl.multiple_of(num[1 + s], 128), aligned)]
                lhs[pl.ds(s * aligned, aligned), :] = columns.T
            t[pl.ds(0, stacked), :] = jnp.dot(lhs[...], r_ref[...], preferred_element_type=f32)
            near = pl.multiple_of(core * aligned + inner, 8)
            far = pl.multiple_of((1 - core) * aligned + inner, 8)
            keep[pl.ds(index * part_rows, part_rows), :] = t[pl.ds(near, part_rows), :]
            send[pl.ds(index * part_rows, part_rows), :] = t[pl.ds(far, part_rows), :]
            if place is not None:
                put_sum(place, t[pl.ds(shares, 1), :])

        for place in (keep, send):
            place[pl.ds(9 * part_rows, extra), :] = jnp.zeros((extra, width), f32)

        copies[0].wait()
        into_t(att, 0)
        row_eight.start()
        residual(lat_ref, 4, unit_b, inv_b, low_b, 5)
        copies[1].wait()
        into_t(low_b, 1)
        row_nine.start()
        activate(7, pre_b, act_b)
        copies[2].wait()
        into_t(act_b, 2)
        residual(stream, 8, unit_c, inv_c, low_c, 9)
        copies[3].wait()
        into_low(low_c, 3, q, bias=11)
        copies[4].wait()
        into_low(low_c, 4, k)
        copies[5].wait()
        into_low(low_c, 5, v, bias=12)
        for h in range(H):
            cols = slice(h * head, (h + 1) * head)

            def attend(rows, c):
                s = scale_self * lax.dot_general(
                    q[rows, cols], k[:, cols], (((1,), (1,)), ((), ())), preferred_element_type=f32
                )
                e = jnp.exp(s - jnp.max(s, axis=1, keepdims=True))
                low = (e / jnp.sum(e, axis=1, keepdims=True)).astype(b16)
                weights[h, rows, :] = low
                mix[rows, cols] = jnp.dot(low, v[:, cols], preferred_element_type=f32).astype(b16)
                return c

            each(part, attend)
        copies[6].wait()
        into_t(mix, 6)
        residual(stream, 13, unit_e, inv_e, low_e, 14)
        row_eight.wait()
        into_t(low_e, 0)
        activate(16, pre_e, act_e)
        row_nine.wait()
        into_t(act_e, 1)

        def finish(rows, c):
            final[rows, :] = (stream[rows, :] + t[rows, :] + row_of(17)).astype(b16)
            return c

        each(chunk, finish)

        cot_copy.wait()
        into_t(cot, 1, flip=True)
        again_two.start()
        activate_back(pre_e)
        gradient(8, act_e, cot, 17)
        gradient(7, low_e, r, 16)
        into_t(r, 0, flip=True)
        again_one.start()
        norm_grad(cot, unit_e, inv_e, 14, 14)
        gradient(6, mix, r, 13)
        into_low(r, 6, d_att, flip=True)
        for h in range(H):
            cols = slice(h * head, (h + 1) * head)
            turned = (((0,), (0,)), ((), ()))
            small[...] = lax.dot_general(weights[h], d_att[:, cols], turned, preferred_element_type=f32).astype(b16)

            def attend_back(rows, c):
                d_weight = lax.dot_general(
                    d_att[rows, cols], v[:, cols], (((1,), (1,)), ((), ())), preferred_element_type=f32
                )
                weight = weights[h, rows, :].astype(f32)
                d_scores = weight * (d_weight - jnp.sum(d_weight * weight, axis=1, keepdims=True))
                d_scores = d_scores.astype(b16)
                weights[h, rows, :] = d_scores
                d_query = jnp.dot(d_scores, k[:, cols], preferred_element_type=f32) * scale_self
                d_att[rows, cols] = d_query.astype(b16)
                return c

            each(part, attend_back)
            d_keys = lax.dot_general(weights[h], q[:, cols], turned, preferred_element_type=f32) * scale_self
            k[:, cols] = d_keys.astype(b16)
            v[:, cols] = small[...]
        gradient(5, low_c, v, 12)
        gradient(4, low_c, k)
        gradient(3, low_c, d_att, 11)
        into_t(d_att, 3, flip=True)
        into_t(k, 4, flip=True, add=True)
        into_t(v, 5, flip=True, add=True)
        norm_grad(stream, unit_c, inv_c, 9, 9)
        gradient(2, act_b, r, 8)
        into_t(r, 2, flip=True)
        activate_back(pre_b)
        gradient(1, low_b, r, 7)
        again_two.wait()
        into_t(r, 1, flip=True)
        norm_grad(stream, unit_b, inv_b, 5, 5)
        gradient(0, att, r, 4)
        again_one.wait()
        into_low(r, 0, d_att, flip=True)
        put_sum(3, jnp.dot(jnp.ones((16, total), b16), d_att[...], preferred_element_type=f32)[0:1, :])

        def leave(rows, c):
            stream_out[rows, :] = stream[rows, :]
            return c

        each(chunk, leave)

    whole = pl.BlockSpec(memory_space=pltpu.VMEM)
    low = pltpu.VMEM((total, width), b16)
    high = pltpu.VMEM((total, width), f32)
    narrow = pltpu.VMEM((total, 128), f32)
    return pl.pallas_call(
        kernel,
        name="latent_part",
        in_specs=[pl.BlockSpec(memory_space=pltpu.SMEM), whole, whole, whole] + [pl.BlockSpec(memory_space=pl.ANY)] * 2,
        out_specs=[whole] * 5,
        out_shape=[
            jax.ShapeDtypeStruct((total, width), b16),
            jax.ShapeDtypeStruct((total, width), b16),
            jax.ShapeDtypeStruct((total, width), f32),
            jax.ShapeDtypeStruct((out_rows, width), f32),
            jax.ShapeDtypeStruct((out_rows, width), f32),
        ],
        scratch_shapes=[
            pltpu.VMEM((7, width, width), b16),
            low, low, low, low, low, low, low, low, low, low,
            pltpu.VMEM((H, total, total), b16),
            high, high, high, high, high, narrow, narrow, narrow, high, high, low,
            pltpu.VMEM((total, head), b16),
            pltpu.VMEM((stacked, total), b16),
            pltpu.SemaphoreType.DMA((12,)),
        ],
        compiler_params=pltpu.CompilerParams(vmem_limit_bytes=65400 * 1024),
    )(numbers, attended, lat, vectors, planes, cotangent)


def body(pixels, lengths, latents, w_square, w_input, vec_d, vec_c, cotangent):
    n = lax.axis_size("ctx")
    bits_all = n.bit_length() - 1
    rows = latents.shape[1]
    width = latents.shape[2]
    own_w = w_square.shape[1]
    channels = pixels.shape[1]
    slots = pixels.shape[2]
    total_rows = rows * n
    head_size = width // H
    scale = 1.0 / math.sqrt(width)
    scale_self = 1.0 / math.sqrt(head_size)
    core = lax.axis_index("seq")
    place = lax.axis_index("ctx")
    parity = place & 1
    pair = place >> 1
    wide = [4 << i for i in range(bits_all - 2)]

    def swap(x, bit):
        return lax.ppermute(x, "ctx", [(i, i ^ bit) for i in range(n)])

    def swap_core(x):
        return lax.ppermute(x, "seq", [(0, 1), (1, 0)])

    def ordered(mine, other, flag, axis):
        first = jnp.where(flag == 0, mine, other)
        second = jnp.where(flag == 0, other, mine)
        return jnp.concatenate([first, second], axis=axis)

    def quad(x, low, high, axis):
        one, two, three = swap(x, low), swap(x, high), swap(x, low | high)
        bit_low, bit_high = (place // low) & 1, (place // high) & 1
        near = ordered(x, one, bit_low, axis)
        far = ordered(two, three, bit_low, axis)
        return ordered(near, far, bit_high, axis)

    def both(x):
        return ordered(x, swap_core(x), core, 1)

    def gather_wide(x):
        rest = list(wide)
        x = x[None]
        while len(rest) > 1:
            x = quad(x[None], rest[0], rest[1], 0)
            x = x.reshape((-1,) + x.shape[2:])
            rest = rest[2:]
        for bit in rest:
            x = ordered(x[None], swap(x[None], bit), (place // bit) & 1, 0)
            x = x.reshape((-1,) + x.shape[2:])
        return x

    def own_steps(array, other):
        x = ordered(pick(array, parity), other, parity, 0)[None]
        for bit in wide:
            other = yield swap(x, bit)
            x = ordered(x, other, (place // bit) & 1, 0)
        other = yield swap(x, 2)
        x = ordered(x[:, None], other[:, None], (place // 2) & 1, 1)
        return x.reshape(total_rows, width)

    lanes = 384
    tall = (channels + 6 + 15) // 16 * 16
    packed = jnp.concatenate(
        [
            w_square[0],
            jnp.pad(w_input[0], ((0, 0), (0, tall - channels))),
            vec_d.T,
            jnp.zeros((own_w, lanes - tall - vec_d.shape[0]), b16),
            jnp.pad(w_input[1], ((0, 0), (0, lanes - channels))),
        ],
        axis=1,
    )
    packed = gather_wide(packed[None])[:, 0]
    packed = quad(packed[:, None], 1, 2, 1)
    packed = both(packed.reshape(1, n * own_w, -1))[0]
    square_first = packed[:, :width]
    packed = lax.optimization_barrier(packed[:, width:])
    v_key = packed[:, :tall]
    v_val = packed[:, lanes : lanes + tall]
    vecf = matmul("kc,dc->kd", jnp.eye(24, lanes - tall, dtype=b16), packed[:, tall:lanes])
    away = jnp.concatenate([pick(latents, 1 - parity), pick(cotangent, 1 - parity)], axis=0)
    away = swap(away, 1)
    lat = ordered(pick(latents, parity), away[:rows], parity, 0)
    lat = gather_wide(lat[None])
    lat = ordered(lat, swap(lat, 2), (place // 2) & 1, 1).reshape(total_rows, width)
    planes = lax.all_gather(w_square[1:], ("seq", "ctx"), axis=1, tiled=True)

    latent = lat.astype(f32)
    norm_a, unit_a, inv_a = layer_norm(latent, vecf[0], vecf[1], 1)
    low_a = norm_a.astype(b16)
    query = (matmul("id,de->ie", low_a, square_first) + vecf[2]).astype(b16)
    gate = (matmul("dc,id->ci", v_key, query) * scale).astype(b16)
    gates = ordered(gate[None], swap(gate, 1)[None], parity, 0)
    steps = own_steps(after(cotangent, gates), away[rows:])
    hanging = [next(steps)]
    gathered = []

    def pace(value):
        if not hanging:
            return value
        value, other = lax.optimization_barrier((value, hanging.pop()))
        try:
            hanging.append(steps.send(other))
        except StopIteration as stop:
            gathered.append(stop.value)
        return value


    gain_in = vec_c.astype(f32)
    norm_x, unit_x, inv_x = layer_norm(pixels.astype(f32), gain_in[0][:, None], gain_in[1][:, None], 1)
    low_x = jnp.pad(norm_x.astype(b16), ((0, 0), (0, tall - channels), (0, 0)))
    position = place * slots + jnp.arange(slots, dtype=jnp.int32)
    valid = (position[None, :] < lengths[:, None])[:, None, :]
    scores = matmul("qci,qcj->qij", gates, low_x)
    top = jnp.max(jnp.where(valid, scores, -1e30), axis=2)
    top_hi, top_lo = split_two(top)
    shift = top_hi.astype(f32) + top_lo.astype(f32)
    expo = jnp.where(valid, jnp.exp(scores - shift[..., None]), 0.0)
    total_hi, total_lo = split_two(jnp.sum(expo, axis=2))
    mixed = matmul("qij,qcj->qci", expo.astype(b16), low_x).astype(b16)
    row = jnp.arange(tall)[:, None]

    def write(v, parts):
        for k, part in enumerate(parts):
            v = jnp.where(row == channels + k, part[..., None, :], v)
        return v

    pay = write(mixed, [top_hi, top_lo, total_hi, total_lo])

    def opened(p):
        s = p[channels : channels + 4].astype(f32)
        return p.astype(f32), s[0] + s[1], s[2] + s[3]

    def merge(a, b):
        va, ta, la = opened(a)
        vb, tb, lb = opened(b)
        t = jnp.maximum(ta, tb)
        ea = jnp.exp(ta - t)
        eb = jnp.exp(tb - t)
        return va * ea + vb * eb, t, la * ea + lb * eb

    def closed(v, t, l):
        return write(v.astype(b16), split_two(t) + split_two(l))

    state = merge(pick(pay, parity), pace(swap(pick(pay, 1 - parity), 1)))
    for bit in [2] + wide:
        mine = closed(*state)
        state = merge(mine, pace(swap(mine, bit)))
    while hanging:
        pace(state[0])
    cot = gathered[0]
    mix_sum, top_all, total_all = state
    mean_x = jnp.where(row < channels, mix_sum / total_all, 0.0)
    mean_low = mean_x.astype(b16)

    attended = (matmul("ci,dc->id", mean_low, v_val) + vecf[3]).astype(b16)
    part_rows = 2 * own_w
    aligned = max(part_rows, 128)
    base = pair * part_rows // aligned * aligned
    inner = pair * part_rows - base
    numbers = jnp.stack([core, base, n * own_w + base, inner]).astype(jnp.int32)
    final, d_attended, d_after_cross, keep, send = latent_part(
        attended, lat, vecf, planes, cot, numbers, part_rows, aligned, scale_self
    )

    def own_rows(array):
        mine = lax.dynamic_slice_in_dim(array, place * rows, rows, 0)
        theirs = lax.dynamic_slice_in_dim(array, (place ^ 1) * rows, rows, 0)
        return ordered(mine[None], swap(theirs, 1)[None], parity, 0)

    def share(a):
        return jnp.concatenate([lax.dynamic_slice_in_dim(a, s * n * own_w + base, aligned, 1) for s in range(2)], axis=1)

    def weight_grad(a, r):
        return matmul("ia,ie->ae", share(a), r)

    def window(part, which):
        return lax.dynamic_slice_in_dim(part, which * aligned + inner, part_rows, 0)

    def halves(x, which):
        return lax.dynamic_slice_in_dim(x, which * own_w, own_w, x.ndim - 2)

    def halved(x, which):
        top = halves(x[: 9 * part_rows].reshape(9, part_rows, width), which).reshape(9 * own_w, width)
        return jnp.concatenate([top, x[9 * part_rows :]], axis=0)

    def sums(x):
        return jnp.sum(x.astype(f32), axis=0, keepdims=True)

    pull = matmul("dc,id->ci", v_val, d_attended).astype(b16)
    delta = jnp.sum(pull.astype(f32) * mean_x, axis=0)
    pieces = split_two(top_all) + split_two(total_all) + split_two(delta)
    sent = write(pull, pieces)
    other = swap(sent, 1)
    core_sums = swap_core(after(send, sent))
    sents = ordered(sent[None], other[None], parity, 0)
    pulls = sents
    side = sents[:, channels : channels + 6].astype(f32)
    top_q = side[:, 0] + side[:, 1]
    total_q = side[:, 2] + side[:, 3]
    delta_q = side[:, 4] + side[:, 5]
    scores_again = matmul("qci,qcj->qij", gates, low_x)
    weight = jnp.where(valid, jnp.exp(scores_again - top_q[..., None]), 0.0) / total_q[..., None]
    d_weight = matmul("qci,qcj->qij", pulls, low_x)
    d_scores = (weight * (d_weight - delta_q[..., None])).astype(b16)
    weight_low = weight.astype(b16)
    force = matmul("qij,qcj->qci", d_scores, low_x).astype(b16)
    mine = pick(force, parity)
    other = swap(pick(force, 1 - parity), 1)
    held = after(d_scores, force)
    d_in_norm = (matmul("qci,qij->qcj", gates, held) + matmul("qci,qij->qcj", pulls, weight_low))[:, :channels]
    grad_pixels = norm_back(d_in_norm, unit_x, inv_x, gain_in[0][:, None], 1)
    grad_vc = [jnp.sum(d_in_norm * unit_x, axis=(0, 2)), jnp.sum(d_in_norm, axis=(0, 2))]
    grad_vc = jnp.pad(jnp.stack(grad_vc), ((0, 0), (0, total_rows - channels)))
    other = after(other, grad_vc)
    force_sum = mine.astype(f32) + other.astype(f32)
    chip_sums = None
    for bit in [2] + wide:
        mine = write(force_sum.astype(b16), split_two(grad_vc[0]) + split_two(grad_vc[1]))
        other = swap(mine, bit)
        if chip_sums is None:
            core_sums = after(keep, mine) + core_sums
            other, core_sums = lax.optimization_barrier((other, core_sums))
            latents_out = own_rows(after(final, mine))
            chip_sums = swap(halved(core_sums, 1 - parity).astype(b16), 1)
            part_att = matmul("ia,ci->ac", share(d_attended), mean_low)
            other = after(other, part_att)
        elif bit == wide[-1]:
            other, chip_sums = lax.optimization_barrier((other, chip_sums))
        force_sum = mine.astype(f32) + other.astype(f32)
        grad_vc = jnp.stack([force_sum[channels] + force_sum[channels + 1], force_sum[channels + 2] + force_sum[channels + 3]])
    force_low = jnp.where(row < channels, force_sum * scale, 0.0).astype(b16)
    d_query = matmul("ci,dc->id", force_low, v_key).astype(b16)
    part0 = weight_grad(low_a, d_query)
    d_norm_a = matmul("ie,de->id", d_query, square_first)
    grad_lat = d_after_cross + norm_back(d_norm_a, unit_a, inv_a, vecf[0], 1)
    grad_latents = own_rows(grad_lat)

    part_q = matmul("ia,ci->ac", share(query), force_low)
    pad_lanes = lanes - tall
    wide_all = width + 2 * lanes

    def gradients(which):
        full = [window(part0, which)]
        for part in (part_q, part_att):
            full.append(jnp.pad(window(part, which), ((0, 0), (0, pad_lanes))))
        return jnp.concatenate(full, axis=1)

    late_vec = jnp.concatenate([sums(d_norm_a * unit_a), sums(d_norm_a), sums(d_query), jnp.pad(grad_vc, ((0, 0), (0, width - total_rows)))], axis=0)
    vectors = jnp.concatenate([late_vec, jnp.zeros((3, width), f32)], axis=0)
    tail = jnp.pad(vectors, ((0, 0), (0, wide_all - width)))
    own = jnp.concatenate([gradients(core), tail], axis=0)
    own = own + swap_core(jnp.concatenate([gradients(1 - core), tail], axis=0).astype(b16)).astype(f32)

    def reduced(which):
        return jnp.concatenate([halves(own[:part_rows], which), own[part_rows:]], axis=0)

    own = reduced(parity) + swap(reduced(1 - parity).astype(b16), 1).astype(f32)
    late = own[None, :own_w, :width]
    chip_sums = halved(core_sums, parity) + chip_sums.astype(f32)
    grad_input = jnp.stack([own[:own_w, width : width + channels], own[:own_w, width + lanes : width + lanes + channels]])
    tail = own[own_w:, :width]
    grad_vc = tail[3:5, :channels]
    vectors = jnp.concatenate([tail[:3], chip_sums[9 * own_w + 3 :]], axis=0)
    grad_vec = lax.dynamic_slice_in_dim(vectors, core * n * own_w + place * own_w, own_w, 1)[: vec_d.shape[0]]
    grad_square = jnp.concatenate([late, chip_sums[: 9 * own_w].reshape(9, own_w, width)], axis=0)
    return (latents_out, grad_latents, grad_pixels, grad_square, grad_input, grad_vec, grad_vc)


def solution(mesh):
    placed = (
        P("seq", None, "ctx"),
        P("seq"),
        P("seq", "ctx", None),
        P(None, ("seq", "ctx"), None),
        P(None, ("seq", "ctx"), None),
        P(None, ("seq", "ctx")),
        P(),
        P("seq", "ctx", None),
    )
    return jax.shard_map(
        body,
        mesh=mesh,
        in_specs=placed,
        out_specs=(
            P("seq", "ctx", None),
            P("seq", "ctx", None),
            P("seq", None, "ctx"),
            P(None, ("seq", "ctx"), None),
            P(None, ("seq", "ctx"), None),
            P(None, ("seq", "ctx")),
            P(),
        ),
        check_vma=False,
    )
```

```python
import math

import jax
import jax.numpy as jnp
from jax import lax
from jax.experimental import pallas as pl
from jax.experimental.pallas import tpu as pltpu
from jax.sharding import PartitionSpec as P

H = 8
epsilon = 1e-05
f32 = jnp.float32
b16 = jnp.bfloat16


def matmul(form, left, right):
    return jnp.einsum(form, left, right, preferred_element_type=f32)


def layer_norm(value, gain, shift, axis):
    center = value - jnp.mean(value, axis=axis, keepdims=True)
    spread = jnp.mean(center * center, axis=axis, keepdims=True)
    inverse = lax.rsqrt(spread + epsilon)
    unit = center * inverse
    return (unit * gain + shift, unit, inverse)


def norm_back(grad, unit, inverse, gain, axis):
    scaled = grad * gain
    inner = (
        scaled
        - jnp.mean(scaled, axis=axis, keepdims=True)
        - unit * jnp.mean(scaled * unit, axis=axis, keepdims=True)
    )
    return inner * inverse


def split_two(value):
    high = value.astype(b16)
    low = (value - high.astype(f32)).astype(b16)
    return high, low


def after(value, *needed):
    return lax.optimization_barrier((value,) + needed)[0]


def pick(array, index):
    return lax.dynamic_index_in_dim(array, index, 0, keepdims=False)


def latent_part(attended, lat, vectors, planes, cotangent, numbers, part_rows, aligned, scale_self):
    total, width = lat.shape
    head = width // H
    extra = vectors.shape[0]
    out_rows = 9 * part_rows + extra
    shares = 2 * aligned
    stacked = shares + 16
    chunk = 256
    block = 512
    part = 512
    cubic = 0.044715
    root = math.sqrt(2.0 / math.pi)

    def kernel(
        num, att, lat_ref, vec, planes_ref, cot_ref, final, d_att, stream_out, keep, send,
        w, cot, low_b, act_b, low_c, q, k, v, mix, low_e, act_e, weights,
        unit_b, unit_c, unit_e, pre_b, pre_e, inv_b, inv_c, inv_e, stream, t, r, small, lhs, sems,
    ):
        core, inner = num[0], num[3]

        def load(plane, slot, sem):
            return pltpu.make_async_copy(planes_ref.at[plane], w.at[slot], sems.at[sem])

        cot_copy = pltpu.make_async_copy(cot_ref, cot, sems.at[11])
        copies = [load(i, i, i) for i in range(7)]
        for copy in copies:
            copy.start()
        cot_copy.start()
        row_eight, row_nine = load(7, 0, 7), load(8, 1, 8)
        again_two, again_one = load(1, 1, 9), load(0, 0, 10)

        lhs[pl.ds(shares, 16), :] = jnp.ones((16, total), b16)

        def each(size, body, carry=None):
            def step(i, c):
                return body(pl.ds(pl.multiple_of(i * size, size), size), c)

            return lax.fori_loop(0, total // size, step, 0 if carry is None else carry)

        def product(a, slot, flip):
            dims = (((1,), (1 if flip else 0,)), ((), ()))
            return lax.dot_general(a, w[slot], dims, preferred_element_type=f32)

        def into_t(a_ref, slot, flip=False, add=False):
            def body(rows, c):
                o = product(a_ref[rows, :], slot, flip)
                t[rows, :] = t[rows, :] + o if add else o
                return c

            each(block, body)

        def into_low(a_ref, slot, out, flip=False, bias=None):
            def body(rows, c):
                o = product(a_ref[rows, :], slot, flip)
                if bias is not None:
                    o = o + vec[bias : bias + 1, :]
                out[rows, :] = o.astype(b16)
                return c

            each(block, body)

        def row_of(i):
            return vec[i : i + 1, :]

        def residual(before, bias, unit, inv, low, gain):
            def body(rows, c):
                x = before[rows, :].astype(f32) + t[rows, :] + row_of(bias)
                stream[rows, :] = x
                center = x - jnp.mean(x, axis=1, keepdims=True)
                inverse = lax.rsqrt(jnp.mean(center * center, axis=1, keepdims=True) + epsilon)
                u = center * inverse
                unit[rows, :] = u
                inv[rows, :] = jnp.broadcast_to(inverse, (chunk, 128))
                low[rows, :] = (u * row_of(gain) + row_of(gain + 1)).astype(b16)
                return c

            each(chunk, body)

        def activate(bias, pre, act):
            def body(rows, c):
                x = t[rows, :] + row_of(bias)
                pre[rows, :] = x
                act[rows, :] = (0.5 * x * (1.0 + jnp.tanh(root * (x + cubic * (x * x * x))))).astype(b16)
                return c

            each(chunk, body)

        def activate_back(pre):
            def body(rows, c):
                x = pre[rows, :]
                square = x * x
                h = jnp.tanh(root * (x + cubic * (square * x)))
                slope = 0.5 * (1.0 + h) + 0.5 * x * (1.0 - h * h) * (root * (1.0 + 3.0 * cubic * square))
                r[rows, :] = (t[rows, :] * slope).astype(b16)
                return c

            each(chunk, body)

        def norm_grad(before, unit, inv, gain, place):
            def body(rows, c):
                g, u = t[rows, :], unit[rows, :]
                scaled = g * row_of(gain)
                inner_grad = (
                    scaled
                    - jnp.mean(scaled, axis=1, keepdims=True)
                    - u * jnp.mean(scaled * u, axis=1, keepdims=True)
                )
                x = before[rows, :].astype(f32) + inner_grad * inv[rows, 0:1]
                stream[rows, :] = x
                r[rows, :] = x.astype(b16)
                first = c[0] + jnp.sum((g * u).reshape(chunk // 8, 8, width), axis=0)
                second = c[1] + jnp.sum(g.reshape(chunk // 8, 8, width), axis=0)
                return first, second

            zero = jnp.zeros((8, width), f32)
            first, second = each(chunk, body, (zero, zero))
            put_sum(place, jnp.sum(first, axis=0, keepdims=True))
            put_sum(place + 1, jnp.sum(second, axis=0, keepdims=True))

        def put_sum(place, value):
            keep[pl.ds(9 * part_rows + place, 1), :] = value
            send[pl.ds(9 * part_rows + place, 1), :] = value

        def gradient(index, a_ref, r_ref, place=None):
            for s in range(2):
                columns = a_ref[:, pl.ds(pl.multiple_of(num[1 + s], 128), aligned)]
                lhs[pl.ds(s * aligned, aligned), :] = columns.T
            t[pl.ds(0, stacked), :] = jnp.dot(lhs[...], r_ref[...], preferred_element_type=f32)
            near = pl.multiple_of(core * aligned + inner, 8)
            far = pl.multiple_of((1 - core) * aligned + inner, 8)
            keep[pl.ds(index * part_rows, part_rows), :] = t[pl.ds(near, part_rows), :]
            send[pl.ds(index * part_rows, part_rows), :] = t[pl.ds(far, part_rows), :]
            if place is not None:
                put_sum(place, t[pl.ds(shares, 1), :])

        for place in (keep, send):
            place[pl.ds(9 * part_rows, extra), :] = jnp.zeros((extra, width), f32)

        copies[0].wait()
        into_t(att, 0)
        row_eight.start()
        residual(lat_ref, 4, unit_b, inv_b, low_b, 5)
        copies[1].wait()
        into_t(low_b, 1)
        row_nine.start()
        activate(7, pre_b, act_b)
        copies[2].wait()
        into_t(act_b, 2)
        residual(stream, 8, unit_c, inv_c, low_c, 9)
        copies[3].wait()
        into_low(low_c, 3, q, bias=11)
        copies[4].wait()
        into_low(low_c, 4, k)
        copies[5].wait()
        into_low(low_c, 5, v, bias=12)
        for h in range(H):
            cols = slice(h * head, (h + 1) * head)

            def attend(rows, c):
                s = scale_self * lax.dot_general(
                    q[rows, cols], k[:, cols], (((1,), (1,)), ((), ())), preferred_element_type=f32
                )
                e = jnp.exp(s - jnp.max(s, axis=1, keepdims=True))
                low = (e / jnp.sum(e, axis=1, keepdims=True)).astype(b16)
                weights[h, rows, :] = low
                mix[rows, cols] = jnp.dot(low, v[:, cols], preferred_element_type=f32).astype(b16)
                return c

            each(part, attend)
        copies[6].wait()
        into_t(mix, 6)
        residual(stream, 13, unit_e, inv_e, low_e, 14)
        row_eight.wait()
        into_t(low_e, 0)
        activate(16, pre_e, act_e)
        row_nine.wait()
        into_t(act_e, 1)

        def finish(rows, c):
            final[rows, :] = (stream[rows, :] + t[rows, :] + row_of(17)).astype(b16)
            return c

        each(chunk, finish)

        cot_copy.wait()
        into_t(cot, 1, flip=True)
        again_two.start()
        activate_back(pre_e)
        gradient(8, act_e, cot, 17)
        gradient(7, low_e, r, 16)
        into_t(r, 0, flip=True)
        again_one.start()
        norm_grad(cot, unit_e, inv_e, 14, 14)
        gradient(6, mix, r, 13)
        into_low(r, 6, d_att, flip=True)
        for h in range(H):
            cols = slice(h * head, (h + 1) * head)
            turned = (((0,), (0,)), ((), ()))
            small[...] = lax.dot_general(weights[h], d_att[:, cols], turned, preferred_element_type=f32).astype(b16)

            def attend_back(rows, c):
                d_weight = lax.dot_general(
                    d_att[rows, cols], v[:, cols], (((1,), (1,)), ((), ())), preferred_element_type=f32
                )
                weight = weights[h, rows, :].astype(f32)
                d_scores = weight * (d_weight - jnp.sum(d_weight * weight, axis=1, keepdims=True))
                d_scores = d_scores.astype(b16)
                weights[h, rows, :] = d_scores
                d_query = jnp.dot(d_scores, k[:, cols], preferred_element_type=f32) * scale_self
                d_att[rows, cols] = d_query.astype(b16)
                return c

            each(part, attend_back)
            d_keys = lax.dot_general(weights[h], q[:, cols], turned, preferred_element_type=f32) * scale_self
            k[:, cols] = d_keys.astype(b16)
            v[:, cols] = small[...]
        gradient(5, low_c, v, 12)
        gradient(4, low_c, k)
        gradient(3, low_c, d_att, 11)
        into_t(d_att, 3, flip=True)
        into_t(k, 4, flip=True, add=True)
        into_t(v, 5, flip=True, add=True)
        norm_grad(stream, unit_c, inv_c, 9, 9)
        gradient(2, act_b, r, 8)
        into_t(r, 2, flip=True)
        activate_back(pre_b)
        gradient(1, low_b, r, 7)
        again_two.wait()
        into_t(r, 1, flip=True)
        norm_grad(stream, unit_b, inv_b, 5, 5)
        gradient(0, att, r, 4)
        again_one.wait()
        into_low(r, 0, d_att, flip=True)
        put_sum(3, jnp.dot(jnp.ones((16, total), b16), d_att[...], preferred_element_type=f32)[0:1, :])

        def leave(rows, c):
            stream_out[rows, :] = stream[rows, :]
            return c

        each(chunk, leave)

    whole = pl.BlockSpec(memory_space=pltpu.VMEM)
    low = pltpu.VMEM((total, width), b16)
    high = pltpu.VMEM((total, width), f32)
    narrow = pltpu.VMEM((total, 128), f32)
    return pl.pallas_call(
        kernel,
        name="latent_part",
        in_specs=[pl.BlockSpec(memory_space=pltpu.SMEM), whole, whole, whole] + [pl.BlockSpec(memory_space=pl.ANY)] * 2,
        out_specs=[whole] * 5,
        out_shape=[
            jax.ShapeDtypeStruct((total, width), b16),
            jax.ShapeDtypeStruct((total, width), b16),
            jax.ShapeDtypeStruct((total, width), f32),
            jax.ShapeDtypeStruct((out_rows, width), f32),
            jax.ShapeDtypeStruct((out_rows, width), f32),
        ],
        scratch_shapes=[
            pltpu.VMEM((7, width, width), b16),
            low, low, low, low, low, low, low, low, low, low,
            pltpu.VMEM((H, total, total), b16),
            high, high, high, high, high, narrow, narrow, narrow, high, high, low,
            pltpu.VMEM((total, head), b16),
            pltpu.VMEM((stacked, total), b16),
            pltpu.SemaphoreType.DMA((12,)),
        ],
        compiler_params=pltpu.CompilerParams(vmem_limit_bytes=65400 * 1024),
    )(numbers, attended, lat, vectors, planes, cotangent)


def body(pixels, lengths, latents, w_square, w_input, vec_d, vec_c, cotangent):
    n = lax.axis_size("ctx")
    bits_all = n.bit_length() - 1
    rows = latents.shape[1]
    width = latents.shape[2]
    own_w = w_square.shape[1]
    channels = pixels.shape[1]
    slots = pixels.shape[2]
    total_rows = rows * n
    head_size = width // H
    scale = 1.0 / math.sqrt(width)
    scale_self = 1.0 / math.sqrt(head_size)
    core = lax.axis_index("seq")
    place = lax.axis_index("ctx")
    parity = place & 1
    pair = place >> 1
    wide = [4 << i for i in range(bits_all - 2)]

    def swap(x, bit):
        return lax.ppermute(x, "ctx", [(i, i ^ bit) for i in range(n)])

    def swap_core(x):
        return lax.ppermute(x, "seq", [(0, 1), (1, 0)])

    def ordered(mine, other, flag, axis):
        first = jnp.where(flag == 0, mine, other)
        second = jnp.where(flag == 0, other, mine)
        return jnp.concatenate([first, second], axis=axis)

    def quad(x, low, high, axis):
        one, two, three = swap(x, low), swap(x, high), swap(x, low | high)
        bit_low, bit_high = (place // low) & 1, (place // high) & 1
        near = ordered(x, one, bit_low, axis)
        far = ordered(two, three, bit_low, axis)
        return ordered(near, far, bit_high, axis)

    def both(x):
        return ordered(x, swap_core(x), core, 1)

    def gather_wide(x):
        rest = list(wide)
        x = x[None]
        while len(rest) > 1:
            x = quad(x[None], rest[0], rest[1], 0)
            x = x.reshape((-1,) + x.shape[2:])
            rest = rest[2:]
        for bit in rest:
            x = ordered(x[None], swap(x[None], bit), (place // bit) & 1, 0)
            x = x.reshape((-1,) + x.shape[2:])
        return x

    def own_steps(array, other):
        x = ordered(pick(array, parity), other, parity, 0)[None]
        for bit in wide:
            other = yield swap(x, bit)
            x = ordered(x, other, (place // bit) & 1, 0)
        other = yield swap(x, 2)
        x = ordered(x[:, None], other[:, None], (place // 2) & 1, 1)
        return x.reshape(total_rows, width)

    lanes = 384
    tall = (channels + 6 + 15) // 16 * 16
    packed = jnp.concatenate(
        [
            w_square[0],
            jnp.pad(w_input[0], ((0, 0), (0, tall - channels))),
            vec_d.T,
            jnp.zeros((own_w, lanes - tall - vec_d.shape[0]), b16),
            jnp.pad(w_input[1], ((0, 0), (0, lanes - channels))),
        ],
        axis=1,
    )
    packed = gather_wide(packed[None])[:, 0]
    packed = quad(packed[:, None], 1, 2, 1)
    packed = both(packed.reshape(1, n * own_w, -1))[0]
    square_first = packed[:, :width]
    packed = lax.optimization_barrier(packed[:, width:])
    v_key = packed[:, :tall]
    v_val = packed[:, lanes : lanes + tall]
    vecf = matmul("kc,dc->kd", jnp.eye(24, lanes - tall, dtype=b16), packed[:, tall:lanes])
    away = jnp.concatenate([pick(latents, 1 - parity), pick(cotangent, 1 - parity)], axis=0)
    away = swap(away, 1)
    lat = ordered(pick(latents, parity), away[:rows], parity, 0)
    lat = gather_wide(lat[None])
    lat = ordered(lat, swap(lat, 2), (place // 2) & 1, 1).reshape(total_rows, width)
    planes = lax.all_gather(w_square[1:], ("seq", "ctx"), axis=1, tiled=True)

    latent = lat.astype(f32)
    norm_a, unit_a, inv_a = layer_norm(latent, vecf[0], vecf[1], 1)
    low_a = norm_a.astype(b16)
    query = (matmul("id,de->ie", low_a, square_first) + vecf[2]).astype(b16)
    gate = (matmul("dc,id->ci", v_key, query) * scale).astype(b16)
    gates = ordered(gate[None], swap(gate, 1)[None], parity, 0)
    steps = own_steps(after(cotangent, gates), away[rows:])
    hanging = [next(steps)]
    gathered = []

    def pace(value):
        if not hanging:
            return value
        value, other = lax.optimization_barrier((value, hanging.pop()))
        try:
            hanging.append(steps.send(other))
        except StopIteration as stop:
            gathered.append(stop.value)
        return value


    gain_in = vec_c.astype(f32)
    norm_x, unit_x, inv_x = layer_norm(pixels.astype(f32), gain_in[0][:, None], gain_in[1][:, None], 1)
    low_x = jnp.pad(norm_x.astype(b16), ((0, 0), (0, tall - channels), (0, 0)))
    position = place * slots + jnp.arange(slots, dtype=jnp.int32)
    valid = (position[None, :] < lengths[:, None])[:, None, :]
    scores = matmul("qci,qcj->qij", gates, low_x)
    top = jnp.max(jnp.where(valid, scores, -1e30), axis=2)
    top_hi, top_lo = split_two(top)
    shift = top_hi.astype(f32) + top_lo.astype(f32)
    expo = jnp.where(valid, jnp.exp(scores - shift[..., None]), 0.0)
    total_hi, total_lo = split_two(jnp.sum(expo, axis=2))
    mixed = matmul("qij,qcj->qci", expo.astype(b16), low_x).astype(b16)
    row = jnp.arange(tall)[:, None]

    def write(v, parts):
        for k, part in enumerate(parts):
            v = jnp.where(row == channels + k, part[..., None, :], v)
        return v

    pay = write(mixed, [top_hi, top_lo, total_hi, total_lo])

    def opened(p):
        s = p[channels : channels + 4].astype(f32)
        return p.astype(f32), s[0] + s[1], s[2] + s[3]

    def merge(a, b):
        va, ta, la = opened(a)
        vb, tb, lb = opened(b)
        t = jnp.maximum(ta, tb)
        ea = jnp.exp(ta - t)
        eb = jnp.exp(tb - t)
        return va * ea + vb * eb, t, la * ea + lb * eb

    def closed(v, t, l):
        return write(v.astype(b16), split_two(t) + split_two(l))

    state = merge(pick(pay, parity), pace(swap(pick(pay, 1 - parity), 1)))
    for bit in [2] + wide:
        mine = closed(*state)
        state = merge(mine, pace(swap(mine, bit)))
    while hanging:
        pace(state[0])
    cot = gathered[0]
    mix_sum, top_all, total_all = state
    mean_x = jnp.where(row < channels, mix_sum / total_all, 0.0)
    mean_low = mean_x.astype(b16)

    attended = (matmul("ci,dc->id", mean_low, v_val) + vecf[3]).astype(b16)
    part_rows = 2 * own_w
    aligned = max(part_rows, 128)
    base = pair * part_rows // aligned * aligned
    inner = pair * part_rows - base
    numbers = jnp.stack([core, base, n * own_w + base, inner]).astype(jnp.int32)
    final, d_attended, d_after_cross, keep, send = latent_part(
        attended, lat, vecf, planes, cot, numbers, part_rows, aligned, scale_self
    )

    def own_rows(array):
        mine = lax.dynamic_slice_in_dim(array, place * rows, rows, 0)
        theirs = lax.dynamic_slice_in_dim(array, (place ^ 1) * rows, rows, 0)
        return ordered(mine[None], swap(theirs, 1)[None], parity, 0)

    def share(a):
        return jnp.concatenate([lax.dynamic_slice_in_dim(a, s * n * own_w + base, aligned, 1) for s in range(2)], axis=1)

    def weight_grad(a, r):
        return matmul("ia,ie->ae", share(a), r)

    def window(part, which):
        return lax.dynamic_slice_in_dim(part, which * aligned + inner, part_rows, 0)

    def halves(x, which):
        return lax.dynamic_slice_in_dim(x, which * own_w, own_w, x.ndim - 2)

    def halved(x, which):
        top = halves(x[: 9 * part_rows].reshape(9, part_rows, width), which).reshape(9 * own_w, width)
        return jnp.concatenate([top, x[9 * part_rows :]], axis=0)

    def sums(x):
        return jnp.sum(x.astype(f32), axis=0, keepdims=True)

    pull = matmul("dc,id->ci", v_val, d_attended).astype(b16)
    delta = jnp.sum(pull.astype(f32) * mean_x, axis=0)
    pieces = split_two(top_all) + split_two(total_all) + split_two(delta)
    sent = write(pull, pieces)
    other = swap(sent, 1)
    core_sums = swap_core(after(send, sent))
    sents = ordered(sent[None], other[None], parity, 0)
    pulls = sents
    side = sents[:, channels : channels + 6].astype(f32)
    top_q = side[:, 0] + side[:, 1]
    total_q = side[:, 2] + side[:, 3]
    delta_q = side[:, 4] + side[:, 5]
    scores_again = matmul("qci,qcj->qij", gates, low_x)
    weight = jnp.where(valid, jnp.exp(scores_again - top_q[..., None]), 0.0) / total_q[..., None]
    d_weight = matmul("qci,qcj->qij", pulls, low_x)
    d_scores = (weight * (d_weight - delta_q[..., None])).astype(b16)
    weight_low = weight.astype(b16)
    force = matmul("qij,qcj->qci", d_scores, low_x).astype(b16)
    mine = pick(force, parity)
    other = swap(pick(force, 1 - parity), 1)
    held = after(d_scores, force)
    d_in_norm = (matmul("qci,qij->qcj", gates, held) + matmul("qci,qij->qcj", pulls, weight_low))[:, :channels]
    grad_pixels = norm_back(d_in_norm, unit_x, inv_x, gain_in[0][:, None], 1)
    grad_vc = [jnp.sum(d_in_norm * unit_x, axis=(0, 2)), jnp.sum(d_in_norm, axis=(0, 2))]
    grad_vc = jnp.pad(jnp.stack(grad_vc), ((0, 0), (0, total_rows - channels)))
    other = after(other, grad_vc)
    force_sum = mine.astype(f32) + other.astype(f32)
    chip_sums = None
    for bit in [2] + wide:
        mine = write(force_sum.astype(b16), split_two(grad_vc[0]) + split_two(grad_vc[1]))
        other = swap(mine, bit)
        if chip_sums is None:
            core_sums = after(keep, mine) + core_sums
            other, core_sums = lax.optimization_barrier((other, core_sums))
            latents_out = own_rows(after(final, mine))
            chip_sums = swap(halved(core_sums, 1 - parity).astype(b16), 1)
            part_att = matmul("ia,ci->ac", share(d_attended), mean_low)
            other = after(other, part_att)
        elif bit == wide[-1]:
            other, chip_sums = lax.optimization_barrier((other, chip_sums))
        force_sum = mine.astype(f32) + other.astype(f32)
        grad_vc = jnp.stack([force_sum[channels] + force_sum[channels + 1], force_sum[channels + 2] + force_sum[channels + 3]])
    force_low = jnp.where(row < channels, force_sum * scale, 0.0).astype(b16)
    d_query = matmul("ci,dc->id", force_low, v_key).astype(b16)
    part0 = weight_grad(low_a, d_query)
    d_norm_a = matmul("ie,de->id", d_query, square_first)
    grad_lat = d_after_cross + norm_back(d_norm_a, unit_a, inv_a, vecf[0], 1)
    grad_latents = own_rows(grad_lat)

    part_q = matmul("ia,ci->ac", share(query), force_low)
    pad_lanes = lanes - tall
    wide_all = width + 2 * lanes

    def gradients(which):
        full = [window(part0, which)]
        for part in (part_q, part_att):
            full.append(jnp.pad(window(part, which), ((0, 0), (0, pad_lanes))))
        return jnp.concatenate(full, axis=1)

    late_vec = jnp.concatenate([sums(d_norm_a * unit_a), sums(d_norm_a), sums(d_query), jnp.pad(grad_vc, ((0, 0), (0, width - total_rows)))], axis=0)
    vectors = jnp.concatenate([late_vec, jnp.zeros((3, width), f32)], axis=0)
    tail = jnp.pad(vectors, ((0, 0), (0, wide_all - width)))
    own = jnp.concatenate([gradients(core), tail], axis=0)
    own = own + swap_core(jnp.concatenate([gradients(1 - core), tail], axis=0).astype(b16)).astype(f32)

    def reduced(which):
        return jnp.concatenate([halves(own[:part_rows], which), own[part_rows:]], axis=0)

    own = reduced(parity) + swap(reduced(1 - parity).astype(b16), 1).astype(f32)
    late = own[None, :own_w, :width]
    chip_sums = halved(core_sums, parity) + chip_sums.astype(f32)
    grad_input = jnp.stack([own[:own_w, width : width + channels], own[:own_w, width + lanes : width + lanes + channels]])
    tail = own[own_w:, :width]
    grad_vc = tail[3:5, :channels]
    vectors = jnp.concatenate([tail[:3], chip_sums[9 * own_w + 3 :]], axis=0)
    grad_vec = lax.dynamic_slice_in_dim(vectors, core * n * own_w + place * own_w, own_w, 1)[: vec_d.shape[0]]
    grad_square = jnp.concatenate([late, chip_sums[: 9 * own_w].reshape(9, own_w, width)], axis=0)
    return (latents_out, grad_latents, grad_pixels, grad_square, grad_input, grad_vec, grad_vc)


def solution(mesh):
    placed = (
        P("seq", None, "ctx"),
        P("seq"),
        P("seq", "ctx", None),
        P(None, ("seq", "ctx"), None),
        P(None, ("seq", "ctx"), None),
        P(None, ("seq", "ctx")),
        P(),
        P("seq", "ctx", None),
    )
    return jax.shard_map(
        body,
        mesh=mesh,
        in_specs=placed,
        out_specs=(
            P("seq", "ctx", None),
            P("seq", "ctx", None),
            P("seq", None, "ctx"),
            P(None, ("seq", "ctx"), None),
            P(None, ("seq", "ctx"), None),
            P(None, ("seq", "ctx")),
            P(),
        ),
        check_vma=False,
    )
```
